256 devices in a mesh: crop: 2 (over core), row: 8 (over x_hi, y), col: 16 (over z, x_lo).
Axes of the slice: x: 4 (x_hi: 2, x_lo: 2; x = x_hi * 2 + x_lo), y: 4, z: 8, core: 2. Of those that a mesh axis runs over, the one named last changes fastest.
Arguments:
- pair_state: bfloat16 [768, 384, 128], P(('crop', 'row'), 'col'), parts along dimension 0, may hold values from -6 to 6
- token_mask: int32 [768], P('crop'), parts along dimension 0, may hold values from 0 to 1, as said below
- block_pattern: int32 [8, 4], P('crop'), parts along dimension 0, may hold values from 0 to 1, as said below
- triangle_norm: float32 [128], replicated, may hold values from 0.1 to 1.9
- triangle_input: bfloat16 [128, 512], replicated, may hold values from -0.5 to 0.5
- triangle_gate: bfloat16 [128, 128], replicated, may hold values from -0.5 to 0.5
- product_norm: float32 [128], replicated, may hold values from 0.1 to 1.9
- triangle_output: bfloat16 [128, 128], replicated, may hold values from -0.5 to 0.5
- attend_norm: float32 [128], replicated, may hold values from 0.1 to 1.9
- attend_inputs: bfloat16 [128, 384], replicated, may hold values from -4 to 4
- attend_gate: bfloat16 [128, 128], replicated, may hold values from -0.5 to 0.5
- attend_bias: bfloat16 [128, 4], replicated, may hold values from -0.5 to 0.5
- attend_output: bfloat16 [128, 128], replicated, may hold values from -0.5 to 0.5
Outputs:
- pair_output: bfloat16 [768, 384, 128], P(('crop', 'row'), 'col'), parts along dimension 0
The draws below stay inside these ranges and needn't reach their ends.
There are 2 independent parts, one for each index of `crop`. The reference program is written for one: setup_inputs(seed, part) draws one part's arguments, and reference() takes and returns one part's arrays. A program takes and returns all parts, laid end to end along the dimension named above; an argument that names none is the same for every part. Nothing has to cross between parts.
Inputs may be any that keep to these rules, and one draw needn't show every extreme that they name: `token_mask`: 1 on a prefix of 96 or more tokens and 0 after it. `block_pattern`: every row allows its own block and block 0.
All inputs are finite; a program needn't handle non-finite values.
Results may differ from the reference program's by a relative error of at most 0.02.
Values may be sent and summed in bfloat16 or wider, within the bound.
A program may use at most 64 MiB of HBM per device.

```python
import math
import jax
import jax.numpy as jnp
from jax import lax

C = 128
H = 4
NB = 4
N = 384


def draw_token_mask(key, part):
    length = jax.random.randint(jax.random.fold_in(key, 11), (), N // NB, N + 1)
    positions = jnp.arange(N)
    return (positions < length).astype(jnp.int32)


def draw_block_pattern(key, part):
    random_bits = jax.random.randint(jax.random.fold_in(key, 12), (NB, NB), 0, 2)
    index_grid = jnp.arange(NB)
    forced = (index_grid[:, None] == index_grid[None, :]) | (index_grid[None, :] == 0)
    return jnp.where(forced, 1, random_bits).astype(jnp.int32)


def draw_attend_inputs(key, part):
    drawn = jax.random.normal(jax.random.fold_in(key, 13), (C, 3 * C), jnp.float32) / math.sqrt(C)
    return jnp.clip(drawn, -4.0, 4.0).astype(jnp.bfloat16)


def levels(key, dims, split, least, top_value):
    level, own = 1.0, jax.random.fold_in(key, 6)
    for axis_at, shards_of in split:
        heights = jnp.exp(jax.random.uniform(jax.random.fold_in(own, axis_at), (shards_of,), jnp.float32, least / len(split), top_value / len(split)))
        level = level * jnp.repeat(heights, dims[axis_at] // shards_of).reshape([-1 if axis == axis_at else 1 for axis in range(len(dims))])
    return level


def centred(key, shape, spread, limit, shards=(), dtype=jnp.bfloat16):
    loudness = levels(key, shape, shards, -0.22, 0.18) if shards else 1.0
    entries = jax.random.normal(key, shape, jnp.float32) * spread * loudness
    return jnp.minimum(jnp.maximum(entries, -limit), limit).astype(dtype)


def setup_inputs(seed: int = 0, part: int = 0) -> dict:
    splits = jax.random.split(jax.random.key(seed), 14)
    part_keys = jax.random.split(jax.random.fold_in(splits[13], part), 14)
    pair_state = centred(part_keys[0], (N, N, C), 1.0, 6.0, ((0, 8), (1, 16)))
    token_mask = draw_token_mask(jax.random.fold_in(jax.random.fold_in(splits[13], part), 71), part)
    block_pattern = draw_block_pattern(jax.random.fold_in(jax.random.fold_in(splits[13], part), 71), part)
    triangle_norm = jnp.clip(1.0 + 0.18 * jax.random.normal(splits[3], (C,), jnp.float32), 0.1, 1.9)
    triangle_input = centred(splits[4], (C, 4 * C), C ** -0.5, 0.5)
    triangle_gate = centred(splits[5], (C, C), C ** -0.5, 0.5)
    product_norm = jnp.clip(1.0 + 0.18 * jax.random.normal(splits[6], (C,), jnp.float32), 0.1, 1.9)
    triangle_output = centred(splits[7], (C, C), C ** -0.5, 0.5)
    attend_norm = jnp.clip(1.0 + 0.18 * jax.random.normal(splits[8], (C,), jnp.float32), 0.1, 1.9)
    attend_inputs = draw_attend_inputs(jax.random.fold_in(splits[13], 71), part)
    attend_gate = centred(splits[10], (C, C), C ** -0.5, 0.5)
    attend_bias = centred(splits[11], (C, H), C ** -0.5, 0.5)
    attend_output = centred(splits[12], (C, C), C ** -0.5, 0.5)
    return dict(pair_state=pair_state, token_mask=token_mask, block_pattern=block_pattern, triangle_norm=triangle_norm, triangle_input=triangle_input, triangle_gate=triangle_gate, product_norm=product_norm, triangle_output=triangle_output, attend_norm=attend_norm, attend_inputs=attend_inputs, attend_gate=attend_gate, attend_bias=attend_bias, attend_output=attend_output)


norm_epsilon = 1e-05

def layer_norm(inputs, gain):
    average = lax.optimization_barrier(jnp.mean(inputs, axis=-1, keepdims=True))
    centered = inputs - average
    variance = lax.optimization_barrier(jnp.mean(centered * centered, axis=-1, keepdims=True))
    return centered * lax.rsqrt(variance + norm_epsilon) * gain

def attend_row(pair_row, attend_inputs, attend_gate, head_bias, allowed):
    channels = pair_row.shape[1]
    head_count = head_bias.shape[0]
    head_width = channels // head_count
    combined = jnp.dot(pair_row, attend_inputs, preferred_element_type=jnp.float32)
    queries = combined[:, :channels].astype(jnp.bfloat16).reshape(-1, head_count, head_width)
    key_rows = combined[:, channels:2 * channels].astype(jnp.bfloat16).reshape(-1, head_count, head_width)
    values = combined[:, 2 * channels:].astype(jnp.bfloat16).reshape(-1, head_count, head_width)
    gate_values = jax.nn.sigmoid(jnp.dot(pair_row, attend_gate, preferred_element_type=jnp.float32))
    scores = jnp.einsum('jhd,khd->hjk', queries.astype(jnp.float32), key_rows.astype(jnp.float32)) / math.sqrt(head_width)
    scores = scores + head_bias.astype(jnp.float32)
    scores = jnp.where(allowed[None], scores, -jnp.inf)
    row_max = lax.optimization_barrier(jnp.max(scores, axis=-1, keepdims=True))
    weights = jnp.exp(scores - row_max)
    probabilities = (weights / lax.optimization_barrier(jnp.sum(weights, axis=-1, keepdims=True))).astype(jnp.bfloat16)
    attended = jnp.einsum('hjk,khd->jhd', probabilities.astype(jnp.float32), values.astype(jnp.float32)).reshape(-1, channels)
    return (gate_values * attended).astype(jnp.bfloat16)

def reference(pair_state, token_mask, block_pattern, triangle_norm, triangle_input, triangle_gate, product_norm, triangle_output, attend_norm, attend_inputs, attend_gate, attend_bias, attend_output):
    state_float = pair_state.astype(jnp.float32)
    normed = layer_norm(state_float, triangle_norm).astype(jnp.bfloat16)
    projected = jnp.dot(normed, triangle_input, preferred_element_type=jnp.float32)
    valid_tokens = token_mask.astype(jnp.float32)
    pair_valid = (valid_tokens[:, None] * valid_tokens[None, :])[:, :, None]
    left_factor = (pair_valid * jax.nn.sigmoid(projected[..., :C]) * projected[..., C:2 * C]).astype(jnp.bfloat16)
    right_factor = (pair_valid * jax.nn.sigmoid(projected[..., 2 * C:3 * C]) * projected[..., 3 * C:]).astype(jnp.bfloat16)
    product = jnp.einsum('ikc,jkc->ijc', left_factor.astype(jnp.float32), right_factor.astype(jnp.float32), precision=lax.Precision.HIGHEST)
    product_normed = layer_norm(product, product_norm).astype(jnp.bfloat16)
    gate_values = jax.nn.sigmoid(jnp.dot(normed, triangle_gate, preferred_element_type=jnp.float32))
    middle = (state_float + gate_values * jnp.dot(product_normed, triangle_output, preferred_element_type=jnp.float32)).astype(jnp.bfloat16)
    attend_normed = layer_norm(middle.astype(jnp.float32), attend_norm).astype(jnp.bfloat16)
    head_bias = jnp.transpose(jnp.dot(attend_normed, attend_bias, preferred_element_type=jnp.float32).astype(jnp.bfloat16), (2, 0, 1))
    block_width = N // NB
    pattern_ok = block_pattern[:, None, :, None] > 0
    allowed = jnp.broadcast_to(pattern_ok, (NB, block_width, NB, block_width)).reshape(N, N) & (token_mask[None, :] > 0)
    attended = lax.map(lambda pair_row: attend_row(pair_row, attend_inputs, attend_gate, head_bias, allowed), attend_normed)
    update = jnp.dot(attended, attend_output, preferred_element_type=jnp.float32)
    return (middle.astype(jnp.float32) + update).astype(jnp.bfloat16)
```

```python
import functools
import math

import jax
import jax.numpy as jnp
import numpy as np
from jax import lax
from jax.experimental import pallas as pl
from jax.experimental.pallas import tpu as pltpu
from jax.sharding import PartitionSpec as P

MESH = pl.DeviceIdType.MESH
F32 = jnp.float32
BF16 = jnp.bfloat16
EPS = 1e-05
ROWS, COLS, C, N = 8, 16, 128, 384
HEADS, WIDTH = 4, 32
ZS, GS, OWN = 8, 16, 3
LOG2E = 1.4426950408889634
MASKED = -1e30


def dot(a, b):
    return jnp.dot(a, b, preferred_element_type=F32)


def dot_nt(a, b):
    return lax.dot_general(a, b, (((1,), (1,)), ((), ())), preferred_element_type=F32)


def dot_tn(a, b):
    return lax.dot_general(a, b, (((0,), (0,)), ((), ())), preferred_element_type=F32)


def wide(gain):
    return jnp.concatenate([gain] * (N // 128), axis=1)


def norm_columns(v, gain):
    centered = v - jnp.mean(v, axis=0, keepdims=True)
    variance = jnp.mean(centered * centered, axis=0, keepdims=True)
    return centered * lax.rsqrt(variance + EPS) * wide(gain)


def sigmoid(v):
    return 1.0 / (1.0 + jnp.exp(-v))


def turned(w):
    return jnp.transpose(w.astype(F32))


def kernel(
    x_ref, mask_ref, pattern_ref, perm_ref,
    norm1_ref, w_in_ref, w_gate_ref, norm2_ref, w_out1_ref,
    norm3_ref, w_qkv_ref, w_gate2_ref, w_bias_ref, w_out2_ref,
    out_ref,
    x_rows, send_l, recv_l, send_z, recv_z, send_p, recv_p, send_x, recv_x,
    bias_all, bias_full, send_o, xt, gate1, mid, an_t, wide_t, bias_t, penalty,
    w_g, w_v, w_gate_t, w_o1_t, w_qv_t, w_k_t, w_gate2_t, w_o2_t, gains,
    r_send, r_recv, l_send, l_recv, z_send, z_recv, p_send, p_recv, x_send, x_recv,
    bz_send, bz_recv, bx_send, bx_recv, by_send, by_recv, o_send, o_recv, local,
):
    row, col = lax.axis_index("row"), lax.axis_index("col")
    z, x_lo = col // 2, col % 2
    x_hi, y = row // 4, row % 4
    g = row * 2 + x_lo
    x_at = x_hi * 2 + x_lo

    def remote(src, dst, send, recv, r, c):
        return pltpu.make_async_remote_copy(
            src_ref=src, dst_ref=dst, send_sem=send, recv_sem=recv,
            device_id={"row": r, "col": c}, device_id_type=MESH,
        )

    def xy_place(other):
        return other // 2, z * 2 + other % 2

    barrier = pltpu.get_barrier_semaphore()
    for d in range(1, COLS):
        pl.semaphore_signal(barrier, inc=1, device_id={"row": row, "col": lax.rem(col + d, COLS)}, device_id_type=MESH)
    for d in range(1, ROWS):
        for e in range(2):
            pl.semaphore_signal(barrier, inc=1, device_id={"row": lax.rem(row + d, ROWS), "col": z * 2 + e}, device_id_type=MESH)

    w_t = jnp.concatenate([turned(w_in_ref[:, s * C : (s + 1) * C]) for s in range(4)], axis=0)
    ga, va, gb, vb = (w_t[s * C : (s + 1) * C].reshape(GS, 8, C) for s in range(4))
    w_g[...] = jnp.concatenate([ga, gb], axis=1).reshape(2 * C, C).astype(BF16)
    w_v[...] = jnp.concatenate([va, vb], axis=1).reshape(2 * C, C).astype(BF16)
    for slot, ref in enumerate((norm1_ref, norm2_ref, norm3_ref)):
        gains[slot] = jnp.transpose(jnp.broadcast_to(ref[...], (C, C)))

    pl.semaphore_wait(barrier, COLS - 1 + 2 * (ROWS - 1))

    def r_copy(d):
        peer = lax.rem(col + d, COLS)
        return remote(x_ref.at[pl.ds(OWN * peer, OWN)], x_rows.at[col], r_send.at[peer], r_recv.at[col], row, peer)

    def r_arrival(d):
        peer = lax.rem(col + d, COLS)
        return remote(x_ref.at[pl.ds(OWN * peer, OWN)], x_rows.at[peer], r_send.at[peer], r_recv.at[peer], row, peer)

    for d in range(1, COLS):
        r_copy(d).start()
    own_rows = pltpu.make_async_copy(x_ref.at[pl.ds(OWN * col, OWN)], x_rows.at[col], local.at[0])
    own_rows.start()

    w_gate_t[...] = turned(w_gate_ref[...]).astype(BF16)
    w_o1_t[...] = turned(w_out1_ref[...]).astype(BF16)
    w_o2_t[...] = turned(w_out2_ref[...]).astype(BF16)
    w_gate2_t[...] = turned(w_gate2_ref[...]).astype(BF16)
    w_qv_t[0] = turned(w_qkv_ref[:, :C]).astype(BF16)
    w_qv_t[1] = turned(w_qkv_ref[:, 2 * C :]).astype(BF16)
    w_k_t[...] = turned(w_qkv_ref[:, C : 2 * C]).astype(BF16)
    mask = mask_ref[...].astype(F32)
    lane = lax.broadcasted_iota(jnp.int32, (1, N), 1)
    key_mask = jnp.transpose(jnp.broadcast_to(mask, (C, N)))
    for b in range(4):
        line = jnp.zeros((1, N), F32)
        for a in range(4):
            inside = (lane >= 96 * a) & (lane < 96 * (a + 1))
            line = line + jnp.where(inside, pattern_ref[a, b].astype(F32), 0.0)
        part = wide(key_mask[96 * b : 96 * (b + 1)]) * line
        penalty[96 * b : 96 * (b + 1), :] = jnp.where(part > 0.0, 0.0, MASKED)

    own_rows.wait()
    for d in range(1, COLS):
        r_arrival(d).wait_recv()

    def l_copy(i, d, arriving):
        peer = lax.rem(g + d, GS)
        r, c = xy_place(peer)
        slot = peer if arriving else g
        return remote(send_l.at[i, peer], recv_l.at[i, slot], l_send.at[i, peer], l_recv.at[i, slot], r, c)

    def l_own(i):
        return pltpu.make_async_copy(send_l.at[i, g], recv_l.at[i, g], local.at[i])

    for i in range(OWN):
        x_t = jnp.transpose(x_rows[:, i].astype(F32).reshape(N, C))
        xt[i] = x_t
        normed = norm_columns(x_t, gains[0]).astype(BF16)
        an_t[i] = normed
        own_token = row * 48 + col * OWN + i
        mine = jnp.sum(jnp.where(lane == own_token, mask, 0.0), axis=1, keepdims=True)
        factors = sigmoid(dot(w_g[...], normed)) * dot(w_v[...], normed) * (mask * mine)
        send_l[i] = factors.astype(BF16).reshape(GS, 16, N)
        for d in range(1, GS):
            l_copy(i, d, False).start()
        l_own(i).start()
    for i in range(OWN):
        gate1[i] = sigmoid(dot(w_gate_t[...], an_t[i]))
    for d in range(1, COLS):
        r_copy(d).wait_send()

    for i in range(OWN):
        l_own(i).wait()
        for d in range(1, GS):
            l_copy(i, d, True).wait_recv()
        arrived = recv_l[i].astype(F32).reshape(GS * 16, N)
        for b in range(3):
            wide_t[b, i * 256 : (i + 1) * 256, :] = arrived[:, b * 128 : (b + 1) * 128]
    for ch in range(16):
        for b in range(3):
            piece = wide_t[b, pl.ds(ch, 48, stride=16), :]
            send_z[ch % 8, ch // 8, :, b * 128 : (b + 1) * 128] = piece.astype(BF16)

    def z_copy(src, dst, send, recv, d, arriving):
        peer = lax.rem(z + d, ZS)
        slot = peer if arriving else z
        return remote(src.at[peer], dst.at[slot], send.at[peer], recv.at[slot], row, peer * 2 + x_lo)

    for d in range(1, ZS):
        z_copy(send_z, recv_z, z_send, z_recv, d, False).start()
    own_z = pltpu.make_async_copy(send_z.at[z], recv_z.at[z], local.at[0])
    own_z.start()
    for i in range(OWN):
        for d in range(1, GS):
            l_copy(i, d, False).wait_send()
    own_z.wait()
    for d in range(1, ZS):
        z_copy(send_z, recv_z, z_send, z_recv, d, True).wait_recv()

    left = recv_z[:, 0].reshape(N, N)
    right = dot(perm_ref[...], recv_z[:, 1].reshape(N, N)).astype(BF16)
    send_p[...] = dot_nt(left, right).astype(BF16).reshape(ZS, 48, N)
    for d in range(1, ZS):
        z_copy(send_p, recv_p, p_send, p_recv, d, False).start()
    own_p = pltpu.make_async_copy(send_p.at[z], recv_p.at[z], local.at[0])
    own_p.start()
    for d in range(1, ZS):
        z_copy(send_z, recv_z, z_send, z_recv, d, False).wait_send()
    own_p.wait()
    for d in range(1, ZS):
        z_copy(send_p, recv_p, p_send, p_recv, d, True).wait_recv()

    arrived = recv_p[...].astype(F32).reshape(N, N)
    for b in range(3):
        wide_t[b, :N, :] = arrived[:, b * 128 : (b + 1) * 128]
    for i in range(OWN):
        for other in range(GS):
            for b in range(3):
                piece = wide_t[b, pl.ds(i * GS + other, 8, stride=48), :]
                send_x[other, i, :, b * 128 : (b + 1) * 128] = piece.astype(BF16)

    def x_copy(d, arriving):
        peer = lax.rem(g + d, GS)
        r, c = xy_place(peer)
        slot = peer if arriving else g
        return remote(send_x.at[peer], recv_x.at[slot], x_send.at[peer], x_recv.at[slot], r, c)

    for d in range(1, GS):
        x_copy(d, False).start()
    own_x = pltpu.make_async_copy(send_x.at[g], recv_x.at[g], local.at[0])
    own_x.start()
    for d in range(1, ZS):
        z_copy(send_p, recv_p, p_send, p_recv, d, False).wait_send()
    own_x.wait()
    for d in range(1, GS):
        x_copy(d, True).wait_recv()

    for i in range(OWN):
        product = recv_x[:, i].astype(F32).reshape(C, N)
        update = dot(w_o1_t[...], norm_columns(product, gains[1]).astype(BF16))
        middle = (xt[i] + gate1[i] * update).astype(BF16).astype(F32)
        mid[i] = middle
        attend = norm_columns(middle, gains[2]).astype(BF16)
        an_t[i] = attend
        bias_all[x_at, z, i] = dot_tn(w_bias_ref[...], attend).astype(BF16)

    def bz_copy(d, arriving):
        peer = lax.rem(z + d, ZS)
        slot = peer if arriving else z
        return remote(bias_all.at[x_at, z], bias_all.at[x_at, slot], bz_send.at[peer], bz_recv.at[slot], row, peer * 2 + x_lo)

    for d in range(1, ZS):
        bz_copy(d, False).start()

    def x_place(at):
        return (at // 2) * 4 + y, z * 2 + at % 2

    up, down = lax.rem(x_at + 1, 4), lax.rem(x_at + 3, 4)
    opposite = lax.rem(x_at + 2, 4)

    def bx_copy(k, arriving):
        target = up if k % 2 == 0 else down
        if k < 2:
            held = (down if k == 0 else up) if arriving else x_at
            ref = bias_all.at[held]
        else:
            held = opposite if arriving else (down if k == 2 else up)
            ref = bias_all.at[held, 4 * (k - 2) : 4 * (k - 1)]
        r, c = x_place(target)
        return remote(ref, ref, bx_send.at[k], bx_recv.at[k], r, c)

    for d in range(1, ZS):
        bz_copy(d, True).wait_recv()
    for k in range(2):
        bx_copy(k, False).start()
    for k in range(2):
        bx_copy(k, True).wait_recv()
        bx_copy(k + 2, False).start()
    for k in range(2, 4):
        bx_copy(k, True).wait_recv()

    for hi in range(2):
        for zz in range(ZS):
            for lo in range(2):
                for i in range(OWN):
                    piece = bias_all[2 * hi + lo, zz, i].astype(F32)
                    at = (((hi * ZS + zz) * 2 + lo) * OWN + i) * 4
                    for b in range(3):
                        wide_t[b, at : at + 4, :] = piece[:, b * 128 : (b + 1) * 128]
    for hi in range(2):
        for h in range(HEADS):
            for b in range(3):
                piece = wide_t[b, pl.ds(hi * 192 + h, 48, stride=4), :]
                bias_full[h, hi, y, :, b * 128 : (b + 1) * 128] = piece.astype(BF16)

    y_up, y_down, y_far = lax.rem(y + 1, 4), lax.rem(y + 3, 4), lax.rem(y + 2, 4)

    def by_copy(k, arriving):
        target = y_up if k % 2 == 0 else y_down
        if k < 2:
            held = (y_down if k == 0 else y_up) if arriving else y
            ref = bias_full.at[:, :, held]
        else:
            held = y_far if arriving else (y_down if k == 2 else y_up)
            ref = bias_full.at[:, k - 2, held]
        return remote(ref, ref, by_send.at[k], by_recv.at[k], x_hi * 4 + target, col)

    for k in range(2):
        by_copy(k, False).start()

    for d in range(1, GS):
        x_copy(d, False).wait_send()

    for k in range(2):
        by_copy(k, True).wait_recv()
        by_copy(k + 2, False).start()
    for k in range(2, 4):
        by_copy(k, True).wait_recv()
    for h in range(HEADS):
        whole = bias_full[h].reshape(N, N).astype(F32)
        bias_t[h] = jnp.transpose(whole) * LOG2E + penalty[...]

    def o_copy(i, d, arriving):
        peer = lax.rem(col + d, COLS)
        slot = peer if arriving else col
        return remote(send_o.at[i, peer], out_ref.at[OWN * slot + i], o_send.at[i, peer], o_recv.at[i, slot], row, peer)

    def o_own(i):
        return pltpu.make_async_copy(send_o.at[i, col], out_ref.at[OWN * col + i], local.at[i])

    scale = LOG2E / math.sqrt(WIDTH)
    head_of = lax.broadcasted_iota(jnp.int32, (C, N), 0)
    for i in range(OWN):
        attend = an_t[i]
        queries = dot(w_qv_t[0], attend) * scale
        values = dot(w_qv_t[1], attend).astype(BF16)
        keys = jnp.transpose(dot(w_k_t[...], attend)).astype(BF16)
        gate2 = sigmoid(dot(w_gate2_t[...], attend))
        parts = []
        for h in range(HEADS):
            inside = (head_of >= WIDTH * h) & (head_of < WIDTH * (h + 1))
            own_queries = jnp.where(inside, queries, 0.0).astype(BF16)
            scores = dot(keys, own_queries) + bias_t[h]
            weights = jnp.exp2(scores - jnp.max(scores, axis=0, keepdims=True))
            total = jnp.sum(weights, axis=0, keepdims=True)
            mixed = dot(values[WIDTH * h : WIDTH * (h + 1)], weights.astype(BF16))
            parts.append(mixed / total)
        gated = (gate2 * jnp.concatenate(parts, axis=0)).astype(BF16)
        result = mid[i] + dot(w_o2_t[...], gated)
        send_o[i] = jnp.transpose(result).reshape(COLS, 24, C).astype(BF16)
        for d in range(1, COLS):
            o_copy(i, d, False).start()
        o_own(i).start()

    for d in range(1, ZS):
        bz_copy(d, False).wait_send()
    for k in range(4):
        bx_copy(k, False).wait_send()
        by_copy(k, False).wait_send()
    for i in range(OWN):
        o_own(i).wait()
        for d in range(1, COLS):
            o_copy(i, d, True).wait_recv()
    for i in range(OWN):
        for d in range(1, COLS):
            o_copy(i, d, False).wait_send()


def token_order():
    perm = np.zeros((N, N), np.float32)
    for t in range(N):
        r, c, i = t // 48, (t % 48) // 3, t % 3
        perm[t, (c // 2) * 48 + i * GS + 2 * r + c % 2] = 1.0
    return perm


def shards(
    pair_state, token_mask, block_pattern, triangle_norm, triangle_input, triangle_gate, product_norm,
    triangle_output, attend_norm, attend_inputs, attend_gate, attend_bias, attend_output,
):
    vmem = pl.BlockSpec(memory_space=pltpu.VMEM)
    smem = pl.BlockSpec(memory_space=pltpu.SMEM)
    dma = pltpu.SemaphoreType.DMA
    V = pltpu.VMEM
    return pl.pallas_call(
        kernel,
        out_shape=jax.ShapeDtypeStruct(pair_state.shape, BF16),
        in_specs=[vmem, vmem, smem] + [vmem] * 11,
        out_specs=vmem,
        scratch_shapes=[
            V((COLS, OWN, 24, C), BF16),
            V((OWN, GS, 16, N), BF16), V((OWN, GS, 16, N), BF16),
            V((ZS, 2, 48, N), BF16), V((ZS, 2, 48, N), BF16),
            V((ZS, 48, N), BF16), V((ZS, 48, N), BF16),
            V((GS, OWN, 8, N), BF16), V((GS, OWN, 8, N), BF16),
            V((4, ZS, OWN, HEADS, N), BF16),
            V((HEADS, 2, 4, 48, N), BF16),
            V((OWN, COLS, 24, C), BF16),
            V((OWN, C, N), F32), V((OWN, C, N), F32), V((OWN, C, N), F32), V((OWN, C, N), BF16),
            V((3, 768, 128), F32), V((HEADS, N, N), F32), V((N, N), F32),
            V((2 * C, C), BF16), V((2 * C, C), BF16), V((C, C), BF16), V((C, C), BF16),
            V((2, C, C), BF16), V((C, C), BF16), V((C, C), BF16), V((C, C), BF16), V((3, C, C), F32),
            dma((COLS,)), dma((COLS,)), dma((OWN, GS)), dma((OWN, GS)), dma((ZS,)), dma((ZS,)),
            dma((ZS,)), dma((ZS,)), dma((GS,)), dma((GS,)),
            dma((ZS,)), dma((ZS,)), dma((4,)), dma((4,)), dma((4,)), dma((4,)),
            dma((OWN, COLS)), dma((OWN, COLS)), dma((4,)),
        ],
        compiler_params=pltpu.CompilerParams(
            collective_id=0, has_side_effects=True, vmem_limit_bytes=60 * 1024 * 1024
        ),
        name="pairformer",
    )(
        pair_state, token_mask.reshape(1, N), block_pattern, jnp.asarray(token_order(), BF16),
        triangle_norm.reshape(1, C), triangle_input, triangle_gate, product_norm.reshape(1, C), triangle_output,
        attend_norm.reshape(1, C), attend_inputs, attend_gate, attend_bias, attend_output,
    )


def solution(mesh):
    tile = P(("crop", "row"), "col", None)
    return jax.shard_map(
        shards,
        mesh=mesh,
        in_specs=(tile, P("crop"), P("crop", None)) + (P(),) * 10,
        out_specs=tile,
        check_vma=False,
    )
```

```python
import functools
import math

import jax
import jax.numpy as jnp
import numpy as np
from jax import lax
from jax.experimental import pallas as pl
from jax.experimental.pallas import tpu as pltpu
from jax.sharding import PartitionSpec as P

MESH = pl.DeviceIdType.MESH
F32 = jnp.float32
BF16 = jnp.bfloat16
EPS = 1e-05
ROWS, COLS, C, N = 8, 16, 128, 384
HEADS, WIDTH = 4, 32
ZS, GS, OWN = 8, 16, 3
LOG2E = 1.4426950408889634
MASKED = -1e30


def dot(a, b):
    return jnp.dot(a, b, preferred_element_type=F32)


def dot_nt(a, b):
    return lax.dot_general(a, b, (((1,), (1,)), ((), ())), preferred_element_type=F32)


def dot_tn(a, b):
    return lax.dot_general(a, b, (((0,), (0,)), ((), ())), preferred_element_type=F32)


def wide(gain):
    return jnp.concatenate([gain] * (N // 128), axis=1)


def norm_columns(v, gain):
    centered = v - jnp.mean(v, axis=0, keepdims=True)
    variance = jnp.mean(centered * centered, axis=0, keepdims=True)
    return centered * lax.rsqrt(variance + EPS) * wide(gain)


def sigmoid(v):
    return 1.0 / (1.0 + jnp.exp(-v))


def turned(w):
    return jnp.transpose(w.astype(F32))


RING_STEPS = (2, 1, 3)
Z_STEPS = (4, 3, 5, 2, 6, 1, 7)
COL_STEPS = tuple((dz, dl) for dz in Z_STEPS for dl in (1, 0)) + ((0, 1),)
XY_STEPS = tuple(sorted(
    ((dx, dy) for dx in range(4) for dy in range(4) if dx or dy),
    key=lambda s: -(min(s[0], 4 - s[0]) + min(s[1], 4 - s[1])),
))


def kernel(
    x_hbm, mask_ref, pattern_ref, perm_hbm,
    norm1_ref, w_in_hbm, w_gate_hbm, norm2_ref, w_out1_hbm,
    norm3_ref, w_qkv_hbm, w_gate2_hbm, w_bias_ref, w_out2_hbm,
    out_ref,
    x_rows, send_l, recv_l, send_z, recv_z, send_p, recv_p, send_x, recv_x,
    bias_all, send_o, xt, gate1, mid, an_t, wide_t, bias_t, penalty, scores_ref, values_ref, gate2_ref,
    perm_ref, w_in_ref, w_gate_ref, w_out1_ref, w_qkv_ref, w_gate2_ref, w_out2_ref,
    w_g, w_v, w_gate_t, w_o1_t, w_qv_t, w_k_t, w_gate2_t, w_o2_t, gains,
    r_send, r_recv, l_send, l_recv, z_send, z_recv, p_send, p_recv, x_send, x_recv,
    bz_send, bz_recv, ba_send, ba_recv, bb_send, bb_recv, o_send, o_recv, local, fetch,
):
    crop, row, col = lax.axis_index("crop"), lax.axis_index("row"), lax.axis_index("col")
    z, x_lo = col // 2, col % 2
    x_hi, y = row // 4, row % 4
    g = row * 2 + x_lo
    x_at = x_hi * 2 + x_lo

    def place(x, y, z):
        return (x // 2) * 4 + y, z * 2 + x % 2

    def signal(r, c):
        pl.semaphore_signal(barrier, inc=1, device_id={"row": r, "col": c}, device_id_type=MESH)

    def remote(src, dst, send, recv, r, c):
        return pltpu.make_async_remote_copy(
            src_ref=src, dst_ref=dst, send_sem=send, recv_sem=recv,
            device_id={"row": r, "col": c}, device_id_type=MESH,
        )

    def col_peer(dz, dl):
        return lax.rem(z + dz, ZS) * 2 + lax.rem(x_lo + dl, 2)

    def xy_peer(dx, dy):
        xx, yy = lax.rem(x_at + dx, 4), lax.rem(y + dy, 4)
        r, c = place(xx, yy, z)
        return r * 2 + xx % 2, r, c

    barrier = pltpu.get_barrier_semaphore()
    for dz, dl in COL_STEPS:
        signal(row, col_peer(dz, dl))
    for dx, dy in XY_STEPS:
        if (dx, dy) != (1, 0) and (dx, dy) != (3, 0) and (dx, dy) != (2, 0):
            _, r, c = xy_peer(dx, dy)
            signal(r, c)
    _, r, c = xy_peer(2, 0)
    signal(r, c)
    far = x_at + 1 + 2 * (1 - x_at % 2)
    r, c = place(lax.rem(far, 4), y, z)
    signal(r, c)

    fetched = [
        pltpu.make_async_copy(src, dst, fetch.at[n])
        for n, (src, dst) in enumerate((
            (w_in_hbm, w_in_ref), (w_gate_hbm, w_gate_ref), (w_out1_hbm, w_out1_ref), (w_qkv_hbm, w_qkv_ref),
            (w_gate2_hbm, w_gate2_ref), (w_out2_hbm, w_out2_ref), (perm_hbm, perm_ref),
        ))
    ]
    for copy in fetched:
        copy.start()

    fetched[0].wait()
    w_t = jnp.concatenate([turned(w_in_ref[:, s * C : (s + 1) * C]) for s in range(4)], axis=0)
    ga, va, gb, vb = (w_t[s * C : (s + 1) * C].reshape(GS, 8, C) for s in range(4))
    w_g[...] = jnp.concatenate([ga, gb], axis=1).reshape(2 * C, C).astype(BF16)
    w_v[...] = jnp.concatenate([va, vb], axis=1).reshape(2 * C, C).astype(BF16)
    for slot, ref in enumerate((norm1_ref, norm2_ref, norm3_ref)):
        gains[slot] = jnp.transpose(jnp.broadcast_to(ref[...], (C, C)))

    pl.semaphore_wait(barrier, COLS - 1 + 2 * (ROWS - 1))

    def r_copy(i, dz, dl, arriving):
        peer = col_peer(dz, dl)
        slot = peer if arriving else col
        return remote(x_hbm.at[OWN * peer + i], x_rows.at[i, slot], r_send.at[i, peer], r_recv.at[i, slot], row, peer)

    def r_own(i):
        return pltpu.make_async_copy(x_hbm.at[OWN * col + i], x_rows.at[i, col], local.at[i])

    for i in range(OWN):
        for dz, dl in COL_STEPS:
            r_copy(i, dz, dl, False).start()
        r_own(i).start()

    for copy in fetched[1:6]:
        copy.wait()
    w_gate_t[...] = turned(w_gate_ref[...]).astype(BF16)
    w_o1_t[...] = turned(w_out1_ref[...]).astype(BF16)
    w_o2_t[...] = turned(w_out2_ref[...]).astype(BF16)
    w_gate2_t[...] = turned(w_gate2_ref[...]).astype(BF16)
    w_qv_t[0] = turned(w_qkv_ref[:, :C]).astype(BF16)
    w_qv_t[1] = turned(w_qkv_ref[:, 2 * C :]).astype(BF16)
    w_k_t[...] = turned(w_qkv_ref[:, C : 2 * C]).astype(BF16)
    mask = mask_ref[...].astype(F32)
    lane = lax.broadcasted_iota(jnp.int32, (1, N), 1)
    key_mask = jnp.transpose(jnp.broadcast_to(mask, (C, N)))
    for b in range(4):
        line = jnp.zeros((1, N), F32)
        for a in range(4):
            inside = (lane >= 96 * a) & (lane < 96 * (a + 1))
            line = line + jnp.where(inside, pattern_ref[a, b].astype(F32), 0.0)
        part = wide(key_mask[96 * b : 96 * (b + 1)]) * line
        penalty[96 * b : 96 * (b + 1), :] = jnp.where(part > 0.0, 0.0, MASKED)
    fetched[6].wait()

    def l_copy(i, dx, dy, arriving):
        peer, r, c = xy_peer(dx, dy)
        slot = peer if arriving else g
        return remote(send_l.at[i, peer], recv_l.at[i, slot], l_send.at[i, peer], l_recv.at[i, slot], r, c)

    def l_own(i):
        return pltpu.make_async_copy(send_l.at[i, g], recv_l.at[i, g], local.at[i])

    for i in range(OWN):
        r_own(i).wait()
        for dz, dl in COL_STEPS:
            r_copy(i, dz, dl, True).wait_recv()
        x_t = jnp.transpose(x_rows[i].astype(F32).reshape(N, C))
        xt[i] = x_t
        normed = norm_columns(x_t, gains[0]).astype(BF16)
        an_t[i] = normed
        own_token = row * 48 + col * OWN + i
        mine = jnp.sum(jnp.where(lane == own_token, mask, 0.0), axis=1, keepdims=True)
        factors = sigmoid(dot(w_g[...], normed)) * dot(w_v[...], normed) * (mask * mine)
        send_l[i] = factors.astype(BF16).reshape(GS, 16, N)
        for dx, dy in XY_STEPS:
            l_copy(i, dx, dy, False).start()
        l_own(i).start()
    for i in range(OWN):
        gate1[i] = sigmoid(dot(w_gate_t[...], an_t[i]))
    for i in range(OWN):
        for dz, dl in COL_STEPS:
            r_copy(i, dz, dl, False).wait_send()

    def z_copy(i, src, dst, send, recv, dz, arriving):
        peer = lax.rem(z + dz, ZS)
        slot = peer if arriving else z
        return remote(src.at[i, peer], dst.at[i, slot], send.at[i, peer], recv.at[i, slot], row, peer * 2 + x_lo)

    def z_own(i, src, dst):
        return pltpu.make_async_copy(src.at[i, z], dst.at[i, z], local.at[i])

    for i in range(OWN):
        l_own(i).wait()
        for dx, dy in XY_STEPS:
            l_copy(i, dx, dy, True).wait_recv()
        arrived = recv_l[i].astype(F32).reshape(GS * 16, N)
        for b in range(3):
            wide_t[b, i * 256 : (i + 1) * 256, :] = arrived[:, b * 128 : (b + 1) * 128]
        for ch in range(16):
            for b in range(3):
                piece = wide_t[b, pl.ds(i * 256 + ch, GS, stride=16), :]
                send_z[i, ch % 8, ch // 8, :, b * 128 : (b + 1) * 128] = piece.astype(BF16)
        for dz in Z_STEPS:
            z_copy(i, send_z, recv_z, z_send, z_recv, dz, False).start()
        z_own(i, send_z, recv_z).start()
    for i in range(OWN):
        for dx, dy in XY_STEPS:
            l_copy(i, dx, dy, False).wait_send()
    for i in range(OWN):
        z_own(i, send_z, recv_z).wait()
        for dz in Z_STEPS:
            z_copy(i, send_z, recv_z, z_send, z_recv, dz, True).wait_recv()

    right = dot(perm_ref[...], recv_z[:, :, 1].reshape(N, N)).astype(BF16)
    for i in range(OWN):
        left = recv_z[i, :, 0].reshape(ZS * GS, N)
        send_p[i] = dot_nt(left, right).astype(BF16).reshape(ZS, GS, N)
        for dz in Z_STEPS:
            z_copy(i, send_p, recv_p, p_send, p_recv, dz, False).start()
        z_own(i, send_p, recv_p).start()

    def x_copy(i, dx, dy, arriving):
        peer, r, c = xy_peer(dx, dy)
        slot = peer if arriving else g
        return remote(send_x.at[i, peer], recv_x.at[i, slot], x_send.at[i, peer], x_recv.at[i, slot], r, c)

    def x_own(i):
        return pltpu.make_async_copy(send_x.at[i, g], recv_x.at[i, g], local.at[i])

    for i in range(OWN):
        for dz in Z_STEPS:
            z_copy(i, send_z, recv_z, z_send, z_recv, dz, False).wait_send()
    for i in range(OWN):
        z_own(i, send_p, recv_p).wait()
        for dz in Z_STEPS:
            z_copy(i, send_p, recv_p, p_send, p_recv, dz, True).wait_recv()
        arrived = recv_p[i].astype(F32).reshape(ZS * GS, N)
        for b in range(3):
            wide_t[b, i * 128 : (i + 1) * 128, :] = arrived[:, b * 128 : (b + 1) * 128]
        for other in range(GS):
            for b in range(3):
                piece = wide_t[b, pl.ds(i * 128 + other, 8, stride=16), :]
                send_x[i, other, :, b * 128 : (b + 1) * 128] = piece.astype(BF16)
        for dx, dy in XY_STEPS:
            x_copy(i, dx, dy, False).start()
        x_own(i).start()

    b_at = y + crop * (x_at - y)
    a_at = x_at + crop * (y - x_at)
    for i in range(OWN):
        x_own(i).wait()
        for dx, dy in XY_STEPS:
            x_copy(i, dx, dy, True).wait_recv()
        product = recv_x[i].astype(F32).reshape(C, N)
        update = dot(w_o1_t[...], norm_columns(product, gains[1]).astype(BF16))
        middle = (xt[i] + gate1[i] * update).astype(BF16).astype(F32)
        mid[i] = middle
        attend = norm_columns(middle, gains[2]).astype(BF16)
        an_t[i] = attend
        bias_all[b_at, a_at, z, i] = dot(w_bias_ref[...], attend).astype(BF16)

    def bz_copy(dz, arriving):
        peer = lax.rem(z + dz, ZS)
        slot = peer if arriving else z
        return remote(
            bias_all.at[b_at, a_at, z], bias_all.at[b_at, a_at, slot], bz_send.at[peer], bz_recv.at[slot],
            row, peer * 2 + x_lo,
        )

    def ring_place(a, b):
        return place(a + crop * (b - a), b + crop * (a - b), z)

    def ba_copy(d, arriving):
        peer = lax.rem(a_at + d, 4)
        slot = peer if arriving else a_at
        r, c = ring_place(peer, b_at)
        return remote(bias_all.at[b_at, a_at], bias_all.at[b_at, slot], ba_send.at[peer], ba_recv.at[slot], r, c)

    def bb_copy(d, arriving):
        peer = lax.rem(b_at + d, 4)
        slot = peer if arriving else b_at
        r, c = ring_place(a_at, peer)
        return remote(bias_all.at[b_at], bias_all.at[slot], bb_send.at[peer], bb_recv.at[slot], r, c)

    for dz in Z_STEPS:
        bz_copy(dz, False).start()

    scale = LOG2E / math.sqrt(WIDTH)
    head_of = lax.broadcasted_iota(jnp.int32, (C, N), 0)

    def project(i):
        attend = an_t[i]
        queries = dot(w_qv_t[0], attend) * scale
        values_ref[i] = dot(w_qv_t[1], attend).astype(BF16)
        keys = jnp.transpose(dot(w_k_t[...], attend)).astype(BF16)
        gate2_ref[i] = sigmoid(dot(w_gate2_t[...], attend))
        for h in range(HEADS):
            inside = (head_of >= WIDTH * h) & (head_of < WIDTH * (h + 1))
            scores_ref[i, h] = dot(keys, jnp.where(inside, queries, 0.0).astype(BF16))

    project(0)
    for dz in Z_STEPS:
        bz_copy(dz, True).wait_recv()
    for d in RING_STEPS:
        ba_copy(d, False).start()
    project(1)
    for d in RING_STEPS:
        ba_copy(d, True).wait_recv()
    for d in RING_STEPS:
        bb_copy(d, False).start()
    project(2)
    for i in range(OWN):
        for dx, dy in XY_STEPS:
            x_copy(i, dx, dy, False).wait_send()
        for dz in Z_STEPS:
            z_copy(i, send_p, recv_p, p_send, p_recv, dz, False).wait_send()
    for d in RING_STEPS:
        bb_copy(d, True).wait_recv()
    for r in range(ROWS):
        for c in range(COLS):
            xx, yy = (r // 4) * 2 + c % 2, r % 4
            b_of, a_of = yy + crop * (xx - yy), xx + crop * (yy - xx)
            for i in range(OWN):
                piece = bias_all[b_of, a_of, c // 2, i].astype(F32)
                at = ((r * COLS + c) * OWN + i) * HEADS
                for b in range(3):
                    wide_t[b, at : at + HEADS, :] = piece[:, b * 128 : (b + 1) * 128]
    for h in range(HEADS):
        for b in range(3):
            part = wide_t[b, pl.ds(h, N, stride=HEADS), :]
            rows = slice(b * 128, (b + 1) * 128)
            bias_t[h, rows, :] = jnp.transpose(part) * LOG2E + penalty[rows, :]

    def o_copy(i, dz, dl, arriving):
        peer = col_peer(dz, dl)
        slot = peer if arriving else col
        return remote(send_o.at[i, peer], out_ref.at[OWN * slot + i], o_send.at[i, peer], o_recv.at[i, slot], row, peer)

    def o_own(i):
        return pltpu.make_async_copy(send_o.at[i, col], out_ref.at[OWN * col + i], local.at[i])

    for i in range(OWN):
        parts = []
        for h in range(HEADS):
            scores = scores_ref[i, h] + bias_t[h]
            weights = jnp.exp2(scores - jnp.max(scores, axis=0, keepdims=True))
            total = jnp.sum(weights, axis=0, keepdims=True)
            mixed = dot(values_ref[i, WIDTH * h : WIDTH * (h + 1)], weights.astype(BF16))
            parts.append(mixed / total)
        gated = (gate2_ref[i] * jnp.concatenate(parts, axis=0)).astype(BF16)
        result = mid[i] + dot(w_o2_t[...], gated)
        send_o[i] = jnp.transpose(result).reshape(COLS, 24, C).astype(BF16)
        for dz, dl in COL_STEPS:
            o_copy(i, dz, dl, False).start()
        o_own(i).start()

    for dz in Z_STEPS:
        bz_copy(dz, False).wait_send()
    for d in RING_STEPS:
        ba_copy(d, False).wait_send()
        bb_copy(d, False).wait_send()
    for i in range(OWN):
        o_own(i).wait()
        for dz, dl in COL_STEPS:
            o_copy(i, dz, dl, True).wait_recv()
    for i in range(OWN):
        for dz, dl in COL_STEPS:
            o_copy(i, dz, dl, False).wait_send()


def token_order():
    perm = np.zeros((N, N), np.float32)
    for t in range(N):
        r, c, i = t // 48, (t % 48) // 3, t % 3
        perm[t, i * ZS * GS + (c // 2) * GS + 2 * r + c % 2] = 1.0
    return perm


def shards(
    pair_state, token_mask, block_pattern, triangle_norm, triangle_input, triangle_gate, product_norm,
    triangle_output, attend_norm, attend_inputs, attend_gate, attend_bias, attend_output,
):
    vmem = pl.BlockSpec(memory_space=pltpu.VMEM)
    hbm = pl.BlockSpec(memory_space=pl.ANY)
    smem = pl.BlockSpec(memory_space=pltpu.SMEM)
    dma = pltpu.SemaphoreType.DMA
    V = pltpu.VMEM
    return pl.pallas_call(
        kernel,
        out_shape=jax.ShapeDtypeStruct(pair_state.shape, BF16),
        in_specs=[hbm, vmem, smem, hbm, vmem, hbm, hbm, vmem, hbm, vmem, hbm, hbm, vmem, hbm],
        out_specs=hbm,
        scratch_shapes=[
            V((OWN, COLS, 24, C), BF16),
            V((OWN, GS, 16, N), BF16), V((OWN, GS, 16, N), BF16),
            V((OWN, ZS, 2, GS, N), BF16), V((OWN, ZS, 2, GS, N), BF16),
            V((OWN, ZS, GS, N), BF16), V((OWN, ZS, GS, N), BF16),
            V((OWN, GS, 8, N), BF16), V((OWN, GS, 8, N), BF16),
            V((4, 4, ZS, OWN, HEADS, N), BF16),
            V((OWN, COLS, 24, C), BF16),
            V((OWN, C, N), F32), V((OWN, C, N), F32), V((OWN, C, N), F32), V((OWN, C, N), BF16),
            V((3, HEADS * N, 128), F32), V((HEADS, N, N), F32), V((N, N), F32),
            V((OWN, HEADS, N, N), F32), V((OWN, C, N), BF16), V((OWN, C, N), F32),
            V((N, N), BF16), V((C, 4 * C), BF16), V((C, C), BF16), V((C, C), BF16),
            V((C, 3 * C), BF16), V((C, C), BF16), V((C, C), BF16),
            V((2 * C, C), BF16), V((2 * C, C), BF16), V((C, C), BF16), V((C, C), BF16),
            V((2, C, C), BF16), V((C, C), BF16), V((C, C), BF16), V((C, C), BF16), V((3, C, C), F32),
            dma((OWN, COLS)), dma((OWN, COLS)), dma((OWN, GS)), dma((OWN, GS)), dma((OWN, ZS)), dma((OWN, ZS)),
            dma((OWN, ZS)), dma((OWN, ZS)), dma((OWN, GS)), dma((OWN, GS)),
            dma((ZS,)), dma((ZS,)), dma((4,)), dma((4,)), dma((4,)), dma((4,)),
            dma((OWN, COLS)), dma((OWN, COLS)), dma((OWN,)), dma((7,)),
        ],
        compiler_params=pltpu.CompilerParams(
            collective_id=0, has_side_effects=True, vmem_limit_bytes=40 * 1024 * 1024
        ),
        name="pairformer",
    )(
        pair_state, token_mask.reshape(1, N), block_pattern, jnp.asarray(token_order(), BF16),
        triangle_norm.reshape(1, C), triangle_input, triangle_gate, product_norm.reshape(1, C), triangle_output,
        attend_norm.reshape(1, C), attend_inputs, attend_gate, attend_bias.T, attend_output,
    )


def solution(mesh):
    tile = P(("crop", "row"), "col", None)
    return jax.shard_map(
        shards,
        mesh=mesh,
        in_specs=(tile, P("crop"), P("crop", None)) + (P(),) * 10,
        out_specs=tile,
        check_vma=False,
    )
```

```python
import functools
import math

import jax
import jax.numpy as jnp
import numpy as np
from jax import lax
from jax.experimental import pallas as pl
from jax.experimental.pallas import tpu as pltpu
from jax.sharding import PartitionSpec as P

MESH = pl.DeviceIdType.MESH
F32 = jnp.float32
BF16 = jnp.bfloat16
EPS = 1e-05
ROWS, COLS, C, N = 8, 16, 128, 384
HEADS, WIDTH = 4, 32
ZS, GS, OWN = 8, 16, 3
LOG2E = 1.4426950408889634
MASKED = -1e30


def dot(a, b):
    return jnp.dot(a, b, preferred_element_type=F32)


def dot_nt(a, b):
    return lax.dot_general(a, b, (((1,), (1,)), ((), ())), preferred_element_type=F32)


def dot_tn(a, b):
    return lax.dot_general(a, b, (((0,), (0,)), ((), ())), preferred_element_type=F32)


def wide(gain):
    return jnp.concatenate([gain] * (N // 128), axis=1)


def norm_columns(v, gain):
    centered = v - jnp.mean(v, axis=0, keepdims=True)
    variance = jnp.mean(centered * centered, axis=0, keepdims=True)
    return centered * lax.rsqrt(variance + EPS) * wide(gain)


def sigmoid(v):
    return 1.0 / (1.0 + jnp.exp(-v))


def far(dz):
    return int(dz in FAR)


def turned(w):
    return jnp.transpose(w.astype(F32))


RING_STEPS = (2, 1, 3)
NEAR, FAR = (1, 7, 2, 6), (3, 5, 4)
Z_STEPS = (4, 3, 5, 2, 6, 1, 7)
COL_STEPS = tuple((dz, dl) for dz in Z_STEPS for dl in (1, 0)) + ((0, 1),)
XY_STEPS = tuple(sorted(
    ((dx, dy) for dx in range(4) for dy in range(4) if dx or dy),
    key=lambda s: -(min(s[0], 4 - s[0]) + min(s[1], 4 - s[1])),
))


def kernel(
    x_hbm, mask_ref, pattern_ref, perm_hbm,
    norm1_ref, w_in_hbm, w_gate_hbm, norm2_ref, w_out1_hbm,
    norm3_ref, w_qkv_hbm, w_gate2_hbm, w_bias_ref, w_out2_hbm,
    out_ref,
    x_rows, send_l, recv_l, send_z, recv_z, send_p, recv_p, send_x, recv_x,
    bias_all, send_o, xt, gate1, mid, an_t, wide_t, bias_t, penalty, scores_ref, values_ref, gate2_ref,
    perm_ref, w_in_ref, w_gate_ref, w_out1_ref, w_qkv_ref, w_gate2_ref, w_out2_ref,
    w_g, w_v, w_gate_t, w_o1_t, w_qv_t, w_k_t, w_gate2_t, w_o2_t, gains,
    r_send, r_recv, l_send, l_recv, z_send, z_recv, p_send, p_recv, x_send, x_recv,
    bz_send, bz_recv, ba_send, ba_recv, bb_send, bb_recv, o_send, o_recv, fetch,
):
    crop, row, col = lax.axis_index("crop"), lax.axis_index("row"), lax.axis_index("col")
    z, x_lo = col // 2, col % 2
    x_hi, y = row // 4, row % 4
    g = row * 2 + x_lo
    x_at = x_hi * 2 + x_lo

    def place(x, y, z):
        return (x // 2) * 4 + y, z * 2 + x % 2

    def signal(r, c):
        pl.semaphore_signal(barrier, inc=1, device_id={"row": r, "col": c}, device_id_type=MESH)

    def remote(src, dst, send, recv, r, c):
        return pltpu.make_async_remote_copy(
            src_ref=src, dst_ref=dst, send_sem=send, recv_sem=recv,
            device_id={"row": r, "col": c}, device_id_type=MESH,
        )

    def arrive(ref, sem):
        pltpu.make_async_copy(ref, ref, sem).wait()

    def col_peer(dz, dl):
        return lax.rem(z + dz, ZS) * 2 + lax.rem(x_lo + dl, 2)

    def xy_peer(dx, dy):
        xx, yy = lax.rem(x_at + dx, 4), lax.rem(y + dy, 4)
        r, c = place(xx, yy, z)
        return r * 2 + xx % 2, r, c

    barrier = pltpu.get_barrier_semaphore()
    for dz, dl in COL_STEPS:
        signal(row, col_peer(dz, dl))
    for dx, dy in XY_STEPS:
        if (dx, dy) != (1, 0) and (dx, dy) != (3, 0) and (dx, dy) != (2, 0):
            _, r, c = xy_peer(dx, dy)
            signal(r, c)
    _, r, c = xy_peer(2, 0)
    signal(r, c)
    other = x_at + 1 + 2 * (1 - x_at % 2)
    r, c = place(lax.rem(other, 4), y, z)
    signal(r, c)

    fetched = [
        pltpu.make_async_copy(src, dst, fetch.at[n])
        for n, (src, dst) in enumerate((
            (w_in_hbm, w_in_ref), (w_gate_hbm, w_gate_ref), (w_out1_hbm, w_out1_ref), (w_qkv_hbm, w_qkv_ref),
            (w_gate2_hbm, w_gate2_ref), (w_out2_hbm, w_out2_ref), (perm_hbm, perm_ref),
        ))
    ]
    for copy in fetched:
        copy.start()

    fetched[0].wait()
    w_t = jnp.concatenate([turned(w_in_ref[:, s * C : (s + 1) * C]) for s in range(4)], axis=0)
    ga, va, gb, vb = (w_t[s * C : (s + 1) * C].reshape(GS, 8, C) for s in range(4))
    w_g[...] = jnp.concatenate([ga, gb], axis=1).reshape(2 * C, C).astype(BF16)
    w_v[...] = jnp.concatenate([va, vb], axis=1).reshape(2 * C, C).astype(BF16)
    for slot, ref in enumerate((norm1_ref, norm2_ref, norm3_ref)):
        gains[slot] = jnp.transpose(jnp.broadcast_to(ref[...], (C, C)))

    pl.semaphore_wait(barrier, COLS - 1 + 2 * (ROWS - 1))

    def r_copy(i, dz, dl):
        peer = col_peer(dz, dl)
        return remote(x_hbm.at[OWN * peer + i], x_rows.at[i, col], r_send, r_recv.at[i], row, peer)

    def r_own(i):
        return pltpu.make_async_copy(x_hbm.at[OWN * col + i], x_rows.at[i, col], r_recv.at[i])

    for i in range(OWN):
        for dz, dl in COL_STEPS:
            r_copy(i, dz, dl).start()
        r_own(i).start()

    for copy in fetched[1:6]:
        copy.wait()
    w_gate_t[...] = turned(w_gate_ref[...]).astype(BF16)
    w_o1_t[...] = turned(w_out1_ref[...]).astype(BF16)
    w_o2_t[...] = turned(w_out2_ref[...]).astype(BF16)
    w_gate2_t[...] = turned(w_gate2_ref[...]).astype(BF16)
    w_qv_t[0] = turned(w_qkv_ref[:, :C]).astype(BF16)
    w_qv_t[1] = turned(w_qkv_ref[:, 2 * C :]).astype(BF16)
    w_k_t[...] = turned(w_qkv_ref[:, C : 2 * C]).astype(BF16)
    mask = mask_ref[...].reshape(1, N).astype(F32)
    lane = lax.broadcasted_iota(jnp.int32, (1, N), 1)
    key_mask = jnp.transpose(jnp.broadcast_to(mask, (C, N)))
    for b in range(4):
        line = jnp.zeros((1, N), F32)
        for a in range(4):
            inside = (lane >= 96 * a) & (lane < 96 * (a + 1))
            line = line + jnp.where(inside, pattern_ref[a, b].astype(F32), 0.0)
        part = wide(key_mask[96 * b : 96 * (b + 1)]) * line
        penalty[96 * b : 96 * (b + 1), :] = jnp.where(part > 0.0, 0.0, MASKED)
    fetched[6].wait()

    def l_copy(i, dx, dy):
        peer, r, c = xy_peer(dx, dy)
        return remote(send_l.at[i, peer], recv_l.at[i, g], l_send, l_recv.at[i], r, c)

    def l_own(i):
        return pltpu.make_async_copy(send_l.at[i, g], recv_l.at[i, g], l_recv.at[i])

    for i in range(OWN):
        arrive(x_rows.at[i], r_recv.at[i])
        x_t = jnp.transpose(x_rows[i].astype(F32).reshape(N, C))
        xt[i] = x_t
        normed = norm_columns(x_t, gains[0]).astype(BF16)
        an_t[i] = normed
        own_token = row * 48 + col * OWN + i
        mine = jnp.sum(jnp.where(lane == own_token, mask, 0.0), axis=1, keepdims=True)
        factors = sigmoid(dot(w_g[...], normed)) * dot(w_v[...], normed) * (mask * mine)
        send_l[i] = factors.astype(BF16).reshape(GS, 16, N)
        for dx, dy in XY_STEPS:
            l_copy(i, dx, dy).start()
        l_own(i).start()
    for i in range(OWN):
        gate1[i] = sigmoid(dot(w_gate_t[...], an_t[i]))

    def z_copy(i, src, dst, send, recv, dz):
        peer = lax.rem(z + dz, ZS)
        return remote(src.at[i, peer], dst.at[i, z], send, recv, row, peer * 2 + x_lo)

    def z_own(i, src, dst, recv):
        return pltpu.make_async_copy(src.at[i, z], dst.at[i, z], recv)

    for i in range(OWN):
        arrive(recv_l.at[i], l_recv.at[i])
        arrived = recv_l[i].astype(F32).reshape(GS * 16, N)
        for b in range(3):
            wide_t[b, i * 256 : (i + 1) * 256, :] = arrived[:, b * 128 : (b + 1) * 128]
        for ch in range(16):
            for b in range(3):
                piece = wide_t[b, pl.ds(i * 256 + ch, GS, stride=16), :]
                send_z[i, ch % 8, ch // 8, :, b * 128 : (b + 1) * 128] = piece.astype(BF16)
        for dz in Z_STEPS:
            z_copy(i, send_z, recv_z, z_send, z_recv, dz).start()
        z_own(i, send_z, recv_z, z_recv).start()
    arrive(recv_z, z_recv)

    right = dot(perm_ref[...], recv_z[:, :, 1].reshape(N, N)).astype(BF16)
    for i in range(OWN):
        left = recv_z[i, :, 0].reshape(ZS * GS, N)
        send_p[i] = dot_nt(left, right).astype(BF16).reshape(ZS, GS, N)
        for dz in Z_STEPS:
            z_copy(i, send_p, recv_p, p_send, p_recv.at[i], dz).start()
        z_own(i, send_p, recv_p, p_recv.at[i]).start()

    def x_copy(i, dx, dy):
        peer, r, c = xy_peer(dx, dy)
        return remote(send_x.at[i, peer], recv_x.at[i, g], x_send, x_recv.at[i], r, c)

    def x_own(i):
        return pltpu.make_async_copy(send_x.at[i, g], recv_x.at[i, g], x_recv.at[i])

    for i in range(OWN):
        arrive(recv_p.at[i], p_recv.at[i])
        arrived = recv_p[i].astype(F32).reshape(ZS * GS, N)
        for b in range(3):
            wide_t[b, i * 128 : (i + 1) * 128, :] = arrived[:, b * 128 : (b + 1) * 128]
        for other in range(GS):
            for b in range(3):
                piece = wide_t[b, pl.ds(i * 128 + other, 8, stride=16), :]
                send_x[i, other, :, b * 128 : (b + 1) * 128] = piece.astype(BF16)
        for dx, dy in XY_STEPS:
            x_copy(i, dx, dy).start()
        x_own(i).start()

    b_at = y + crop * (x_at - y)
    a_at = x_at + crop * (y - x_at)
    for i in range(OWN):
        arrive(recv_x.at[i], x_recv.at[i])
        product = recv_x[i].astype(F32).reshape(C, N)
        update = dot(w_o1_t[...], norm_columns(product, gains[1]).astype(BF16))
        middle = (xt[i] + gate1[i] * update).astype(BF16).astype(F32)
        mid[i] = middle
        attend = norm_columns(middle, gains[2]).astype(BF16)
        an_t[i] = attend
        bias_all[b_at, a_at, z, i] = dot(w_bias_ref[...], attend).astype(BF16)

    def ring_place(a, b, z):
        return place(a + crop * (b - a), b + crop * (a - b), z)

    def bz_copy(dz):
        ref = bias_all.at[b_at, a_at, z]
        r, c = ring_place(a_at, b_at, lax.rem(z + dz, ZS))
        return remote(ref, ref, bz_send, bz_recv.at[far(dz)], r, c)

    def ba_copy(dz, d):
        ref = bias_all.at[b_at, a_at, lax.rem(z + dz, ZS)]
        r, c = ring_place(lax.rem(a_at + d, 4), b_at, z)
        return remote(ref, ref, ba_send, ba_recv.at[far(dz)], r, c)

    def bb_copy(dz, da, d):
        ref = bias_all.at[b_at, lax.rem(a_at + da, 4), lax.rem(z + dz, ZS)]
        r, c = ring_place(a_at, lax.rem(b_at + d, 4), z)
        return remote(ref, ref, bb_send, bb_recv, r, c)

    def pass_on(group):
        for dz in group:
            for d in RING_STEPS:
                ba_copy(dz, d).start()
        for dz in group:
            for d in RING_STEPS:
                bb_copy(dz, 0, d).start()

    def pass_on_b(group):
        for da in RING_STEPS:
            for dz in group:
                for d in RING_STEPS:
                    bb_copy(dz, da, d).start()

    for dz in Z_STEPS:
        bz_copy(dz).start()
    pass_on((0,))

    scale = LOG2E / math.sqrt(WIDTH)
    head_of = lax.broadcasted_iota(jnp.int32, (C, N), 0)

    def project(i):
        attend = an_t[i]
        queries = dot(w_qv_t[0], attend) * scale
        values_ref[i] = dot(w_qv_t[1], attend).astype(BF16)
        keys = jnp.transpose(dot(w_k_t[...], attend)).astype(BF16)
        gate2_ref[i] = sigmoid(dot(w_gate2_t[...], attend))
        for h in range(HEADS):
            inside = (head_of >= WIDTH * h) & (head_of < WIDTH * (h + 1))
            scores_ref[i, h] = dot(keys, jnp.where(inside, queries, 0.0).astype(BF16))

    project(0)
    arrive(bias_all.at[0, 0, :4], bz_recv.at[0])
    pass_on(NEAR)
    arrive(bias_all.at[0, 0, :3], bz_recv.at[1])
    pass_on(FAR)
    project(1)
    arrive(bias_all.at[0, :3, :5], ba_recv.at[0])
    pass_on_b((0,) + NEAR)
    arrive(bias_all.at[0, :3, :3], ba_recv.at[1])
    pass_on_b(FAR)
    project(2)
    arrive(bias_all.at[:3], bb_recv)
    for r in range(ROWS):
        for c in range(COLS):
            xx, yy = (r // 4) * 2 + c % 2, r % 4
            b_of, a_of = yy + crop * (xx - yy), xx + crop * (yy - xx)
            for i in range(OWN):
                piece = bias_all[b_of, a_of, c // 2, i].astype(F32)
                at = ((r * COLS + c) * OWN + i) * HEADS
                for b in range(3):
                    wide_t[b, at : at + HEADS, :] = piece[:, b * 128 : (b + 1) * 128]
    for h in range(HEADS):
        for b in range(3):
            part = wide_t[b, pl.ds(h, N, stride=HEADS), :]
            rows = slice(b * 128, (b + 1) * 128)
            bias_t[h, rows, :] = jnp.transpose(part) * LOG2E + penalty[rows, :]

    def o_copy(i, dz, dl):
        peer = col_peer(dz, dl)
        return remote(send_o.at[i, peer], out_ref.at[OWN * col + i], o_send, o_recv, row, peer)

    def o_own(i):
        return pltpu.make_async_copy(send_o.at[i, col], out_ref.at[OWN * col + i], o_recv)

    for i in range(OWN):
        parts = []
        for h in range(HEADS):
            scores = scores_ref[i, h] + bias_t[h]
            weights = jnp.exp2(scores - jnp.max(scores, axis=0, keepdims=True))
            total = jnp.sum(weights, axis=0, keepdims=True)
            mixed = dot(values_ref[i, WIDTH * h : WIDTH * (h + 1)], weights.astype(BF16))
            parts.append(mixed / total)
        gated = (gate2_ref[i] * jnp.concatenate(parts, axis=0)).astype(BF16)
        result = mid[i] + dot(w_o2_t[...], gated)
        send_o[i] = jnp.transpose(result).reshape(COLS, 24, C).astype(BF16)
        for dz, dl in COL_STEPS:
            o_copy(i, dz, dl).start()
        o_own(i).start()

    arrive(x_rows.at[:, :15], r_send)
    arrive(send_l.at[:, :15], l_send)
    arrive(send_z.at[:, :7], z_send)
    arrive(send_p.at[:, :7], p_send)
    arrive(send_x.at[:, :15], x_send)
    arrive(bias_all.at[0, 0, :7], bz_send)
    arrive(bias_all.at[0, :3], ba_send)
    arrive(bias_all.at[:3], bb_send)
    arrive(send_o.at[:, :15], o_send)
    arrive(out_ref, o_recv)


def token_order():
    perm = np.zeros((N, N), np.float32)
    for t in range(N):
        r, c, i = t // 48, (t % 48) // 3, t % 3
        perm[t, i * ZS * GS + (c // 2) * GS + 2 * r + c % 2] = 1.0
    return perm


def shards(
    pair_state, token_mask, block_pattern, triangle_norm, triangle_input, triangle_gate, product_norm,
    triangle_output, attend_norm, attend_inputs, attend_gate, attend_bias, attend_output,
):
    vmem = pl.BlockSpec(memory_space=pltpu.VMEM)
    hbm = pl.BlockSpec(memory_space=pl.ANY)
    smem = pl.BlockSpec(memory_space=pltpu.SMEM)
    dma = pltpu.SemaphoreType.DMA
    V = pltpu.VMEM
    return pl.pallas_call(
        kernel,
        out_shape=jax.ShapeDtypeStruct(pair_state.shape, BF16),
        in_specs=[hbm, vmem, smem, hbm, vmem, hbm, hbm, vmem, hbm, vmem, hbm, hbm, vmem, hbm],
        out_specs=hbm,
        scratch_shapes=[
            V((OWN, COLS, 24, C), BF16),
            V((OWN, GS, 16, N), BF16), V((OWN, GS, 16, N), BF16),
            V((OWN, ZS, 2, GS, N), BF16), V((OWN, ZS, 2, GS, N), BF16),
            V((OWN, ZS, GS, N), BF16), V((OWN, ZS, GS, N), BF16),
            V((OWN, GS, 8, N), BF16), V((OWN, GS, 8, N), BF16),
            V((4, 4, ZS, OWN, HEADS, N), BF16),
            V((OWN, COLS, 24, C), BF16),
            V((OWN, C, N), F32), V((OWN, C, N), F32), V((OWN, C, N), F32), V((OWN, C, N), BF16),
            V((3, HEADS * N, 128), F32), V((HEADS, N, N), F32), V((N, N), F32),
            V((OWN, HEADS, N, N), F32), V((OWN, C, N), BF16), V((OWN, C, N), F32),
            V((N, N), BF16), V((C, 4 * C), BF16), V((C, C), BF16), V((C, C), BF16),
            V((C, 3 * C), BF16), V((C, C), BF16), V((C, C), BF16),
            V((2 * C, C), BF16), V((2 * C, C), BF16), V((C, C), BF16), V((C, C), BF16),
            V((2, C, C), BF16), V((C, C), BF16), V((C, C), BF16), V((C, C), BF16), V((3, C, C), F32),
            dma, dma((OWN,)), dma, dma((OWN,)), dma, dma, dma, dma((OWN,)), dma, dma((OWN,)),
            dma, dma((2,)), dma, dma((2,)), dma, dma, dma, dma, dma((7,)),
        ],
        compiler_params=pltpu.CompilerParams(
            collective_id=0, has_side_effects=True, vmem_limit_bytes=63 * 1024 * 1024
        ),
        name="pairformer",
    )(
        pair_state, token_mask, block_pattern, jnp.asarray(token_order(), BF16),
        triangle_norm.reshape(1, C), triangle_input, triangle_gate, product_norm.reshape(1, C), triangle_output,
        attend_norm.reshape(1, C), attend_inputs, attend_gate, attend_bias.T, attend_output,
    )


def solution(mesh):
    tile = P(("crop", "row"), "col", None)
    return jax.shard_map(
        shards,
        mesh=mesh,
        in_specs=(tile, P("crop"), P("crop", None)) + (P(),) * 10,
        out_specs=tile,
        check_vma=False,
    )
```

```python
import functools
import math

import jax
import jax.numpy as jnp
import numpy as np
from jax import lax
from jax.experimental import pallas as pl
from jax.experimental.pallas import tpu as pltpu
from jax.sharding import PartitionSpec as P

MESH = pl.DeviceIdType.MESH
F32 = jnp.float32
BF16 = jnp.bfloat16
EPS = 1e-05
ROWS, COLS, C, N = 8, 16, 128, 384
HEADS, WIDTH = 4, 32
ZS, GS, OWN = 8, 16, 3
LOG2E = 1.4426950408889634
MASKED = -1e30


def dot(a, b):
    return jnp.dot(a, b, preferred_element_type=F32)


def dot_nt(a, b):
    return lax.dot_general(a, b, (((1,), (1,)), ((), ())), preferred_element_type=F32)


def dot_tn(a, b):
    return lax.dot_general(a, b, (((0,), (0,)), ((), ())), preferred_element_type=F32)


def wide(gain):
    return jnp.concatenate([gain] * (N // 128), axis=1)


def norm_columns(v, gain):
    centered = v - jnp.mean(v, axis=0, keepdims=True)
    variance = jnp.mean(centered * centered, axis=0, keepdims=True)
    return centered * lax.rsqrt(variance + EPS) * wide(gain)


def sigmoid(v):
    return 1.0 / (1.0 + jnp.exp(-v))


def turned(w):
    return jnp.transpose(w.astype(F32))


RING_STEPS = (2, 1, 3)
Z_STEPS = (4, 3, 5, 2, 6, 1, 7)
COL_STEPS = tuple((dz, dl) for dz in Z_STEPS for dl in (1, 0)) + ((0, 1),)
XY_STEPS = tuple(sorted(
    ((dx, dy) for dx in range(4) for dy in range(4) if dx or dy),
    key=lambda s: -(min(s[0], 4 - s[0]) + min(s[1], 4 - s[1])),
))


def kernel(
    x_hbm, mask_ref, pattern_ref, perm_hbm,
    norm1_ref, w_in_hbm, w_gate_hbm, norm2_ref, w_out1_hbm,
    norm3_ref, w_qkv_hbm, w_gate2_hbm, w_bias_ref, w_out2_hbm,
    out_ref,
    x_rows, send_l, recv_l, send_z, recv_z, send_p, recv_p, send_x, recv_x,
    bias_all, send_o, xt, gate1, mid, an_t, wide_t, bias_t, penalty, scores_ref, values_ref, gate2_ref,
    x_ref, perm_ref, w_in_ref, w_gate_ref, w_out1_ref, w_qkv_ref, w_gate2_ref, w_out2_ref,
    w_g, w_v, w_gate_t, w_o1_t, w_qv_t, w_k_t, w_gate2_t, w_o2_t, gains,
    r_send, r_recv, l_send, l_recv, z_send, z_recv, p_send, p_recv, x_send, x_recv,
    bz_send, bz_recv, ba_send, ba_recv, bb_send, bb_recv, o_send, o_recv, fetch,
):
    crop, row, col = lax.axis_index("crop"), lax.axis_index("row"), lax.axis_index("col")
    z, x_lo = col // 2, col % 2
    x_hi, y = row // 4, row % 4
    g = row * 2 + x_lo
    x_at = x_hi * 2 + x_lo

    def place(x, y, z):
        return (x // 2) * 4 + y, z * 2 + x % 2

    def signal(r, c):
        pl.semaphore_signal(barrier, inc=1, device_id={"row": r, "col": c}, device_id_type=MESH)

    def remote(src, dst, send, recv, r, c):
        return pltpu.make_async_remote_copy(
            src_ref=src, dst_ref=dst, send_sem=send, recv_sem=recv,
            device_id={"row": r, "col": c}, device_id_type=MESH,
        )

    def arrive(ref, sem):
        pltpu.make_async_copy(ref, ref, sem).wait()

    def col_peer(dz, dl):
        return lax.rem(z + dz, ZS) * 2 + lax.rem(x_lo + dl, 2)

    def xy_peer(dx, dy):
        xx, yy = lax.rem(x_at + dx, 4), lax.rem(y + dy, 4)
        r, c = place(xx, yy, z)
        return r * 2 + xx % 2, r, c

    barrier = pltpu.get_barrier_semaphore()
    for dz, dl in COL_STEPS:
        signal(row, col_peer(dz, dl))
    for dx, dy in XY_STEPS:
        if (dx, dy) != (1, 0) and (dx, dy) != (3, 0) and (dx, dy) != (2, 0):
            _, r, c = xy_peer(dx, dy)
            signal(r, c)
    _, r, c = xy_peer(2, 0)
    signal(r, c)
    other = x_at + 1 + 2 * (1 - x_at % 2)
    r, c = place(lax.rem(other, 4), y, z)
    signal(r, c)

    fetched = [
        pltpu.make_async_copy(src, dst, fetch.at[n])
        for n, (src, dst) in enumerate((
            (w_in_hbm, w_in_ref), (w_gate_hbm, w_gate_ref), (w_out1_hbm, w_out1_ref), (w_qkv_hbm, w_qkv_ref),
            (w_gate2_hbm, w_gate2_ref), (w_out2_hbm, w_out2_ref), (perm_hbm, perm_ref), (x_hbm, x_ref),
        ))
    ]
    for copy in fetched:
        copy.start()

    fetched[0].wait()
    w_t = jnp.concatenate([turned(w_in_ref[:, s * C : (s + 1) * C]) for s in range(4)], axis=0)
    ga, va, gb, vb = (w_t[s * C : (s + 1) * C].reshape(GS, 8, C) for s in range(4))
    w_g[...] = jnp.concatenate([ga, gb], axis=1).reshape(2 * C, C).astype(BF16)
    w_v[...] = jnp.concatenate([va, vb], axis=1).reshape(2 * C, C).astype(BF16)
    for slot, ref in enumerate((norm1_ref, norm2_ref, norm3_ref)):
        gains[slot] = jnp.transpose(jnp.broadcast_to(ref[...], (C, C)))

    fetched[7].wait()
    pl.semaphore_wait(barrier, COLS - 1 + 2 * (ROWS - 1))

    def r_copy(i, dz, dl):
        peer = col_peer(dz, dl)
        return remote(x_ref.at[OWN * peer + i], x_rows.at[i, col], r_send, r_recv.at[i], row, peer)

    def r_own(i):
        return pltpu.make_async_copy(x_ref.at[OWN * col + i], x_rows.at[i, col], r_recv.at[i])

    for i in range(OWN):
        for dz, dl in COL_STEPS:
            r_copy(i, dz, dl).start()
        r_own(i).start()

    for copy in fetched[1:6]:
        copy.wait()
    w_gate_t[...] = turned(w_gate_ref[...]).astype(BF16)
    w_o1_t[...] = turned(w_out1_ref[...]).astype(BF16)
    w_o2_t[...] = turned(w_out2_ref[...]).astype(BF16)
    w_gate2_t[...] = turned(w_gate2_ref[...]).astype(BF16)
    w_qv_t[0] = turned(w_qkv_ref[:, :C]).astype(BF16)
    w_qv_t[1] = turned(w_qkv_ref[:, 2 * C :]).astype(BF16)
    w_k_t[...] = turned(w_qkv_ref[:, C : 2 * C]).astype(BF16)
    mask = mask_ref[...].reshape(1, N).astype(F32)
    lane = lax.broadcasted_iota(jnp.int32, (1, N), 1)
    key_mask = jnp.transpose(jnp.broadcast_to(mask, (C, N)))
    for b in range(4):
        line = jnp.zeros((1, N), F32)
        for a in range(4):
            inside = (lane >= 96 * a) & (lane < 96 * (a + 1))
            line = line + jnp.where(inside, pattern_ref[a, b].astype(F32), 0.0)
        part = wide(key_mask[96 * b : 96 * (b + 1)]) * line
        penalty[96 * b : 96 * (b + 1), :] = jnp.where(part > 0.0, 0.0, MASKED)
    fetched[6].wait()

    def l_copy(i, dx, dy):
        peer, r, c = xy_peer(dx, dy)
        return remote(send_l.at[i, peer], recv_l.at[i, g], l_send, l_recv.at[i], r, c)

    def l_own(i):
        return pltpu.make_async_copy(send_l.at[i, g], recv_l.at[i, g], l_recv.at[i])

    for i in range(OWN):
        arrive(x_rows.at[i], r_recv.at[i])
        x_t = jnp.transpose(x_rows[i].astype(F32).reshape(N, C))
        xt[i] = x_t
        normed = norm_columns(x_t, gains[0]).astype(BF16)
        an_t[i] = normed
        own_token = row * 48 + col * OWN + i
        mine = jnp.sum(jnp.where(lane == own_token, mask, 0.0), axis=1, keepdims=True)
        factors = sigmoid(dot(w_g[...], normed)) * dot(w_v[...], normed) * (mask * mine)
        send_l[i] = factors.astype(BF16).reshape(GS, 16, N)
        for dx, dy in XY_STEPS:
            l_copy(i, dx, dy).start()
        l_own(i).start()
    for i in range(OWN):
        gate1[i] = sigmoid(dot(w_gate_t[...], an_t[i]))

    def z_copy(i, src, dst, send, recv, dz):
        peer = lax.rem(z + dz, ZS)
        return remote(src.at[i, peer], dst.at[i, z], send, recv, row, peer * 2 + x_lo)

    def z_own(i, src, dst, recv):
        return pltpu.make_async_copy(src.at[i, z], dst.at[i, z], recv)

    for i in range(OWN):
        arrive(recv_l.at[i], l_recv.at[i])
        arrived = recv_l[i].astype(F32).reshape(GS * 16, N)
        for b in range(3):
            wide_t[b, i * 256 : (i + 1) * 256, :] = arrived[:, b * 128 : (b + 1) * 128]
        for ch in range(16):
            for b in range(3):
                piece = wide_t[b, pl.ds(i * 256 + ch, GS, stride=16), :]
                send_z[i, ch % 8, ch // 8, :, b * 128 : (b + 1) * 128] = piece.astype(BF16)
        for dz in Z_STEPS:
            z_copy(i, send_z, recv_z, z_send, z_recv, dz).start()
        z_own(i, send_z, recv_z, z_recv).start()
    arrive(recv_z, z_recv)

    right = dot(perm_ref[...], recv_z[:, :, 1].reshape(N, N)).astype(BF16)
    for i in range(OWN):
        left = recv_z[i, :, 0].reshape(ZS * GS, N)
        send_p[i] = dot_nt(left, right).astype(BF16).reshape(ZS, GS, N)
        for dz in Z_STEPS:
            z_copy(i, send_p, recv_p, p_send, p_recv.at[i], dz).start()
        z_own(i, send_p, recv_p, p_recv.at[i]).start()

    def x_copy(i, dx, dy):
        peer, r, c = xy_peer(dx, dy)
        return remote(send_x.at[i, peer], recv_x.at[i, g], x_send, x_recv.at[i], r, c)

    def x_own(i):
        return pltpu.make_async_copy(send_x.at[i, g], recv_x.at[i, g], x_recv.at[i])

    for i in range(OWN):
        arrive(recv_p.at[i], p_recv.at[i])
        arrived = recv_p[i].astype(F32).reshape(ZS * GS, N)
        for b in range(3):
            wide_t[b, i * 128 : (i + 1) * 128, :] = arrived[:, b * 128 : (b + 1) * 128]
        for other in range(GS):
            for b in range(3):
                piece = wide_t[b, pl.ds(i * 128 + other, 8, stride=16), :]
                send_x[i, other, :, b * 128 : (b + 1) * 128] = piece.astype(BF16)
        for dx, dy in XY_STEPS:
            x_copy(i, dx, dy).start()
        x_own(i).start()

    b_at = y + crop * (x_at - y)
    a_at = x_at + crop * (y - x_at)
    def ring_place(a, b, z):
        return place(a + crop * (b - a), b + crop * (a - b), z)

    def bz_copy(i, dz):
        ref = bias_all.at[i, b_at, a_at, z]
        r, c = ring_place(a_at, b_at, lax.rem(z + dz, ZS))
        return remote(ref, ref, bz_send, bz_recv.at[i], r, c)

    def ba_copy(i, d):
        ref = bias_all.at[i, b_at, a_at]
        r, c = ring_place(lax.rem(a_at + d, 4), b_at, z)
        return remote(ref, ref, ba_send, ba_recv.at[i], r, c)

    def bb_copy(i, da, d):
        ref = bias_all.at[i, b_at, lax.rem(a_at + da, 4)]
        r, c = ring_place(a_at, lax.rem(b_at + d, 4), z)
        return remote(ref, ref, bb_send, bb_recv.at[i], r, c)

    for i in range(OWN):
        arrive(recv_x.at[i], x_recv.at[i])
        product = recv_x[i].astype(F32).reshape(C, N)
        update = dot(w_o1_t[...], norm_columns(product, gains[1]).astype(BF16))
        middle = (xt[i] + gate1[i] * update).astype(BF16).astype(F32)
        mid[i] = middle
        attend = norm_columns(middle, gains[2]).astype(BF16)
        an_t[i] = attend
        bias_all[i, b_at, a_at, z] = dot(w_bias_ref[...], attend).astype(BF16)
        for dz in Z_STEPS:
            bz_copy(i, dz).start()

    scale = LOG2E / math.sqrt(WIDTH)
    head_of = lax.broadcasted_iota(jnp.int32, (C, N), 0)

    def project(i):
        attend = an_t[i]
        queries = dot(w_qv_t[0], attend) * scale
        values_ref[i] = dot(w_qv_t[1], attend).astype(BF16)
        keys = jnp.transpose(dot(w_k_t[...], attend)).astype(BF16)
        gate2_ref[i] = sigmoid(dot(w_gate2_t[...], attend))
        for h in range(HEADS):
            inside = (head_of >= WIDTH * h) & (head_of < WIDTH * (h + 1))
            scores_ref[i, h] = dot(keys, jnp.where(inside, queries, 0.0).astype(BF16))

    project(0)
    for i in range(OWN):
        arrive(bias_all.at[i, 0, 0, :7], bz_recv.at[i])
        for d in RING_STEPS:
            ba_copy(i, d).start()
        for d in RING_STEPS:
            bb_copy(i, 0, d).start()
    project(1)
    for i in range(OWN):
        arrive(bias_all.at[i, 0, :3], ba_recv.at[i])
        for da in RING_STEPS:
            for d in RING_STEPS:
                bb_copy(i, da, d).start()
    project(2)
    for i in range(OWN):
        arrive(bias_all.at[i, :3], bb_recv.at[i])
        for r in range(ROWS):
            for c in range(COLS):
                xx, yy = (r // 4) * 2 + c % 2, r % 4
                b_of, a_of = yy + crop * (xx - yy), xx + crop * (yy - xx)
                piece = bias_all[i, b_of, a_of, c // 2].astype(F32)
                at = ((r * COLS + c) * OWN + i) * HEADS
                for b in range(3):
                    wide_t[b, at : at + HEADS, :] = piece[:, b * 128 : (b + 1) * 128]
    for h in range(HEADS):
        for b in range(3):
            part = wide_t[b, pl.ds(h, N, stride=HEADS), :]
            rows = slice(b * 128, (b + 1) * 128)
            bias_t[h, rows, :] = jnp.transpose(part) * LOG2E + penalty[rows, :]

    def o_copy(i, dz, dl):
        peer = col_peer(dz, dl)
        return remote(send_o.at[i, peer], out_ref.at[OWN * col + i], o_send, o_recv, row, peer)

    def o_own(i):
        return pltpu.make_async_copy(send_o.at[i, col], out_ref.at[OWN * col + i], o_recv)

    for i in range(OWN):
        parts = []
        for h in range(HEADS):
            scores = scores_ref[i, h] + bias_t[h]
            weights = jnp.exp2(scores - jnp.max(scores, axis=0, keepdims=True))
            total = jnp.sum(weights, axis=0, keepdims=True)
            mixed = dot(values_ref[i, WIDTH * h : WIDTH * (h + 1)], weights.astype(BF16))
            parts.append(mixed / total)
        gated = (gate2_ref[i] * jnp.concatenate(parts, axis=0)).astype(BF16)
        result = mid[i] + dot(w_o2_t[...], gated)
        send_o[i] = jnp.transpose(result).reshape(COLS, 24, C).astype(BF16)
        for dz, dl in COL_STEPS:
            o_copy(i, dz, dl).start()
        o_own(i).start()

    arrive(x_rows.at[:, :15], r_send)
    arrive(send_l.at[:, :15], l_send)
    arrive(send_z.at[:, :7], z_send)
    arrive(send_p.at[:, :7], p_send)
    arrive(send_x.at[:, :15], x_send)
    arrive(bias_all.at[:, 0, 0, :7], bz_send)
    arrive(bias_all.at[:, 0, :3], ba_send)
    arrive(bias_all.at[:, :3], bb_send)
    arrive(send_o.at[:, :15], o_send)
    arrive(out_ref, o_recv)


def token_order():
    perm = np.zeros((N, N), np.float32)
    for t in range(N):
        r, c, i = t // 48, (t % 48) // 3, t % 3
        perm[t, i * ZS * GS + (c // 2) * GS + 2 * r + c % 2] = 1.0
    return perm


def shards(
    pair_state, token_mask, block_pattern, triangle_norm, triangle_input, triangle_gate, product_norm,
    triangle_output, attend_norm, attend_inputs, attend_gate, attend_bias, attend_output,
):
    vmem = pl.BlockSpec(memory_space=pltpu.VMEM)
    hbm = pl.BlockSpec(memory_space=pl.ANY)
    smem = pl.BlockSpec(memory_space=pltpu.SMEM)
    dma = pltpu.SemaphoreType.DMA
    V = pltpu.VMEM
    return pl.pallas_call(
        kernel,
        out_shape=jax.ShapeDtypeStruct(pair_state.shape, BF16),
        in_specs=[hbm, vmem, smem, hbm, vmem, hbm, hbm, vmem, hbm, vmem, hbm, hbm, vmem, hbm],
        out_specs=hbm,
        scratch_shapes=[
            V((OWN, COLS, 24, C), BF16),
            V((OWN, GS, 16, N), BF16), V((OWN, GS, 16, N), BF16),
            V((OWN, ZS, 2, GS, N), BF16), V((OWN, ZS, 2, GS, N), BF16),
            V((OWN, ZS, GS, N), BF16), V((OWN, ZS, GS, N), BF16),
            V((OWN, GS, 8, N), BF16), V((OWN, GS, 8, N), BF16),
            V((OWN, 4, 4, ZS, HEADS, N), BF16),
            V((OWN, COLS, 24, C), BF16),
            V((OWN, C, N), F32), V((OWN, C, N), F32), V((OWN, C, N), F32), V((OWN, C, N), BF16),
            V((3, HEADS * N, 128), F32), V((HEADS, N, N), F32), V((N, N), F32),
            V((OWN, HEADS, N, N), F32), V((OWN, C, N), BF16), V((OWN, C, N), F32),
            V((48, 24, C), BF16), V((N, N), BF16), V((C, 4 * C), BF16), V((C, C), BF16), V((C, C), BF16),
            V((C, 3 * C), BF16), V((C, C), BF16), V((C, C), BF16),
            V((2 * C, C), BF16), V((2 * C, C), BF16), V((C, C), BF16), V((C, C), BF16),
            V((2, C, C), BF16), V((C, C), BF16), V((C, C), BF16), V((C, C), BF16), V((3, C, C), F32),
            dma, dma((OWN,)), dma, dma((OWN,)), dma, dma, dma, dma((OWN,)), dma, dma((OWN,)),
            dma, dma((OWN,)), dma, dma((OWN,)), dma, dma((OWN,)), dma, dma, dma((8,)),
        ],
        compiler_params=pltpu.CompilerParams(
            collective_id=0, has_side_effects=True, vmem_limit_bytes=63 * 1024 * 1024
        ),
        name="pairformer",
    )(
        pair_state, token_mask, block_pattern, jnp.asarray(token_order(), BF16),
        triangle_norm.reshape(1, C), triangle_input, triangle_gate, product_norm.reshape(1, C), triangle_output,
        attend_norm.reshape(1, C), attend_inputs, attend_gate, attend_bias.T, attend_output,
    )


def solution(mesh):
    tile = P(("crop", "row"), "col", None)
    return jax.shard_map(
        shards,
        mesh=mesh,
        in_specs=(tile, P("crop"), P("crop", None)) + (P(),) * 10,
        out_specs=tile,
        check_vma=False,
    )
```

```python
import functools
import math

import jax
import jax.numpy as jnp
import numpy as np
from jax import lax
from jax.experimental import pallas as pl
from jax.experimental.pallas import tpu as pltpu
from jax.sharding import PartitionSpec as P

MESH = pl.DeviceIdType.MESH
F32 = jnp.float32
BF16 = jnp.bfloat16
EPS = 1e-05
ROWS, COLS, C, N = 8, 16, 128, 384
HEADS, WIDTH = 4, 32
ZS, GS, OWN = 8, 16, 3
LOG2E = 1.4426950408889634
MASKED = -1e30


def dot(a, b):
    return jnp.dot(a, b, preferred_element_type=F32)


def dot_nt(a, b):
    return lax.dot_general(a, b, (((1,), (1,)), ((), ())), preferred_element_type=F32)


def dot_tn(a, b):
    return lax.dot_general(a, b, (((0,), (0,)), ((), ())), preferred_element_type=F32)


def wide(gain):
    return jnp.concatenate([gain] * (N // 128), axis=1)


def norm_columns(v, gain):
    centered = v - jnp.mean(v, axis=0, keepdims=True)
    variance = jnp.mean(centered * centered, axis=0, keepdims=True)
    return centered * lax.rsqrt(variance + EPS) * wide(gain)


def sigmoid(v):
    return 1.0 / (1.0 + jnp.exp(-v))


def turned(w):
    return jnp.transpose(w.astype(F32))


RING_STEPS = (2, 1, 3)
Z_STEPS = (4, 3, 5, 2, 6, 1, 7)
COL_STEPS = tuple((dz, dl) for dz in Z_STEPS for dl in (1, 0)) + ((0, 1),)
XY_STEPS = tuple(sorted(
    ((dx, dy) for dx in range(4) for dy in range(4) if dx or dy),
    key=lambda s: -(min(s[0], 4 - s[0]) + min(s[1], 4 - s[1])),
))


def kernel(
    x_hbm, mask_ref, pattern_ref, perm_hbm,
    norm1_ref, w_in_hbm, w_gate_hbm, norm2_ref, w_out1_hbm,
    norm3_ref, w_qkv_hbm, w_gate2_hbm, w_bias_ref, w_out2_hbm,
    out_ref,
    x_rows, send_l, recv_l, send_z, recv_z, send_p, recv_p, send_x, recv_x,
    bias_all, send_o, xt, gate1, mid, an_t, wide_t, bias_t, penalty, scores_ref, values_ref, gate2_ref,
    x_ref, perm_ref, w_in_ref, w_gate_ref, w_out1_ref, w_qkv_ref, w_gate2_ref, w_out2_ref,
    w_g, w_v, w_gate_t, w_o1_t, w_qv_t, w_k_t, w_gate2_t, w_o2_t, gains,
    r_send, r_recv, l_send, l_recv, z_send, z_recv, p_send, p_recv, x_send, x_recv,
    bz_send, bz_recv, ba_send, bx_recv, by_recv, bb_send, bb_recv, o_send, o_recv, fetch,
):
    row, col = lax.axis_index("row"), lax.axis_index("col")
    z, x_lo = col // 2, col % 2
    x_hi, y = row // 4, row % 4
    g = row * 2 + x_lo
    x_at = x_hi * 2 + x_lo

    def place(x, y, z):
        return (x // 2) * 4 + y, z * 2 + x % 2

    def signal(r, c):
        pl.semaphore_signal(barrier, inc=1, device_id={"row": r, "col": c}, device_id_type=MESH)

    def remote(src, dst, send, recv, r, c):
        return pltpu.make_async_remote_copy(
            src_ref=src, dst_ref=dst, send_sem=send, recv_sem=recv,
            device_id={"row": r, "col": c}, device_id_type=MESH,
        )

    def arrive(ref, sem):
        pltpu.make_async_copy(ref, ref, sem).wait()

    def col_peer(dz, dl):
        return lax.rem(z + dz, ZS) * 2 + lax.rem(x_lo + dl, 2)

    def xy_peer(dx, dy):
        xx, yy = lax.rem(x_at + dx, 4), lax.rem(y + dy, 4)
        r, c = place(xx, yy, z)
        return r * 2 + xx % 2, r, c

    barrier = pltpu.get_barrier_semaphore()
    for dz, dl in COL_STEPS:
        signal(row, col_peer(dz, dl))
    for dx, dy in XY_STEPS:
        if (dx, dy) != (1, 0) and (dx, dy) != (3, 0) and (dx, dy) != (2, 0):
            _, r, c = xy_peer(dx, dy)
            signal(r, c)
    _, r, c = xy_peer(2, 0)
    signal(r, c)
    other = x_at + 1 + 2 * (1 - x_at % 2)
    r, c = place(lax.rem(other, 4), y, z)
    signal(r, c)

    fetched = [
        pltpu.make_async_copy(src, dst, fetch.at[n])
        for n, (src, dst) in enumerate((
            (w_in_hbm, w_in_ref), (w_gate_hbm, w_gate_ref), (w_out1_hbm, w_out1_ref), (w_qkv_hbm, w_qkv_ref),
            (w_gate2_hbm, w_gate2_ref), (w_out2_hbm, w_out2_ref), (perm_hbm, perm_ref), (x_hbm, x_ref),
        ))
    ]
    for copy in fetched:
        copy.start()

    fetched[0].wait()
    w_t = jnp.concatenate([turned(w_in_ref[:, s * C : (s + 1) * C]) for s in range(4)], axis=0)
    ga, va, gb, vb = (w_t[s * C : (s + 1) * C].reshape(GS, 8, C) for s in range(4))
    w_g[...] = jnp.concatenate([ga, gb], axis=1).reshape(2 * C, C).astype(BF16)
    w_v[...] = jnp.concatenate([va, vb], axis=1).reshape(2 * C, C).astype(BF16)
    for slot, ref in enumerate((norm1_ref, norm2_ref, norm3_ref)):
        gains[slot] = jnp.transpose(jnp.broadcast_to(ref[...], (C, C)))

    fetched[7].wait()
    pl.semaphore_wait(barrier, COLS - 1 + 2 * (ROWS - 1))

    def r_copy(i, dz, dl):
        peer = col_peer(dz, dl)
        return remote(x_ref.at[OWN * peer + i], x_rows.at[i, col], r_send, r_recv.at[i], row, peer)

    def r_own(i):
        return pltpu.make_async_copy(x_ref.at[OWN * col + i], x_rows.at[i, col], r_recv.at[i])

    for i in range(OWN):
        for dz, dl in COL_STEPS:
            r_copy(i, dz, dl).start()
        r_own(i).start()

    for copy in fetched[1:6]:
        copy.wait()
    w_gate_t[...] = turned(w_gate_ref[...]).astype(BF16)
    w_o1_t[...] = turned(w_out1_ref[...]).astype(BF16)
    w_o2_t[...] = turned(w_out2_ref[...]).astype(BF16)
    w_gate2_t[...] = turned(w_gate2_ref[...]).astype(BF16)
    w_qv_t[0] = turned(w_qkv_ref[:, :C]).astype(BF16)
    w_qv_t[1] = turned(w_qkv_ref[:, 2 * C :]).astype(BF16)
    w_k_t[...] = turned(w_qkv_ref[:, C : 2 * C]).astype(BF16)
    mask = mask_ref[...].reshape(1, N).astype(F32)
    lane = lax.broadcasted_iota(jnp.int32, (1, N), 1)
    key_mask = jnp.transpose(jnp.broadcast_to(mask, (C, N)))
    for b in range(4):
        line = jnp.zeros((1, N), F32)
        for a in range(4):
            inside = (lane >= 96 * a) & (lane < 96 * (a + 1))
            line = line + jnp.where(inside, pattern_ref[a, b].astype(F32), 0.0)
        part = wide(key_mask[96 * b : 96 * (b + 1)]) * line
        penalty[96 * b : 96 * (b + 1), :] = jnp.where(part > 0.0, 0.0, MASKED)
    fetched[6].wait()

    def l_copy(i, dx, dy):
        peer, r, c = xy_peer(dx, dy)
        return remote(send_l.at[i, peer], recv_l.at[i, g], l_send, l_recv.at[i], r, c)

    def l_own(i):
        return pltpu.make_async_copy(send_l.at[i, g], recv_l.at[i, g], l_recv.at[i])

    for i in range(OWN):
        arrive(x_rows.at[i], r_recv.at[i])
        x_t = jnp.transpose(x_rows[i].astype(F32).reshape(N, C))
        xt[i] = x_t
        normed = norm_columns(x_t, gains[0]).astype(BF16)
        an_t[i] = normed
        own_token = row * 48 + col * OWN + i
        mine = jnp.sum(jnp.where(lane == own_token, mask, 0.0), axis=1, keepdims=True)
        factors = sigmoid(dot(w_g[...], normed)) * dot(w_v[...], normed) * (mask * mine)
        send_l[i] = factors.astype(BF16).reshape(GS, 16, N)
        for dx, dy in XY_STEPS:
            l_copy(i, dx, dy).start()
        l_own(i).start()
    for i in range(OWN):
        gate1[i] = sigmoid(dot(w_gate_t[...], an_t[i]))

    def z_copy(i, src, dst, send, recv, dz):
        peer = lax.rem(z + dz, ZS)
        return remote(src.at[i, peer], dst.at[i, z], send, recv, row, peer * 2 + x_lo)

    def z_own(i, src, dst, recv):
        return pltpu.make_async_copy(src.at[i, z], dst.at[i, z], recv)

    for i in range(OWN):
        arrive(recv_l.at[i], l_recv.at[i])
        arrived = recv_l[i].astype(F32).reshape(GS * 16, N)
        for b in range(3):
            wide_t[b, i * 256 : (i + 1) * 256, :] = arrived[:, b * 128 : (b + 1) * 128]
        for ch in range(16):
            for b in range(3):
                piece = wide_t[b, pl.ds(i * 256 + ch, GS, stride=16), :]
                send_z[i, ch % 8, ch // 8, :, b * 128 : (b + 1) * 128] = piece.astype(BF16)
        for dz in Z_STEPS:
            z_copy(i, send_z, recv_z, z_send, z_recv, dz).start()
        z_own(i, send_z, recv_z, z_recv).start()
    arrive(recv_z, z_recv)

    right = dot(perm_ref[...], recv_z[:, :, 1].reshape(N, N)).astype(BF16)
    for i in range(OWN):
        left = recv_z[i, :, 0].reshape(ZS * GS, N)
        send_p[i] = dot_nt(left, right).astype(BF16).reshape(ZS, GS, N)
        for dz in Z_STEPS:
            z_copy(i, send_p, recv_p, p_send, p_recv.at[i], dz).start()
        z_own(i, send_p, recv_p, p_recv.at[i]).start()

    def x_copy(i, dx, dy):
        peer, r, c = xy_peer(dx, dy)
        return remote(send_x.at[i, peer], recv_x.at[i, g], x_send, x_recv.at[i], r, c)

    def x_own(i):
        return pltpu.make_async_copy(send_x.at[i, g], recv_x.at[i, g], x_recv.at[i])

    for i in range(OWN):
        arrive(recv_p.at[i], p_recv.at[i])
        arrived = recv_p[i].astype(F32).reshape(ZS * GS, N)
        for b in range(3):
            wide_t[b, i * 128 : (i + 1) * 128, :] = arrived[:, b * 128 : (b + 1) * 128]
        for other in range(GS):
            for b in range(3):
                piece = wide_t[b, pl.ds(i * 128 + other, 8, stride=16), :]
                send_x[i, other, :, b * 128 : (b + 1) * 128] = piece.astype(BF16)
        for dx, dy in XY_STEPS:
            x_copy(i, dx, dy).start()
        x_own(i).start()

    def bz_copy(i, dz):
        ref = bias_all.at[i, x_at, y, z]
        return remote(ref, ref, bz_send, bz_recv.at[i], *place(x_at, y, lax.rem(z + dz, ZS)))

    def plane_copy(ref, send, recv, dx, dy):
        return remote(ref, ref, send, recv, *place(lax.rem(x_at + dx, 4), lax.rem(y + dy, 4), z))

    def own_pieces(i):
        ref = bias_all.at[i, x_at, y]
        for d in RING_STEPS:
            plane_copy(ref, ba_send, bx_recv.at[i], d, 0).start()
            plane_copy(ref, ba_send, by_recv.at[i], 0, d).start()

    def passed_pieces(i):
        for e in RING_STEPS:
            from_x = bias_all.at[i, lax.rem(x_at + e, 4), y, :4]
            from_y = bias_all.at[i, x_at, lax.rem(y + e, 4), 4:]
            for d in RING_STEPS:
                plane_copy(from_x, bb_send, bb_recv.at[i], 0, d).start()
                plane_copy(from_y, bb_send, bb_recv.at[i], d, 0).start()

    for i in range(OWN):
        arrive(recv_x.at[i], x_recv.at[i])
        product = recv_x[i].astype(F32).reshape(C, N)
        update = dot(w_o1_t[...], norm_columns(product, gains[1]).astype(BF16))
        middle = (xt[i] + gate1[i] * update).astype(BF16).astype(F32)
        mid[i] = middle
        attend = norm_columns(middle, gains[2]).astype(BF16)
        an_t[i] = attend
        bias_all[i, x_at, y, z] = dot(w_bias_ref[...], attend).astype(BF16)
        for dz in Z_STEPS:
            bz_copy(i, dz).start()

    scale = LOG2E / math.sqrt(WIDTH)
    head_of = lax.broadcasted_iota(jnp.int32, (C, N), 0)

    def project(i):
        attend = an_t[i]
        queries = dot(w_qv_t[0], attend) * scale
        values_ref[i] = dot(w_qv_t[1], attend).astype(BF16)
        keys = jnp.transpose(dot(w_k_t[...], attend)).astype(BF16)
        gate2_ref[i] = sigmoid(dot(w_gate2_t[...], attend))
        for h in range(HEADS):
            inside = (head_of >= WIDTH * h) & (head_of < WIDTH * (h + 1))
            scores_ref[i, h] = dot(keys, jnp.where(inside, queries, 0.0).astype(BF16))

    project(0)
    for i in range(OWN):
        arrive(bias_all.at[i, 0, 0, :7], bz_recv.at[i])
        own_pieces(i)
    project(1)
    for i in range(OWN):
        arrive(bias_all.at[i, 0, :3], bx_recv.at[i])
        arrive(bias_all.at[i, 0, :3], by_recv.at[i])
        passed_pieces(i)
    project(2)
    for i in range(OWN):
        arrive(bias_all.at[i, :3, :3], bb_recv.at[i])
        for r in range(ROWS):
            for c in range(COLS):
                xx, yy = (r // 4) * 2 + c % 2, r % 4
                piece = bias_all[i, xx, yy, c // 2].astype(F32)
                at = ((r * COLS + c) * OWN + i) * HEADS
                for b in range(3):
                    wide_t[b, at : at + HEADS, :] = piece[:, b * 128 : (b + 1) * 128]
    for h in range(HEADS):
        for b in range(3):
            part = wide_t[b, pl.ds(h, N, stride=HEADS), :]
            rows = slice(b * 128, (b + 1) * 128)
            bias_t[h, rows, :] = jnp.transpose(part) * LOG2E + penalty[rows, :]

    def o_copy(i, dz, dl):
        peer = col_peer(dz, dl)
        return remote(send_o.at[i, peer], out_ref.at[OWN * col + i], o_send, o_recv, row, peer)

    def o_own(i):
        return pltpu.make_async_copy(send_o.at[i, col], out_ref.at[OWN * col + i], o_recv)

    for i in range(OWN):
        parts = []
        for h in range(HEADS):
            scores = scores_ref[i, h] + bias_t[h]
            weights = jnp.exp2(scores - jnp.max(scores, axis=0, keepdims=True))
            total = jnp.sum(weights, axis=0, keepdims=True)
            mixed = dot(values_ref[i, WIDTH * h : WIDTH * (h + 1)], weights.astype(BF16))
            parts.append(mixed / total)
        gated = (gate2_ref[i] * jnp.concatenate(parts, axis=0)).astype(BF16)
        result = mid[i] + dot(w_o2_t[...], gated)
        send_o[i] = jnp.transpose(result).reshape(COLS, 24, C).astype(BF16)
        for dz, dl in COL_STEPS:
            o_copy(i, dz, dl).start()
        o_own(i).start()

    arrive(x_rows.at[:, :15], r_send)
    arrive(send_l.at[:, :15], l_send)
    arrive(send_z.at[:, :7], z_send)
    arrive(send_p.at[:, :7], p_send)
    arrive(send_x.at[:, :15], x_send)
    arrive(bias_all.at[:, 0, 0, :7], bz_send)
    arrive(bias_all.at[:, :2, :3], ba_send)
    arrive(bias_all.at[:, :3, :3], bb_send)
    arrive(send_o.at[:, :15], o_send)
    arrive(out_ref, o_recv)


def token_order():
    perm = np.zeros((N, N), np.float32)
    for t in range(N):
        r, c, i = t // 48, (t % 48) // 3, t % 3
        perm[t, i * ZS * GS + (c // 2) * GS + 2 * r + c % 2] = 1.0
    return perm


def shards(
    pair_state, token_mask, block_pattern, triangle_norm, triangle_input, triangle_gate, product_norm,
    triangle_output, attend_norm, attend_inputs, attend_gate, attend_bias, attend_output,
):
    vmem = pl.BlockSpec(memory_space=pltpu.VMEM)
    hbm = pl.BlockSpec(memory_space=pl.ANY)
    smem = pl.BlockSpec(memory_space=pltpu.SMEM)
    dma = pltpu.SemaphoreType.DMA
    V = pltpu.VMEM
    return pl.pallas_call(
        kernel,
        out_shape=jax.ShapeDtypeStruct(pair_state.shape, BF16),
        in_specs=[hbm, vmem, smem, hbm, vmem, hbm, hbm, vmem, hbm, vmem, hbm, hbm, vmem, hbm],
        out_specs=hbm,
        scratch_shapes=[
            V((OWN, COLS, 24, C), BF16),
            V((OWN, GS, 16, N), BF16), V((OWN, GS, 16, N), BF16),
            V((OWN, ZS, 2, GS, N), BF16), V((OWN, ZS, 2, GS, N), BF16),
            V((OWN, ZS, GS, N), BF16), V((OWN, ZS, GS, N), BF16),
            V((OWN, GS, 8, N), BF16), V((OWN, GS, 8, N), BF16),
            V((OWN, 4, 4, ZS, HEADS, N), BF16),
            V((OWN, COLS, 24, C), BF16),
            V((OWN, C, N), F32), V((OWN, C, N), F32), V((OWN, C, N), F32), V((OWN, C, N), BF16),
            V((3, HEADS * N, 128), F32), V((HEADS, N, N), F32), V((N, N), F32),
            V((OWN, HEADS, N, N), F32), V((OWN, C, N), BF16), V((OWN, C, N), F32),
            V((48, 24, C), BF16), V((N, N), BF16), V((C, 4 * C), BF16), V((C, C), BF16), V((C, C), BF16),
            V((C, 3 * C), BF16), V((C, C), BF16), V((C, C), BF16),
            V((2 * C, C), BF16), V((2 * C, C), BF16), V((C, C), BF16), V((C, C), BF16),
            V((2, C, C), BF16), V((C, C), BF16), V((C, C), BF16), V((C, C), BF16), V((3, C, C), F32),
            dma, dma((OWN,)), dma, dma((OWN,)), dma, dma, dma, dma((OWN,)), dma, dma((OWN,)),
            dma, dma((OWN,)), dma, dma((OWN,)), dma((OWN,)), dma, dma((OWN,)), dma, dma, dma((8,)),
        ],
        compiler_params=pltpu.CompilerParams(
            collective_id=0, has_side_effects=True, vmem_limit_bytes=63 * 1024 * 1024
        ),
        name="pairformer",
    )(
        pair_state, token_mask, block_pattern, jnp.asarray(token_order(), BF16),
        triangle_norm.reshape(1, C), triangle_input, triangle_gate, product_norm.reshape(1, C), triangle_output,
        attend_norm.reshape(1, C), attend_inputs, attend_gate, attend_bias.T, attend_output,
    )


def solution(mesh):
    tile = P(("crop", "row"), "col", None)
    return jax.shard_map(
        shards,
        mesh=mesh,
        in_specs=(tile, P("crop"), P("crop", None)) + (P(),) * 10,
        out_specs=tile,
        check_vma=False,
    )
```

```python
import functools
import math

import jax
import jax.numpy as jnp
import numpy as np
from jax import lax
from jax.experimental import pallas as pl
from jax.experimental.pallas import tpu as pltpu
from jax.sharding import PartitionSpec as P

MESH = pl.DeviceIdType.MESH
F32 = jnp.float32
BF16 = jnp.bfloat16
EPS = 1e-05
ROWS, COLS, C, N = 8, 16, 128, 384
HEADS, WIDTH = 4, 32
ZS, GS, OWN = 8, 16, 3
LOG2E = 1.4426950408889634
MASKED = -1e30


def dot(a, b):
    return jnp.dot(a, b, preferred_element_type=F32)


def dot_nt(a, b):
    return lax.dot_general(a, b, (((1,), (1,)), ((), ())), preferred_element_type=F32)


def dot_tn(a, b):
    return lax.dot_general(a, b, (((0,), (0,)), ((), ())), preferred_element_type=F32)


def wide(gain):
    return jnp.concatenate([gain] * (N // 128), axis=1)


def norm_columns(v, gain):
    centered = v - jnp.mean(v, axis=0, keepdims=True)
    variance = jnp.mean(centered * centered, axis=0, keepdims=True)
    return centered * lax.rsqrt(variance + EPS) * wide(gain)


def sigmoid(v):
    return 1.0 / (1.0 + jnp.exp(-v))


def turned(w):
    return jnp.transpose(w.astype(F32))


RING_STEPS = (2, 1, 3)
Z_STEPS = (4, 3, 5, 2, 6, 1, 7)
COL_STEPS = tuple((dz, dl) for dz in Z_STEPS for dl in (1, 0)) + ((0, 1),)
XY_STEPS = tuple(sorted(
    ((dx, dy) for dx in range(4) for dy in range(4) if dx or dy),
    key=lambda s: -(min(s[0], 4 - s[0]) + min(s[1], 4 - s[1])),
))


def kernel(
    x_hbm, mask_ref, pattern_ref, perm_hbm,
    norm1_ref, w_in_hbm, w_gate_hbm, norm2_ref, w_out1_hbm,
    norm3_ref, w_qkv_hbm, w_gate2_hbm, w_bias_ref, w_out2_hbm,
    out_ref,
    x_rows, send_lz, recv_lz, send_rx, recv_rx, send_rz, recv_rz, send_lx, recv_lx, send_p, recv_p, send_x, recv_x,
    bias_all, send_o, xt, gate1, mid, an_t, wide_t, bias_t, penalty, scores_ref, values_ref, gate2_ref,
    x_ref, perm_ref, w_in_ref, w_gate_ref, w_out1_ref, w_qkv_ref, w_gate2_ref, w_out2_ref,
    w_g, w_v, w_gate_t, w_o1_t, w_qv_t, w_k_t, w_gate2_t, w_o2_t, gains, z_order,
    r_send, r_recv, lz_send, lz_recv, rx_send, rx_recv, rz_send, rz_recv, lx_send, lx_recv, p_send, p_recv, x_send, x_recv,
    bz_send, bz_recv, ba_send, bx_recv, by_recv, bb_send, bb_recv, o_send, o_recv, fetch,
):
    row, col = lax.axis_index("row"), lax.axis_index("col")
    z, x_lo = col // 2, col % 2
    x_hi, y = row // 4, row % 4
    g = row * 2 + x_lo
    x_at = x_hi * 2 + x_lo

    def place(x, y, z):
        return (x // 2) * 4 + y, z * 2 + x % 2

    def signal(r, c):
        pl.semaphore_signal(barrier, inc=1, device_id={"row": r, "col": c}, device_id_type=MESH)

    def remote(src, dst, send, recv, r, c):
        return pltpu.make_async_remote_copy(
            src_ref=src, dst_ref=dst, send_sem=send, recv_sem=recv,
            device_id={"row": r, "col": c}, device_id_type=MESH,
        )

    def arrive(ref, sem):
        pltpu.make_async_copy(ref, ref, sem).wait()

    def col_peer(dz, dl):
        return lax.rem(z + dz, ZS) * 2 + lax.rem(x_lo + dl, 2)

    def xy_peer(dx, dy):
        xx, yy = lax.rem(x_at + dx, 4), lax.rem(y + dy, 4)
        r, c = place(xx, yy, z)
        return r * 2 + xx % 2, r, c

    barrier = pltpu.get_barrier_semaphore()
    for dz, dl in COL_STEPS:
        signal(row, col_peer(dz, dl))
    for dx, dy in XY_STEPS:
        if (dx, dy) != (1, 0) and (dx, dy) != (3, 0) and (dx, dy) != (2, 0):
            _, r, c = xy_peer(dx, dy)
            signal(r, c)
    _, r, c = xy_peer(2, 0)
    signal(r, c)
    other = x_at + 1 + 2 * (1 - x_at % 2)
    r, c = place(lax.rem(other, 4), y, z)
    signal(r, c)

    fetched = [
        pltpu.make_async_copy(src, dst, fetch.at[n])
        for n, (src, dst) in enumerate((
            (w_in_hbm, w_in_ref), (w_gate_hbm, w_gate_ref), (w_out1_hbm, w_out1_ref), (w_qkv_hbm, w_qkv_ref),
            (w_gate2_hbm, w_gate2_ref), (w_out2_hbm, w_out2_ref), (perm_hbm, perm_ref), (x_hbm, x_ref),
        ))
    ]
    for copy in fetched:
        copy.start()

    fetched[0].wait()
    w_t = jnp.concatenate([turned(w_in_ref[:, s * C : (s + 1) * C]) for s in range(4)], axis=0)
    ga, va, gb, vb = (w_t[s * C : (s + 1) * C].astype(BF16) for s in range(4))
    line, at = (lax.broadcasted_iota(jnp.int32, (C, C), d) for d in range(2))
    z_first = jnp.where((line & 15) * ZS + (line >> 4) == at, 1.0, 0.0).astype(BF16)
    z_order[...] = z_first
    w_g[:C], w_g[C:] = dot(z_first, ga).astype(BF16), gb
    w_v[:C], w_v[C:] = dot(z_first, va).astype(BF16), vb
    for slot, ref in enumerate((norm1_ref, norm2_ref, norm3_ref)):
        gains[slot] = jnp.transpose(jnp.broadcast_to(ref[...], (C, C)))

    fetched[7].wait()
    pl.semaphore_wait(barrier, COLS - 1 + 2 * (ROWS - 1))

    def r_copy(i, dz, dl):
        peer = col_peer(dz, dl)
        return remote(x_ref.at[OWN * peer + i], x_rows.at[i, col], r_send, r_recv.at[i], row, peer)

    def r_own(i):
        return pltpu.make_async_copy(x_ref.at[OWN * col + i], x_rows.at[i, col], r_recv.at[i])

    for i in range(OWN):
        for dz, dl in COL_STEPS:
            r_copy(i, dz, dl).start()
        r_own(i).start()

    for copy in fetched[1:6]:
        copy.wait()
    w_gate_t[...] = turned(w_gate_ref[...]).astype(BF16)
    w_o1_t[...] = turned(w_out1_ref[...]).astype(BF16)
    w_o2_t[...] = turned(w_out2_ref[...]).astype(BF16)
    w_gate2_t[...] = turned(w_gate2_ref[...]).astype(BF16)
    w_qv_t[0] = turned(w_qkv_ref[:, :C]).astype(BF16)
    w_qv_t[1] = turned(w_qkv_ref[:, 2 * C :]).astype(BF16)
    w_k_t[...] = turned(w_qkv_ref[:, C : 2 * C]).astype(BF16)
    mask = mask_ref[...].reshape(1, N).astype(F32)
    lane = lax.broadcasted_iota(jnp.int32, (1, N), 1)
    key_mask = jnp.transpose(jnp.broadcast_to(mask, (C, N)))
    for b in range(4):
        line = jnp.zeros((1, N), F32)
        for a in range(4):
            inside = (lane >= 96 * a) & (lane < 96 * (a + 1))
            line = line + jnp.where(inside, pattern_ref[a, b].astype(F32), 0.0)
        part = wide(key_mask[96 * b : 96 * (b + 1)]) * line
        penalty[96 * b : 96 * (b + 1), :] = jnp.where(part > 0.0, 0.0, MASKED)
    fetched[6].wait()

    def z_copy(i, src, dst, send, recv, dz):
        peer = lax.rem(z + dz, ZS)
        return remote(src.at[i, peer], dst.at[i, z], send, recv, row, peer * 2 + x_lo)

    def z_exchange(i, src, dst, send, recv):
        for dz in Z_STEPS:
            z_copy(i, src, dst, send, recv, dz).start()
        pltpu.make_async_copy(src.at[i, z], dst.at[i, z], recv).start()

    def xy_exchange(i, src, dst, send, recv):
        for dx, dy in XY_STEPS:
            peer, r, c = xy_peer(dx, dy)
            remote(src.at[i, peer], dst.at[i, g], send, recv, r, c).start()
        pltpu.make_async_copy(src.at[i, g], dst.at[i, g], recv).start()

    for i in range(OWN):
        arrive(x_rows.at[i], r_recv.at[i])
        x_t = jnp.transpose(x_rows[i].astype(F32).reshape(N, C))
        xt[i] = x_t
        normed = norm_columns(x_t, gains[0]).astype(BF16)
        an_t[i] = normed
        own_token = row * 48 + col * OWN + i
        mine = jnp.sum(jnp.where(lane == own_token, mask, 0.0), axis=1, keepdims=True)
        factors = sigmoid(dot(w_g[...], normed)) * dot(w_v[...], normed) * (mask * mine)
        send_lz[i] = factors[:C].astype(BF16).reshape(ZS, GS, N)
        send_rx[i] = factors[C:].reshape(GS, ZS, N).astype(BF16)
        z_exchange(i, send_lz, recv_lz, lz_send, lz_recv.at[i])
        xy_exchange(i, send_rx, recv_rx, rx_send, rx_recv.at[i])
    for i in range(OWN):
        gate1[i] = sigmoid(dot(w_gate_t[...], an_t[i]))

    def spread(i, half, arrived):
        base = (2 * i + half) * C
        for b in range(3):
            wide_t[b, base : base + C, :] = arrived[:, b * 128 : (b + 1) * 128]
        return base

    def right_on(i):
        arrive(recv_rx.at[i], rx_recv.at[i])
        base = spread(i, 0, recv_rx[i].astype(F32).reshape(C, N))
        for to in range(ZS):
            for b in range(3):
                piece = wide_t[b, pl.ds(base + to, GS, stride=ZS), :]
                send_rz[i, to, :, b * 128 : (b + 1) * 128] = piece.astype(BF16)
        z_exchange(i, send_rz, recv_rz, rz_send, rz_recv)

    def left_on(i):
        arrive(recv_lz.at[i], lz_recv.at[i])
        base = spread(i, 1, recv_lz[i].astype(F32).reshape(C, N))
        for to in range(GS):
            for b in range(3):
                piece = wide_t[b, pl.ds(base + to, ZS, stride=GS), :]
                send_lx[i, to, :, b * 128 : (b + 1) * 128] = piece.astype(BF16)
        xy_exchange(i, send_lx, recv_lx, lx_send, lx_recv.at[i])

    right_on(0)
    right_on(1)
    left_on(0)
    right_on(2)
    left_on(1)
    left_on(2)
    arrive(recv_rz, rz_recv)
    right = dot(perm_ref[...], recv_rz[...].reshape(N, N)).astype(BF16)
    for i in range(OWN):
        arrive(recv_lx.at[i], lx_recv.at[i])
        left = dot(z_order[...], recv_lx[i].astype(F32).reshape(C, N).astype(BF16)).astype(BF16)
        send_p[i] = dot_nt(left, right).astype(BF16).reshape(ZS, GS, N)
        z_exchange(i, send_p, recv_p, p_send, p_recv.at[i])

    for i in range(OWN):
        arrive(recv_p.at[i], p_recv.at[i])
        base = spread(i, 0, recv_p[i].astype(F32).reshape(C, N))
        for to in range(GS):
            for b in range(3):
                piece = wide_t[b, pl.ds(base + to, ZS, stride=GS), :]
                send_x[i, to, :, b * 128 : (b + 1) * 128] = piece.astype(BF16)
        xy_exchange(i, send_x, recv_x, x_send, x_recv.at[i])

    def bz_copy(i, dz):
        ref = bias_all.at[i, x_at, y, z]
        return remote(ref, ref, bz_send, bz_recv.at[i], *place(x_at, y, lax.rem(z + dz, ZS)))

    def plane_copy(ref, send, recv, dx, dy):
        return remote(ref, ref, send, recv, *place(lax.rem(x_at + dx, 4), lax.rem(y + dy, 4), z))

    def own_pieces(i):
        ref = bias_all.at[i, x_at, y]
        for d in RING_STEPS:
            plane_copy(ref, ba_send, bx_recv.at[i], d, 0).start()
            plane_copy(ref, ba_send, by_recv.at[i], 0, d).start()

    def passed_pieces(i):
        for e in RING_STEPS:
            from_x = bias_all.at[i, lax.rem(x_at + e, 4), y, :4]
            from_y = bias_all.at[i, x_at, lax.rem(y + e, 4), 4:]
            for d in RING_STEPS:
                plane_copy(from_x, bb_send, bb_recv.at[i], 0, d).start()
                plane_copy(from_y, bb_send, bb_recv.at[i], d, 0).start()

    for i in range(OWN):
        arrive(recv_x.at[i], x_recv.at[i])
        product = recv_x[i].astype(F32).reshape(C, N)
        update = dot(w_o1_t[...], norm_columns(product, gains[1]).astype(BF16))
        middle = (xt[i] + gate1[i] * update).astype(BF16).astype(F32)
        mid[i] = middle
        attend = norm_columns(middle, gains[2]).astype(BF16)
        an_t[i] = attend
        bias_all[i, x_at, y, z] = dot(w_bias_ref[...], attend).astype(BF16)
        for dz in Z_STEPS:
            bz_copy(i, dz).start()

    scale = LOG2E / math.sqrt(WIDTH)
    head_of = lax.broadcasted_iota(jnp.int32, (C, N), 0)

    def project(i):
        attend = an_t[i]
        queries = dot(w_qv_t[0], attend) * scale
        values_ref[i] = dot(w_qv_t[1], attend).astype(BF16)
        keys = jnp.transpose(dot(w_k_t[...], attend)).astype(BF16)
        gate2_ref[i] = sigmoid(dot(w_gate2_t[...], attend))
        for h in range(HEADS):
            inside = (head_of >= WIDTH * h) & (head_of < WIDTH * (h + 1))
            scores_ref[i, h] = dot(keys, jnp.where(inside, queries, 0.0).astype(BF16))

    project(0)
    for i in range(OWN):
        arrive(bias_all.at[i, 0, 0, :7], bz_recv.at[i])
        own_pieces(i)
    project(1)
    for i in range(OWN):
        arrive(bias_all.at[i, 0, :3], bx_recv.at[i])
        arrive(bias_all.at[i, 0, :3], by_recv.at[i])
        passed_pieces(i)
    project(2)
    for i in range(OWN):
        arrive(bias_all.at[i, :3, :3], bb_recv.at[i])
        for r in range(ROWS):
            for c in range(COLS):
                xx, yy = (r // 4) * 2 + c % 2, r % 4
                piece = bias_all[i, xx, yy, c // 2].astype(F32)
                at = ((r * COLS + c) * OWN + i) * HEADS
                for b in range(3):
                    wide_t[b, at : at + HEADS, :] = piece[:, b * 128 : (b + 1) * 128]
    for h in range(HEADS):
        for b in range(3):
            part = wide_t[b, pl.ds(h, N, stride=HEADS), :]
            rows = slice(b * 128, (b + 1) * 128)
            bias_t[h, rows, :] = jnp.transpose(part) * LOG2E + penalty[rows, :]

    def o_copy(i, dz, dl):
        peer = col_peer(dz, dl)
        return remote(send_o.at[i, peer], out_ref.at[OWN * col + i], o_send, o_recv, row, peer)

    def o_own(i):
        return pltpu.make_async_copy(send_o.at[i, col], out_ref.at[OWN * col + i], o_recv)

    for i in range(OWN):
        parts = []
        for h in range(HEADS):
            scores = scores_ref[i, h] + bias_t[h]
            weights = jnp.exp2(scores - jnp.max(scores, axis=0, keepdims=True))
            total = jnp.sum(weights, axis=0, keepdims=True)
            mixed = dot(values_ref[i, WIDTH * h : WIDTH * (h + 1)], weights.astype(BF16))
            parts.append(mixed / total)
        gated = (gate2_ref[i] * jnp.concatenate(parts, axis=0)).astype(BF16)
        result = mid[i] + dot(w_o2_t[...], gated)
        send_o[i] = jnp.transpose(result).reshape(COLS, 24, C).astype(BF16)
        for dz, dl in COL_STEPS:
            o_copy(i, dz, dl).start()
        o_own(i).start()

    arrive(x_rows.at[:, :15], r_send)
    arrive(send_lz.at[:, :7], lz_send)
    arrive(send_rx.at[:, :15], rx_send)
    arrive(send_rz.at[:, :7], rz_send)
    arrive(send_lx.at[:, :15], lx_send)
    arrive(send_p.at[:, :7], p_send)
    arrive(send_x.at[:, :15], x_send)
    arrive(bias_all.at[:, 0, 0, :7], bz_send)
    arrive(bias_all.at[:, :2, :3], ba_send)
    arrive(bias_all.at[:, :3, :3], bb_send)
    arrive(send_o.at[:, :15], o_send)
    arrive(out_ref, o_recv)


def token_order():
    perm = np.zeros((N, N), np.float32)
    for t in range(N):
        r, c, i = t // 48, (t % 48) // 3, t % 3
        perm[t, i * ZS * GS + (c // 2) * GS + 2 * r + c % 2] = 1.0
    return perm


def shards(
    pair_state, token_mask, block_pattern, triangle_norm, triangle_input, triangle_gate, product_norm,
    triangle_output, attend_norm, attend_inputs, attend_gate, attend_bias, attend_output,
):
    vmem = pl.BlockSpec(memory_space=pltpu.VMEM)
    hbm = pl.BlockSpec(memory_space=pl.ANY)
    smem = pl.BlockSpec(memory_space=pltpu.SMEM)
    dma = pltpu.SemaphoreType.DMA
    V = pltpu.VMEM
    return pl.pallas_call(
        kernel,
        out_shape=jax.ShapeDtypeStruct(pair_state.shape, BF16),
        in_specs=[hbm, vmem, smem, hbm, vmem, hbm, hbm, vmem, hbm, vmem, hbm, hbm, vmem, hbm],
        out_specs=hbm,
        scratch_shapes=[
            V((OWN, COLS, 24, C), BF16),
            V((OWN, ZS, GS, N), BF16), V((OWN, ZS, GS, N), BF16), V((OWN, GS, ZS, N), BF16), V((OWN, GS, ZS, N), BF16),
            V((OWN, ZS, GS, N), BF16), V((OWN, ZS, GS, N), BF16), V((OWN, GS, ZS, N), BF16), V((OWN, GS, ZS, N), BF16),
            V((OWN, ZS, GS, N), BF16), V((OWN, ZS, GS, N), BF16),
            V((OWN, GS, 8, N), BF16), V((OWN, GS, 8, N), BF16),
            V((OWN, 4, 4, ZS, HEADS, N), BF16),
            V((OWN, COLS, 24, C), BF16),
            V((OWN, C, N), F32), V((OWN, C, N), F32), V((OWN, C, N), F32), V((OWN, C, N), BF16),
            V((3, HEADS * N, 128), F32), V((HEADS, N, N), F32), V((N, N), F32),
            V((OWN, HEADS, N, N), F32), V((OWN, C, N), BF16), V((OWN, C, N), F32),
            V((48, 24, C), BF16), V((N, N), BF16), V((C, 4 * C), BF16), V((C, C), BF16), V((C, C), BF16),
            V((C, 3 * C), BF16), V((C, C), BF16), V((C, C), BF16),
            V((2 * C, C), BF16), V((2 * C, C), BF16), V((C, C), BF16), V((C, C), BF16),
            V((2, C, C), BF16), V((C, C), BF16), V((C, C), BF16), V((C, C), BF16), V((3, C, C), F32), V((C, C), BF16),
            dma, dma((OWN,)), dma, dma((OWN,)), dma, dma((OWN,)), dma, dma, dma, dma((OWN,)),
            dma, dma((OWN,)), dma, dma((OWN,)),
            dma, dma((OWN,)), dma, dma((OWN,)), dma((OWN,)), dma, dma((OWN,)), dma, dma, dma((8,)),
        ],
        compiler_params=pltpu.CompilerParams(
            collective_id=0, has_side_effects=True, vmem_limit_bytes=63 * 1024 * 1024
        ),
        name="pairformer",
    )(
        pair_state, token_mask, block_pattern, jnp.asarray(token_order(), BF16),
        triangle_norm.reshape(1, C), triangle_input, triangle_gate, product_norm.reshape(1, C), triangle_output,
        attend_norm.reshape(1, C), attend_inputs, attend_gate, attend_bias.T, attend_output,
    )


def solution(mesh):
    tile = P(("crop", "row"), "col", None)
    return jax.shard_map(
        shards,
        mesh=mesh,
        in_specs=(tile, P("crop"), P("crop", None)) + (P(),) * 10,
        out_specs=tile,
        check_vma=False,
    )
```

```python
import functools
import math

import jax
import jax.numpy as jnp
import numpy as np
from jax import lax
from jax.experimental import pallas as pl
from jax.experimental.pallas import tpu as pltpu
from jax.sharding import PartitionSpec as P

MESH = pl.DeviceIdType.MESH
F32 = jnp.float32
BF16 = jnp.bfloat16
EPS = 1e-05
ROWS, COLS, C, N = 8, 16, 128, 384
HEADS, WIDTH = 4, 32
ZS, GS, OWN = 8, 16, 3
LOG2E = 1.4426950408889634
MASKED = -1e30


def dot(a, b):
    return jnp.dot(a, b, preferred_element_type=F32)


def dot_nt(a, b):
    return lax.dot_general(a, b, (((1,), (1,)), ((), ())), preferred_element_type=F32)


def dot_tn(a, b):
    return lax.dot_general(a, b, (((0,), (0,)), ((), ())), preferred_element_type=F32)


def wide(gain):
    return jnp.concatenate([gain] * (N // 128), axis=1)


def norm_columns(v, gain):
    centered = v - jnp.mean(v, axis=0, keepdims=True)
    variance = jnp.mean(centered * centered, axis=0, keepdims=True)
    return centered * lax.rsqrt(variance + EPS) * wide(gain)


def sigmoid(v):
    return 1.0 / (1.0 + jnp.exp(-v))


def turned(w):
    return jnp.transpose(w.astype(F32))


RING_STEPS = (2, 1, 3)
Z_STEPS = (4, 3, 5, 2, 6, 1, 7)
COL_STEPS = tuple((dz, dl) for dz in Z_STEPS for dl in (1, 0)) + ((0, 1),)
XY_STEPS = tuple(sorted(
    ((dx, dy) for dx in range(4) for dy in range(4) if dx or dy),
    key=lambda s: -(min(s[0], 4 - s[0]) + min(s[1], 4 - s[1])),
))


def kernel(
    x_hbm, mask_ref, pattern_ref, perm_hbm,
    norm1_ref, w_in_hbm, w_gate_hbm, norm2_ref, w_out1_hbm,
    norm3_ref, w_qkv_hbm, w_gate2_hbm, w_bias_ref, w_out2_hbm,
    out_ref,
    x_rows, send_lz, recv_lz, send_rx, recv_rx, send_rz, recv_rz, send_lx, recv_lx, send_p, recv_p, send_x, recv_x,
    bias_all, send_o, xt, gate1, mid, an_t, wide_t, bias_t, penalty, scores_ref, values_ref, gate2_ref,
    x_ref, perm_ref, w_in_ref, w_gate_ref, w_out1_ref, w_qkv_ref, w_gate2_ref, w_out2_ref,
    w_g, w_v, w_gate_t, w_o1_t, w_qv_t, w_k_t, w_gate2_t, w_o2_t, gains, z_order,
    r_send, r_recv, lz_send, lz_recv, rx_send, rx_recv, rz_send, rz_recv, lx_send, lx_recv, p_send, p_recv, x_send, x_recv,
    bz_send, bz_recv, ba_send, bx_recv, by_recv, bb_send, bb_recv, o_send, o_recv, fetch,
):
    row, col = lax.axis_index("row"), lax.axis_index("col")
    z, x_lo = col // 2, col % 2
    x_hi, y = row // 4, row % 4
    g = row * 2 + x_lo
    x_at = x_hi * 2 + x_lo

    def place(x, y, z):
        return (x // 2) * 4 + y, z * 2 + x % 2

    def signal(r, c):
        pl.semaphore_signal(barrier, inc=1, device_id={"row": r, "col": c}, device_id_type=MESH)

    def remote(src, dst, send, recv, r, c):
        return pltpu.make_async_remote_copy(
            src_ref=src, dst_ref=dst, send_sem=send, recv_sem=recv,
            device_id={"row": r, "col": c}, device_id_type=MESH,
        )

    def arrive(ref, sem):
        pltpu.make_async_copy(ref, ref, sem).wait()

    def col_peer(dz, dl):
        return lax.rem(z + dz, ZS) * 2 + lax.rem(x_lo + dl, 2)

    def xy_peer(dx, dy):
        xx, yy = lax.rem(x_at + dx, 4), lax.rem(y + dy, 4)
        r, c = place(xx, yy, z)
        return r * 2 + xx % 2, r, c

    barrier = pltpu.get_barrier_semaphore()
    for dz, dl in COL_STEPS:
        signal(row, col_peer(dz, dl))
    for dx, dy in XY_STEPS:
        if (dx, dy) != (1, 0) and (dx, dy) != (3, 0) and (dx, dy) != (2, 0):
            _, r, c = xy_peer(dx, dy)
            signal(r, c)
    _, r, c = xy_peer(2, 0)
    signal(r, c)
    other = x_at + 1 + 2 * (1 - x_at % 2)
    r, c = place(lax.rem(other, 4), y, z)
    signal(r, c)

    fetched = [
        pltpu.make_async_copy(src, dst, fetch.at[n])
        for n, (src, dst) in enumerate((
            (w_in_hbm, w_in_ref), (w_gate_hbm, w_gate_ref), (w_out1_hbm, w_out1_ref), (w_qkv_hbm, w_qkv_ref),
            (w_gate2_hbm, w_gate2_ref), (w_out2_hbm, w_out2_ref), (perm_hbm, perm_ref), (x_hbm, x_ref),
        ))
    ]
    for copy in fetched:
        copy.start()

    fetched[0].wait()
    w_t = jnp.concatenate([turned(w_in_ref[:, s * C : (s + 1) * C]) for s in range(4)], axis=0)
    ga, va, gb, vb = (w_t[s * C : (s + 1) * C].astype(BF16) for s in range(4))
    line, at = (lax.broadcasted_iota(jnp.int32, (C, C), d) for d in range(2))
    z_first = jnp.where((line & 15) * ZS + (line >> 4) == at, 1.0, 0.0).astype(BF16)
    z_order[...] = z_first
    w_g[:C], w_g[C:] = dot(z_first, ga).astype(BF16), gb
    w_v[:C], w_v[C:] = dot(z_first, va).astype(BF16), vb
    for slot, ref in enumerate((norm1_ref, norm2_ref, norm3_ref)):
        gains[slot] = jnp.transpose(jnp.broadcast_to(ref[...], (C, C)))

    fetched[7].wait()
    pl.semaphore_wait(barrier, COLS - 1 + 2 * (ROWS - 1))

    def r_copy(i, dz, dl):
        peer = col_peer(dz, dl)
        return remote(x_ref.at[OWN * peer + i], x_rows.at[i, col], r_send, r_recv.at[i], row, peer)

    def r_own(i):
        return pltpu.make_async_copy(x_ref.at[OWN * col + i], x_rows.at[i, col], r_recv.at[i])

    for i in range(OWN):
        for dz, dl in COL_STEPS:
            r_copy(i, dz, dl).start()
        r_own(i).start()

    for copy in fetched[1:6]:
        copy.wait()
    w_gate_t[...] = turned(w_gate_ref[...]).astype(BF16)
    w_o1_t[...] = turned(w_out1_ref[...]).astype(BF16)
    w_o2_t[...] = turned(w_out2_ref[...]).astype(BF16)
    w_gate2_t[...] = turned(w_gate2_ref[...]).astype(BF16)
    w_qv_t[0] = turned(w_qkv_ref[:, :C]).astype(BF16)
    w_qv_t[1] = turned(w_qkv_ref[:, 2 * C :]).astype(BF16)
    w_k_t[...] = turned(w_qkv_ref[:, C : 2 * C]).astype(BF16)
    length = jnp.sum(mask_ref[...].reshape(1, N).astype(F32), axis=1, keepdims=True)
    lane = lax.broadcasted_iota(jnp.int32, (1, N), 1)
    mask = jnp.where((OWN * (lane & 127) + (lane >> 7)).astype(F32) < length, 1.0, 0.0)
    key_mask = jnp.transpose(jnp.broadcast_to(mask, (C, N)))
    for b in range(4):
        line = jnp.zeros((1, N), F32)
        for a in range(4):
            line = line + jnp.where(((lane & 127) >> 5) == a, pattern_ref[a, b].astype(F32), 0.0)
        for i in range(OWN):
            rows = slice(i * 128 + 32 * b, i * 128 + 32 * (b + 1))
            penalty[rows, :] = jnp.where(wide(key_mask[rows]) * line > 0.0, 0.0, MASKED)
    fetched[6].wait()

    def z_copy(i, src, dst, send, recv, dz):
        peer = lax.rem(z + dz, ZS)
        return remote(src.at[i, peer], dst.at[i, z], send, recv, row, peer * 2 + x_lo)

    def z_exchange(i, src, dst, send, recv):
        for dz in Z_STEPS:
            z_copy(i, src, dst, send, recv, dz).start()
        pltpu.make_async_copy(src.at[i, z], dst.at[i, z], recv).start()

    def xy_exchange(i, src, dst, send, recv):
        for dx, dy in XY_STEPS:
            peer, r, c = xy_peer(dx, dy)
            remote(src.at[i, peer], dst.at[i, g], send, recv, r, c).start()
        pltpu.make_async_copy(src.at[i, g], dst.at[i, g], recv).start()

    for i in range(OWN):
        arrive(x_rows.at[i], r_recv.at[i])
        wide_t[0, i * N : (i + 1) * N, :] = x_rows[i].astype(F32).reshape(N, C)
        x_t = jnp.concatenate(
            [jnp.transpose(wide_t[0, pl.ds(i * N + b, 128, stride=OWN), :]) for b in range(OWN)], axis=1
        )
        xt[i] = x_t
        normed = norm_columns(x_t, gains[0]).astype(BF16)
        an_t[i] = normed
        own_token = row * 48 + col * OWN + i
        mine = jnp.where(own_token.astype(F32) < length, 1.0, 0.0)
        factors = sigmoid(dot(w_g[...], normed)) * dot(w_v[...], normed) * (mask * mine)
        send_lz[i] = factors[:C].astype(BF16).reshape(ZS, GS, N)
        send_rx[i] = factors[C:].reshape(GS, ZS, N).astype(BF16)
        z_exchange(i, send_lz, recv_lz, lz_send, lz_recv.at[i])
        xy_exchange(i, send_rx, recv_rx, rx_send, rx_recv.at[i])
    for i in range(OWN):
        gate1[i] = sigmoid(dot(w_gate_t[...], an_t[i]))

    def spread(i, half, arrived):
        base = (2 * i + half) * C
        for b in range(3):
            wide_t[b, base : base + C, :] = arrived[:, b * 128 : (b + 1) * 128]
        return base

    def right_on(i):
        arrive(recv_rx.at[i], rx_recv.at[i])
        base = spread(i, 0, recv_rx[i].astype(F32).reshape(C, N))
        for to in range(ZS):
            for b in range(3):
                piece = wide_t[b, pl.ds(base + to, GS, stride=ZS), :]
                send_rz[i, to, :, b * 128 : (b + 1) * 128] = piece.astype(BF16)
        z_exchange(i, send_rz, recv_rz, rz_send, rz_recv)

    def left_on(i):
        arrive(recv_lz.at[i], lz_recv.at[i])
        base = spread(i, 1, recv_lz[i].astype(F32).reshape(C, N))
        for to in range(GS):
            for b in range(3):
                piece = wide_t[b, pl.ds(base + to, ZS, stride=GS), :]
                send_lx[i, to, :, b * 128 : (b + 1) * 128] = piece.astype(BF16)
        xy_exchange(i, send_lx, recv_lx, lx_send, lx_recv.at[i])

    right_on(0)
    right_on(1)
    left_on(0)
    right_on(2)
    left_on(1)
    left_on(2)
    arrive(recv_rz, rz_recv)
    right = jnp.concatenate(
        [dot(perm_ref[...], recv_rz[i].reshape(C, N)).astype(BF16) for i in range(OWN)], axis=0
    )
    for i in range(OWN):
        arrive(recv_lx.at[i], lx_recv.at[i])
        left = dot(z_order[...], recv_lx[i].astype(F32).reshape(C, N).astype(BF16)).astype(BF16)
        send_p[i] = dot_nt(left, right).astype(BF16).reshape(ZS, GS, N)
        z_exchange(i, send_p, recv_p, p_send, p_recv.at[i])

    for i in range(OWN):
        arrive(recv_p.at[i], p_recv.at[i])
        base = spread(i, 0, recv_p[i].astype(F32).reshape(C, N))
        for to in range(GS):
            for b in range(3):
                piece = wide_t[b, pl.ds(base + to, ZS, stride=GS), :]
                send_x[i, to, :, b * 128 : (b + 1) * 128] = piece.astype(BF16)
        xy_exchange(i, send_x, recv_x, x_send, x_recv.at[i])

    def bz_copy(i, dz):
        ref = bias_all.at[i, x_at, y, z]
        return remote(ref, ref, bz_send, bz_recv.at[i], *place(x_at, y, lax.rem(z + dz, ZS)))

    def plane_copy(ref, send, recv, dx, dy):
        return remote(ref, ref, send, recv, *place(lax.rem(x_at + dx, 4), lax.rem(y + dy, 4), z))

    def own_pieces(i):
        ref = bias_all.at[i, x_at, y]
        for d in RING_STEPS:
            plane_copy(ref, ba_send, bx_recv.at[i], d, 0).start()
            plane_copy(ref, ba_send, by_recv.at[i], 0, d).start()

    def passed_pieces(i):
        for e in RING_STEPS:
            from_x = bias_all.at[i, lax.rem(x_at + e, 4), y, :4]
            from_y = bias_all.at[i, x_at, lax.rem(y + e, 4), 4:]
            for d in RING_STEPS:
                plane_copy(from_x, bb_send, bb_recv.at[i], 0, d).start()
                plane_copy(from_y, bb_send, bb_recv.at[i], d, 0).start()

    for i in range(OWN):
        arrive(recv_x.at[i], x_recv.at[i])
        product = recv_x[i].astype(F32).reshape(C, N)
        update = dot(w_o1_t[...], norm_columns(product, gains[1]).astype(BF16))
        middle = (xt[i] + gate1[i] * update).astype(BF16).astype(F32)
        mid[i] = middle
        attend = norm_columns(middle, gains[2]).astype(BF16)
        an_t[i] = attend
        bias_all[i, x_at, y, z] = dot(w_bias_ref[...], attend).astype(BF16)
        for dz in Z_STEPS:
            bz_copy(i, dz).start()

    scale = LOG2E / math.sqrt(WIDTH)
    head_of = lax.broadcasted_iota(jnp.int32, (C, N), 0)

    def project(i):
        attend = an_t[i]
        queries = dot(w_qv_t[0], attend) * scale
        values_ref[i] = dot(w_qv_t[1], attend).astype(BF16)
        keys = jnp.transpose(dot(w_k_t[...], attend)).astype(BF16)
        gate2_ref[i] = sigmoid(dot(w_gate2_t[...], attend))
        for h in range(HEADS):
            inside = (head_of >= WIDTH * h) & (head_of < WIDTH * (h + 1))
            scores_ref[i, h] = dot(keys, jnp.where(inside, queries, 0.0).astype(BF16))

    project(0)
    for i in range(OWN):
        arrive(bias_all.at[i, 0, 0, :7], bz_recv.at[i])
        own_pieces(i)
    project(1)
    for i in range(OWN):
        arrive(bias_all.at[i, 0, :3], bx_recv.at[i])
        arrive(bias_all.at[i, 0, :3], by_recv.at[i])
        passed_pieces(i)
    project(2)
    def o_copy(b, dz, dl):
        peer = col_peer(dz, dl)
        return remote(send_o.at[b, peer], out_ref.at[b, pl.ds(OWN * col, OWN)], o_send, o_recv, row, peer)

    def o_own(b):
        return pltpu.make_async_copy(send_o.at[b, col], out_ref.at[b, pl.ds(OWN * col, OWN)], o_recv)

    for b in range(OWN):
        arrive(bias_all.at[b, :3, :3], bb_recv.at[b])
        base = b * C * HEADS
        for r in range(ROWS):
            for c in range(COLS):
                piece = bias_all[b, (r // 4) * 2 + c % 2, r % 4, c // 2].astype(F32)
                at = base + (r * COLS + c) * HEADS
                for k in range(3):
                    wide_t[k, at : at + HEADS, :] = piece[:, k * 128 : (k + 1) * 128]
        lanes = slice(b * 128, (b + 1) * 128)
        for h in range(HEADS):
            for k in range(3):
                part = wide_t[k, pl.ds(base + h, C, stride=HEADS), :]
                rows = slice(k * 128, (k + 1) * 128)
                bias_t[h, rows, :] = jnp.transpose(part) * LOG2E + penalty[rows, lanes]
        for i in range(OWN):
            parts = []
            for h in range(HEADS):
                scores = scores_ref[i, h, :, lanes] + bias_t[h]
                weights = jnp.exp2(scores - jnp.max(scores, axis=0, keepdims=True))
                total = jnp.sum(weights, axis=0, keepdims=True)
                mixed = dot(values_ref[i, WIDTH * h : WIDTH * (h + 1)], weights.astype(BF16))
                parts.append(mixed / total)
            gated = (gate2_ref[i, :, lanes] * jnp.concatenate(parts, axis=0)).astype(BF16)
            result = mid[i, :, lanes] + dot(w_o2_t[...], gated)
            send_o[b, :, i] = jnp.transpose(result).reshape(COLS, 8, C).astype(BF16)
        for dz, dl in COL_STEPS:
            o_copy(b, dz, dl).start()
        o_own(b).start()

    arrive(x_rows.at[:, :15], r_send)
    arrive(send_lz.at[:, :7], lz_send)
    arrive(send_rx.at[:, :15], rx_send)
    arrive(send_rz.at[:, :7], rz_send)
    arrive(send_lx.at[:, :15], lx_send)
    arrive(send_p.at[:, :7], p_send)
    arrive(send_x.at[:, :15], x_send)
    arrive(bias_all.at[:, 0, 0, :7], bz_send)
    arrive(bias_all.at[:, :2, :3], ba_send)
    arrive(bias_all.at[:, :3, :3], bb_send)
    arrive(send_o.at[:, :15], o_send)
    arrive(out_ref, o_recv)


def interleave(blocks_ref, out_ref, lines):
    for b in range(OWN):
        lines[pl.ds(b, N, stride=OWN), :] = blocks_ref[b].astype(F32).reshape(N, C)
    out_ref[...] = lines[...].reshape(out_ref.shape).astype(BF16)


def owner_order():
    perm = np.zeros((C, C), np.float32)
    for owner in range(C):
        r, c = owner // COLS, owner % COLS
        perm[owner, (c // 2) * GS + 2 * r + c % 2] = 1.0
    return perm


def shards(
    pair_state, token_mask, block_pattern, triangle_norm, triangle_input, triangle_gate, product_norm,
    triangle_output, attend_norm, attend_inputs, attend_gate, attend_bias, attend_output,
):
    vmem = pl.BlockSpec(memory_space=pltpu.VMEM)
    hbm = pl.BlockSpec(memory_space=pl.ANY)
    smem = pl.BlockSpec(memory_space=pltpu.SMEM)
    dma = pltpu.SemaphoreType.DMA
    V = pltpu.VMEM
    blocks = pl.pallas_call(
        kernel,
        out_shape=jax.ShapeDtypeStruct((OWN, 48, 8, C), BF16),
        in_specs=[hbm, vmem, smem, hbm, vmem, hbm, hbm, vmem, hbm, vmem, hbm, hbm, vmem, hbm],
        out_specs=hbm,
        scratch_shapes=[
            V((OWN, COLS, 24, C), BF16),
            V((OWN, ZS, GS, N), BF16), V((OWN, ZS, GS, N), BF16), V((OWN, GS, ZS, N), BF16), V((OWN, GS, ZS, N), BF16),
            V((OWN, ZS, GS, N), BF16), V((OWN, ZS, GS, N), BF16), V((OWN, GS, ZS, N), BF16), V((OWN, GS, ZS, N), BF16),
            V((OWN, ZS, GS, N), BF16), V((OWN, ZS, GS, N), BF16),
            V((OWN, GS, 8, N), BF16), V((OWN, GS, 8, N), BF16),
            V((OWN, 4, 4, ZS, HEADS, N), BF16),
            V((OWN, COLS, OWN, 8, C), BF16),
            V((OWN, C, N), F32), V((OWN, C, N), F32), V((OWN, C, N), F32), V((OWN, C, N), BF16),
            V((3, HEADS * N, 128), F32), V((HEADS, N, C), F32), V((N, N), F32),
            V((OWN, HEADS, N, N), F32), V((OWN, C, N), BF16), V((OWN, C, N), F32),
            V((48, 24, C), BF16), V((C, C), BF16), V((C, 4 * C), BF16), V((C, C), BF16), V((C, C), BF16),
            V((C, 3 * C), BF16), V((C, C), BF16), V((C, C), BF16),
            V((2 * C, C), BF16), V((2 * C, C), BF16), V((C, C), BF16), V((C, C), BF16),
            V((2, C, C), BF16), V((C, C), BF16), V((C, C), BF16), V((C, C), BF16), V((3, C, C), F32), V((C, C), BF16),
            dma, dma((OWN,)), dma, dma((OWN,)), dma, dma((OWN,)), dma, dma, dma, dma((OWN,)),
            dma, dma((OWN,)), dma, dma((OWN,)),
            dma, dma((OWN,)), dma, dma((OWN,)), dma((OWN,)), dma, dma((OWN,)), dma, dma, dma((8,)),
        ],
        compiler_params=pltpu.CompilerParams(
            collective_id=0, has_side_effects=True, vmem_limit_bytes=63 * 1024 * 1024
        ),
        name="pairformer",
    )(
        pair_state, token_mask, block_pattern, jnp.asarray(owner_order(), BF16),
        triangle_norm.reshape(1, C), triangle_input, triangle_gate, product_norm.reshape(1, C), triangle_output,
        attend_norm.reshape(1, C), attend_inputs, attend_gate, attend_bias.T, attend_output,
    )
    return pl.pallas_call(
        interleave,
        out_shape=jax.ShapeDtypeStruct(pair_state.shape, BF16),
        in_specs=[vmem],
        out_specs=vmem,
        scratch_shapes=[V((48 * 24, C), F32)],
        name="interleave",
    )(blocks)


def solution(mesh):
    tile = P(("crop", "row"), "col", None)
    return jax.shard_map(
        shards,
        mesh=mesh,
        in_specs=(tile, P("crop"), P("crop", None)) + (P(),) * 10,
        out_specs=tile,
        check_vma=False,
    )
```

```python
import functools
import math

import jax
import jax.numpy as jnp
import numpy as np
from jax import lax
from jax.experimental import pallas as pl
from jax.experimental.pallas import tpu as pltpu
from jax.sharding import PartitionSpec as P

MESH = pl.DeviceIdType.MESH
F32 = jnp.float32
BF16 = jnp.bfloat16
EPS = 1e-05
ROWS, COLS, C, N = 8, 16, 128, 384
HEADS, WIDTH = 4, 32
ZS, GS, OWN = 8, 16, 3
LOG2E = 1.4426950408889634
MASKED = -1e30


def dot(a, b):
    return jnp.dot(a, b, preferred_element_type=F32)


def dot_nt(a, b):
    return lax.dot_general(a, b, (((1,), (1,)), ((), ())), preferred_element_type=F32)


def dot_tn(a, b):
    return lax.dot_general(a, b, (((0,), (0,)), ((), ())), preferred_element_type=F32)


def wide(gain):
    return jnp.concatenate([gain] * (N // 128), axis=1)


def norm_columns(v, gain):
    centered = v - jnp.mean(v, axis=0, keepdims=True)
    variance = jnp.mean(centered * centered, axis=0, keepdims=True)
    return centered * lax.rsqrt(variance + EPS) * wide(gain)


def sigmoid(v):
    return 1.0 / (1.0 + jnp.exp(-v))


def turned(w):
    return jnp.transpose(w.astype(F32))


RING_STEPS = (2, 1, 3)
Z_STEPS = (4, 3, 5, 2, 6, 1, 7)
COL_STEPS = tuple((dz, dl) for dz in Z_STEPS for dl in (1, 0)) + ((0, 1),)
XY_STEPS = tuple(sorted(
    ((dx, dy) for dx in range(4) for dy in range(4) if dx or dy),
    key=lambda s: -(min(s[0], 4 - s[0]) + min(s[1], 4 - s[1])),
))


def kernel(
    x_hbm, mask_hbm, pattern_hbm, perm_hbm,
    norm1_hbm, w_in_hbm, w_gate_hbm, norm2_hbm, w_out1_hbm,
    norm3_hbm, w_qkv_hbm, w_gate2_hbm, w_bias_hbm, w_out2_hbm,
    out_ref,
    x_rows, send_lz, recv_lz, send_rx, recv_rx, send_rz, recv_rz, send_lx, recv_lx, send_p, recv_p, send_x, recv_x,
    bias_all, send_o, xt, gate1, mid, an_t, wide_t, bias_t, penalty, scores_ref, values_ref, gate2_ref,
    mask_ref, pattern_ref, norms_ref, w_bias_ref,
    x_ref, perm_ref, w_in_ref, w_gate_ref, w_out1_ref, w_qkv_ref, w_gate2_ref, w_out2_ref,
    w_g, w_v, w_gate_t, w_o1_t, w_qv_t, w_k_t, w_gate2_t, w_o2_t, gains, z_order,
    r_send, r_recv, lz_send, lz_recv, rx_send, rx_recv, rz_send, rz_recv, lx_send, lx_recv, p_send, p_recv, x_send, x_recv,
    bz_send, bz_recv, ba_send, bx_recv, by_recv, bb_send, bb_recv, o_send, o_recv, fetch,
):
    row, col = lax.axis_index("row"), lax.axis_index("col")
    z, x_lo = col // 2, col % 2
    x_hi, y = row // 4, row % 4
    g = row * 2 + x_lo
    x_at = x_hi * 2 + x_lo

    def place(x, y, z):
        return (x // 2) * 4 + y, z * 2 + x % 2

    def signal(r, c):
        pl.semaphore_signal(barrier, inc=1, device_id={"row": r, "col": c}, device_id_type=MESH)

    def remote(src, dst, send, recv, r, c):
        return pltpu.make_async_remote_copy(
            src_ref=src, dst_ref=dst, send_sem=send, recv_sem=recv,
            device_id={"row": r, "col": c}, device_id_type=MESH,
        )

    def arrive(ref, sem):
        pltpu.make_async_copy(ref, ref, sem).wait()

    def col_peer(dz, dl):
        return lax.rem(z + dz, ZS) * 2 + lax.rem(x_lo + dl, 2)

    def xy_peer(dx, dy):
        xx, yy = lax.rem(x_at + dx, 4), lax.rem(y + dy, 4)
        r, c = place(xx, yy, z)
        return r * 2 + xx % 2, r, c

    barrier = pltpu.get_barrier_semaphore()
    for dz, dl in COL_STEPS:
        signal(row, col_peer(dz, dl))
    for dx, dy in XY_STEPS:
        if (dx, dy) != (1, 0) and (dx, dy) != (3, 0) and (dx, dy) != (2, 0):
            _, r, c = xy_peer(dx, dy)
            signal(r, c)
    _, r, c = xy_peer(2, 0)
    signal(r, c)
    other = x_at + 1 + 2 * (1 - x_at % 2)
    r, c = place(lax.rem(other, 4), y, z)
    signal(r, c)

    fetched = [
        pltpu.make_async_copy(src, dst, fetch.at[n])
        for n, (src, dst) in enumerate((
            (w_in_hbm, w_in_ref), (w_gate_hbm, w_gate_ref), (w_out1_hbm, w_out1_ref), (w_qkv_hbm, w_qkv_ref),
            (w_gate2_hbm, w_gate2_ref), (w_out2_hbm, w_out2_ref), (perm_hbm, perm_ref), (x_hbm, x_ref),
            (norm1_hbm, norms_ref.at[0]), (norm2_hbm, norms_ref.at[1]), (norm3_hbm, norms_ref.at[2]),
            (mask_hbm, mask_ref), (pattern_hbm, pattern_ref), (w_bias_hbm, w_bias_ref),
        ))
    ]
    for copy in fetched:
        copy.start()

    fetched[0].wait()
    w_t = jnp.concatenate([turned(w_in_ref[:, s * C : (s + 1) * C]) for s in range(4)], axis=0)
    ga, va, gb, vb = (w_t[s * C : (s + 1) * C].astype(BF16) for s in range(4))
    line, at = (lax.broadcasted_iota(jnp.int32, (C, C), d) for d in range(2))
    z_first = jnp.where((line & 15) * ZS + (line >> 4) == at, 1.0, 0.0).astype(BF16)
    z_order[...] = z_first
    w_g[:C], w_g[C:] = dot(z_first, ga).astype(BF16), gb
    w_v[:C], w_v[C:] = dot(z_first, va).astype(BF16), vb
    for slot in range(3):
        fetched[8 + slot].wait()
        gains[slot] = jnp.transpose(jnp.broadcast_to(norms_ref[slot], (C, C)))

    fetched[7].wait()
    pl.semaphore_wait(barrier, COLS - 1 + 2 * (ROWS - 1))

    def r_copy(i, dz, dl):
        peer = col_peer(dz, dl)
        return remote(x_ref.at[OWN * peer + i], x_rows.at[i, col], r_send, r_recv.at[i], row, peer)

    def r_own(i):
        return pltpu.make_async_copy(x_ref.at[OWN * col + i], x_rows.at[i, col], r_recv.at[i])

    for i in range(OWN):
        for dz, dl in COL_STEPS:
            r_copy(i, dz, dl).start()
        r_own(i).start()

    for copy in fetched[1:6] + fetched[11:]:
        copy.wait()
    w_gate_t[...] = turned(w_gate_ref[...]).astype(BF16)
    w_o1_t[...] = turned(w_out1_ref[...]).astype(BF16)
    w_o2_t[...] = turned(w_out2_ref[...]).astype(BF16)
    w_gate2_t[...] = turned(w_gate2_ref[...]).astype(BF16)
    w_qv_t[0] = turned(w_qkv_ref[:, :C]).astype(BF16)
    w_qv_t[1] = turned(w_qkv_ref[:, 2 * C :]).astype(BF16)
    w_k_t[...] = turned(w_qkv_ref[:, C : 2 * C]).astype(BF16)
    length = jnp.sum(mask_ref[...].reshape(1, N).astype(F32), axis=1, keepdims=True)
    lane = lax.broadcasted_iota(jnp.int32, (1, N), 1)
    mask = jnp.where((OWN * (lane & 127) + (lane >> 7)).astype(F32) < length, 1.0, 0.0)
    key_mask = jnp.transpose(jnp.broadcast_to(mask, (C, N)))
    for b in range(4):
        line = jnp.zeros((1, N), F32)
        for a in range(4):
            line = line + jnp.where(((lane & 127) >> 5) == a, pattern_ref[a, b].astype(F32), 0.0)
        for i in range(OWN):
            rows = slice(i * 128 + 32 * b, i * 128 + 32 * (b + 1))
            penalty[rows, :] = jnp.where(wide(key_mask[rows]) * line > 0.0, 0.0, MASKED)
    fetched[6].wait()

    def z_copy(i, src, dst, send, recv, dz):
        peer = lax.rem(z + dz, ZS)
        return remote(src.at[i, peer], dst.at[i, z], send, recv, row, peer * 2 + x_lo)

    def z_exchange(i, src, dst, send, recv):
        for dz in Z_STEPS:
            z_copy(i, src, dst, send, recv, dz).start()
        pltpu.make_async_copy(src.at[i, z], dst.at[i, z], recv).start()

    def xy_exchange(i, src, dst, send, recv):
        for dx, dy in XY_STEPS:
            peer, r, c = xy_peer(dx, dy)
            remote(src.at[i, peer], dst.at[i, g], send, recv, r, c).start()
        pltpu.make_async_copy(src.at[i, g], dst.at[i, g], recv).start()

    for i in range(OWN):
        arrive(x_rows.at[i], r_recv.at[i])
        wide_t[0, i * N : (i + 1) * N, :] = x_rows[i].astype(F32).reshape(N, C)
        x_t = jnp.concatenate(
            [jnp.transpose(wide_t[0, pl.ds(i * N + b, 128, stride=OWN), :]) for b in range(OWN)], axis=1
        )
        xt[i] = x_t
        normed = norm_columns(x_t, gains[0]).astype(BF16)
        an_t[i] = normed
        own_token = row * 48 + col * OWN + i
        mine = jnp.where(own_token.astype(F32) < length, 1.0, 0.0)
        factors = sigmoid(dot(w_g[...], normed)) * dot(w_v[...], normed) * (mask * mine)
        send_lz[i] = factors[:C].astype(BF16).reshape(ZS, GS, N)
        send_rx[i] = factors[C:].reshape(GS, ZS, N).astype(BF16)
        z_exchange(i, send_lz, recv_lz, lz_send, lz_recv.at[i])
        xy_exchange(i, send_rx, recv_rx, rx_send, rx_recv.at[i])
    for i in range(OWN):
        gate1[i] = sigmoid(dot(w_gate_t[...], an_t[i]))

    def spread(i, half, arrived):
        base = (2 * i + half) * C
        for b in range(3):
            wide_t[b, base : base + C, :] = arrived[:, b * 128 : (b + 1) * 128]
        return base

    def right_on(i):
        arrive(recv_rx.at[i], rx_recv.at[i])
        base = spread(i, 0, recv_rx[i].astype(F32).reshape(C, N))
        for to in range(ZS):
            for b in range(3):
                piece = wide_t[b, pl.ds(base + to, GS, stride=ZS), :]
                send_rz[i, to, :, b * 128 : (b + 1) * 128] = piece.astype(BF16)
        z_exchange(i, send_rz, recv_rz, rz_send, rz_recv)

    def left_on(i):
        arrive(recv_lz.at[i], lz_recv.at[i])
        base = spread(i, 1, recv_lz[i].astype(F32).reshape(C, N))
        for to in range(GS):
            for b in range(3):
                piece = wide_t[b, pl.ds(base + to, ZS, stride=GS), :]
                send_lx[i, to, :, b * 128 : (b + 1) * 128] = piece.astype(BF16)
        xy_exchange(i, send_lx, recv_lx, lx_send, lx_recv.at[i])

    right_on(0)
    right_on(1)
    left_on(0)
    right_on(2)
    left_on(1)
    left_on(2)
    arrive(recv_rz, rz_recv)
    right = jnp.concatenate(
        [dot(perm_ref[...], recv_rz[i].reshape(C, N)).astype(BF16) for i in range(OWN)], axis=0
    )
    for i in range(OWN):
        arrive(recv_lx.at[i], lx_recv.at[i])
        left = dot(z_order[...], recv_lx[i].astype(F32).reshape(C, N).astype(BF16)).astype(BF16)
        send_p[i] = dot_nt(left, right).astype(BF16).reshape(ZS, GS, N)
        z_exchange(i, send_p, recv_p, p_send, p_recv.at[i])

    for i in range(OWN):
        arrive(recv_p.at[i], p_recv.at[i])
        base = spread(i, 0, recv_p[i].astype(F32).reshape(C, N))
        for to in range(GS):
            for b in range(3):
                piece = wide_t[b, pl.ds(base + to, ZS, stride=GS), :]
                send_x[i, to, :, b * 128 : (b + 1) * 128] = piece.astype(BF16)
        xy_exchange(i, send_x, recv_x, x_send, x_recv.at[i])

    def bz_copy(i, dz):
        ref = bias_all.at[i, x_at, y, z]
        return remote(ref, ref, bz_send, bz_recv.at[i], *place(x_at, y, lax.rem(z + dz, ZS)))

    def plane_copy(ref, send, recv, dx, dy):
        return remote(ref, ref, send, recv, *place(lax.rem(x_at + dx, 4), lax.rem(y + dy, 4), z))

    def own_pieces(i):
        ref = bias_all.at[i, x_at, y]
        for d in RING_STEPS:
            plane_copy(ref, ba_send, bx_recv.at[i], d, 0).start()
            plane_copy(ref, ba_send, by_recv.at[i], 0, d).start()

    def passed_pieces(i):
        for e in RING_STEPS:
            from_x = bias_all.at[i, lax.rem(x_at + e, 4), y, :4]
            from_y = bias_all.at[i, x_at, lax.rem(y + e, 4), 4:]
            for d in RING_STEPS:
                plane_copy(from_x, bb_send, bb_recv.at[i], 0, d).start()
                plane_copy(from_y, bb_send, bb_recv.at[i], d, 0).start()

    scale = LOG2E / math.sqrt(WIDTH)
    head_of = lax.broadcasted_iota(jnp.int32, (C, N), 0)

    def project(i):
        attend = an_t[i]
        queries = dot(w_qv_t[0], attend) * scale
        values_ref[i] = dot(w_qv_t[1], attend).astype(BF16)
        keys = jnp.transpose(dot(w_k_t[...], attend)).astype(BF16)
        gate2_ref[i] = sigmoid(dot(w_gate2_t[...], attend))
        for h in range(HEADS):
            inside = (head_of >= WIDTH * h) & (head_of < WIDTH * (h + 1))
            scores_ref[i, h] = dot(keys, jnp.where(inside, queries, 0.0).astype(BF16)) + penalty[...]

    for i in range(OWN):
        arrive(recv_x.at[i], x_recv.at[i])
        product = recv_x[i].astype(F32).reshape(C, N)
        update = dot(w_o1_t[...], norm_columns(product, gains[1]).astype(BF16))
        middle = (xt[i] + gate1[i] * update).astype(BF16).astype(F32)
        mid[i] = middle
        attend = norm_columns(middle, gains[2]).astype(BF16)
        an_t[i] = attend
        bias_all[i, x_at, y, z] = (dot(w_bias_ref[...], attend) * LOG2E).astype(BF16)
        for dz in Z_STEPS:
            bz_copy(i, dz).start()
        project(i)

    for i in range(OWN):
        arrive(bias_all.at[i, 0, 0, :7], bz_recv.at[i])
        own_pieces(i)
    for i in range(OWN):
        arrive(bias_all.at[i, 0, :3], bx_recv.at[i])
        arrive(bias_all.at[i, 0, :3], by_recv.at[i])
        passed_pieces(i)
    def o_copy(b, dz, dl):
        peer = col_peer(dz, dl)
        return remote(send_o.at[b, peer], out_ref.at[b, pl.ds(OWN * col, OWN)], o_send, o_recv, row, peer)

    def o_own(b):
        return pltpu.make_async_copy(send_o.at[b, col], out_ref.at[b, pl.ds(OWN * col, OWN)], o_recv)

    for b in range(OWN):
        arrive(bias_all.at[b, :3, :3], bb_recv.at[b])
        base = b * C * HEADS
        for r in range(ROWS):
            for c in range(COLS):
                piece = bias_all[b, (r // 4) * 2 + c % 2, r % 4, c // 2].astype(F32)
                at = base + (r * COLS + c) * HEADS
                for k in range(3):
                    wide_t[k, at : at + HEADS, :] = piece[:, k * 128 : (k + 1) * 128]
        lanes = slice(b * 128, (b + 1) * 128)
        for h in range(HEADS):
            for k in range(3):
                part = wide_t[k, pl.ds(base + h, C, stride=HEADS), :]
                bias_t[h, k * 128 : (k + 1) * 128, :] = jnp.transpose(part)
        for i in range(OWN):
            parts = []
            for h in range(HEADS):
                scores = scores_ref[i, h, :, lanes] + bias_t[h]
                weights = jnp.exp2(scores - jnp.max(scores, axis=0, keepdims=True))
                total = jnp.sum(weights, axis=0, keepdims=True)
                mixed = dot(values_ref[i, WIDTH * h : WIDTH * (h + 1)], weights.astype(BF16))
                parts.append(mixed / total)
            gated = (gate2_ref[i, :, lanes] * jnp.concatenate(parts, axis=0)).astype(BF16)
            result = mid[i, :, lanes] + dot(w_o2_t[...], gated)
            send_o[b, :, i] = jnp.transpose(result).reshape(COLS, 8, C).astype(BF16)
        for dz, dl in COL_STEPS:
            o_copy(b, dz, dl).start()
        o_own(b).start()

    arrive(x_rows.at[:, :15], r_send)
    arrive(send_lz.at[:, :7], lz_send)
    arrive(send_rx.at[:, :15], rx_send)
    arrive(send_rz.at[:, :7], rz_send)
    arrive(send_lx.at[:, :15], lx_send)
    arrive(send_p.at[:, :7], p_send)
    arrive(send_x.at[:, :15], x_send)
    arrive(bias_all.at[:, 0, 0, :7], bz_send)
    arrive(bias_all.at[:, :2, :3], ba_send)
    arrive(bias_all.at[:, :3, :3], bb_send)
    arrive(send_o.at[:, :15], o_send)
    arrive(out_ref, o_recv)


def interleave(blocks_ref, out_ref, lines):
    for b in range(OWN):
        lines[pl.ds(b, N, stride=OWN), :] = blocks_ref[b].astype(F32).reshape(N, C)
    out_ref[...] = lines[...].reshape(out_ref.shape).astype(BF16)


def owner_order():
    perm = np.zeros((C, C), np.float32)
    for owner in range(C):
        r, c = owner // COLS, owner % COLS
        perm[owner, (c // 2) * GS + 2 * r + c % 2] = 1.0
    return perm


def shards(
    pair_state, token_mask, block_pattern, triangle_norm, triangle_input, triangle_gate, product_norm,
    triangle_output, attend_norm, attend_inputs, attend_gate, attend_bias, attend_output,
):
    vmem = pl.BlockSpec(memory_space=pltpu.VMEM)
    hbm = pl.BlockSpec(memory_space=pl.ANY)
    dma = pltpu.SemaphoreType.DMA
    V = pltpu.VMEM
    blocks = pl.pallas_call(
        kernel,
        out_shape=jax.ShapeDtypeStruct((OWN, 48, 8, C), BF16),
        in_specs=[hbm] * 14,
        out_specs=hbm,
        scratch_shapes=[
            V((OWN, COLS, 24, C), BF16),
            V((OWN, ZS, GS, N), BF16), V((OWN, ZS, GS, N), BF16), V((OWN, GS, ZS, N), BF16), V((OWN, GS, ZS, N), BF16),
            V((OWN, ZS, GS, N), BF16), V((OWN, ZS, GS, N), BF16), V((OWN, GS, ZS, N), BF16), V((OWN, GS, ZS, N), BF16),
            V((OWN, ZS, GS, N), BF16), V((OWN, ZS, GS, N), BF16),
            V((OWN, GS, 8, N), BF16), V((OWN, GS, 8, N), BF16),
            V((OWN, 4, 4, ZS, HEADS, N), BF16),
            V((OWN, COLS, OWN, 8, C), BF16),
            V((OWN, C, N), F32), V((OWN, C, N), F32), V((OWN, C, N), F32), V((OWN, C, N), BF16),
            V((3, HEADS * N, 128), F32), V((HEADS, N, C), F32), V((N, N), F32),
            V((OWN, HEADS, N, N), F32), V((OWN, C, N), BF16), V((OWN, C, N), F32),
            V((N,), jnp.int32), pltpu.SMEM((4, 4), jnp.int32), V((3, 1, C), F32), V((HEADS, C), BF16),
            V((48, 24, C), BF16), V((C, C), BF16), V((C, 4 * C), BF16), V((C, C), BF16), V((C, C), BF16),
            V((C, 3 * C), BF16), V((C, C), BF16), V((C, C), BF16),
            V((2 * C, C), BF16), V((2 * C, C), BF16), V((C, C), BF16), V((C, C), BF16),
            V((2, C, C), BF16), V((C, C), BF16), V((C, C), BF16), V((C, C), BF16), V((3, C, C), F32), V((C, C), BF16),
            dma, dma((OWN,)), dma, dma((OWN,)), dma, dma((OWN,)), dma, dma, dma, dma((OWN,)),
            dma, dma((OWN,)), dma, dma((OWN,)),
            dma, dma((OWN,)), dma, dma((OWN,)), dma((OWN,)), dma, dma((OWN,)), dma, dma, dma((14,)),
        ],
        compiler_params=pltpu.CompilerParams(
            collective_id=0, has_side_effects=True, vmem_limit_bytes=63 * 1024 * 1024
        ),
        name="pairformer",
    )(
        pair_state, token_mask, block_pattern, jnp.asarray(owner_order(), BF16),
        triangle_norm.reshape(1, C), triangle_input, triangle_gate, product_norm.reshape(1, C), triangle_output,
        attend_norm.reshape(1, C), attend_inputs, attend_gate, attend_bias.T, attend_output,
    )
    return pl.pallas_call(
        interleave,
        out_shape=jax.ShapeDtypeStruct(pair_state.shape, BF16),
        in_specs=[vmem],
        out_specs=vmem,
        scratch_shapes=[V((48 * 24, C), F32)],
        name="interleave",
    )(blocks)


def solution(mesh):
    tile = P(("crop", "row"), "col", None)
    return jax.shard_map(
        shards,
        mesh=mesh,
        in_specs=(tile, P("crop"), P("crop", None)) + (P(),) * 10,
        out_specs=tile,
        check_vma=False,
    )
```

```python
import functools
import math

import jax
import jax.numpy as jnp
import numpy as np
from jax import lax
from jax.experimental import pallas as pl
from jax.experimental.pallas import tpu as pltpu
from jax.sharding import PartitionSpec as P

MESH = pl.DeviceIdType.MESH
F32 = jnp.float32
BF16 = jnp.bfloat16
EPS = 1e-05
ROWS, COLS, C, N = 8, 16, 128, 384
HEADS, WIDTH = 4, 32
ZS, GS, OWN = 8, 16, 3
LOG2E = 1.4426950408889634
MASKED = -1e30


def dot(a, b):
    return jnp.dot(a, b, preferred_element_type=F32)


def dot_nt(a, b):
    return lax.dot_general(a, b, (((1,), (1,)), ((), ())), preferred_element_type=F32)


def dot_tn(a, b):
    return lax.dot_general(a, b, (((0,), (0,)), ((), ())), preferred_element_type=F32)


def wide(gain):
    return jnp.concatenate([gain] * (N // 128), axis=1)


def norm_columns(v, gain):
    centered = v - jnp.mean(v, axis=0, keepdims=True)
    variance = jnp.mean(centered * centered, axis=0, keepdims=True)
    return centered * lax.rsqrt(variance + EPS) * wide(gain)


def sigmoid(v):
    return 1.0 / (1.0 + jnp.exp(-v))


def turned(w):
    return jnp.transpose(w.astype(F32))


RING_STEPS = (2, 1, 3)
Z_STEPS = (4, 3, 5, 2, 6, 1, 7)
COL_STEPS = tuple((dz, dl) for dz in Z_STEPS for dl in (1, 0)) + ((0, 1),)
XY_STEPS = tuple(sorted(
    ((dx, dy) for dx in range(4) for dy in range(4) if dx or dy),
    key=lambda s: -(min(s[0], 4 - s[0]) + min(s[1], 4 - s[1])),
))


def kernel(
    x_hbm, mask_hbm, pattern_hbm, perm_hbm,
    norm1_hbm, w_in_hbm, w_gate_hbm, norm2_hbm, w_out1_hbm,
    norm3_hbm, w_qkv_hbm, w_gate2_hbm, w_bias_hbm, w_out2_hbm,
    out_ref,
    x_rows, send_lz, recv_lz, send_rx, recv_rx, send_rz, recv_rz, send_lx, recv_lx, send_p, recv_p, send_x, recv_x,
    bias_all, send_o, xt, gate1, mid, an_t, wide_t, bias_t, penalty, scores_ref, values_ref, gate2_ref,
    mask_ref, pattern_ref, norms_ref, w_bias_ref,
    x_ref, perm_ref, w_in_ref, w_gate_ref, w_out1_ref, w_qkv_ref, w_gate2_ref, w_out2_ref,
    w_g, w_v, w_gate_t, w_o1_t, w_qv_t, w_k_t, w_gate2_t, w_o2_t, gains, z_order,
    r_send, r_recv, lz_send, lz_recv, rx_send, rx_recv, rz_send, rz_recv, lx_send, lx_recv, p_send, p_recv, x_send, x_recv,
    bz_send, bz_recv, ba_send, bx_recv, by_recv, bb_send, bb_recv, o_send, o_recv, fetch,
):
    row, col = lax.axis_index("row"), lax.axis_index("col")
    z, x_lo = col // 2, col % 2
    x_hi, y = row // 4, row % 4
    g = row * 2 + x_lo
    x_at = x_hi * 2 + x_lo

    def place(x, y, z):
        return (x // 2) * 4 + y, z * 2 + x % 2

    def signal(r, c):
        pl.semaphore_signal(barrier, inc=1, device_id={"row": r, "col": c}, device_id_type=MESH)

    def remote(src, dst, send, recv, r, c):
        return pltpu.make_async_remote_copy(
            src_ref=src, dst_ref=dst, send_sem=send, recv_sem=recv,
            device_id={"row": r, "col": c}, device_id_type=MESH,
        )

    def arrive(ref, sem):
        pltpu.make_async_copy(ref, ref, sem).wait()

    def col_peer(dz, dl):
        return lax.rem(z + dz, ZS) * 2 + lax.rem(x_lo + dl, 2)

    def xy_peer(dx, dy):
        xx, yy = lax.rem(x_at + dx, 4), lax.rem(y + dy, 4)
        r, c = place(xx, yy, z)
        return r * 2 + xx % 2, r, c

    barrier = pltpu.get_barrier_semaphore()
    for dz, dl in COL_STEPS:
        signal(row, col_peer(dz, dl))
    for dx, dy in XY_STEPS:
        if (dx, dy) != (1, 0) and (dx, dy) != (3, 0) and (dx, dy) != (2, 0):
            _, r, c = xy_peer(dx, dy)
            signal(r, c)
    _, r, c = xy_peer(2, 0)
    signal(r, c)
    other = x_at + 1 + 2 * (1 - x_at % 2)
    r, c = place(lax.rem(other, 4), y, z)
    signal(r, c)

    fetched = [
        pltpu.make_async_copy(src, dst, fetch.at[n])
        for n, (src, dst) in enumerate((
            (w_in_hbm, w_in_ref), (w_gate_hbm, w_gate_ref), (w_out1_hbm, w_out1_ref), (w_qkv_hbm, w_qkv_ref),
            (w_gate2_hbm, w_gate2_ref), (w_out2_hbm, w_out2_ref), (perm_hbm, perm_ref), (x_hbm, x_ref),
            (norm1_hbm, norms_ref.at[0]), (norm2_hbm, norms_ref.at[1]), (norm3_hbm, norms_ref.at[2]),
            (mask_hbm, mask_ref), (pattern_hbm, pattern_ref), (w_bias_hbm, w_bias_ref),
        ))
    ]
    for copy in fetched:
        copy.start()

    fetched[0].wait()
    w_t = jnp.concatenate([turned(w_in_ref[:, s * C : (s + 1) * C]) for s in range(4)], axis=0)
    ga, va, gb, vb = (w_t[s * C : (s + 1) * C].astype(BF16) for s in range(4))
    line, at = (lax.broadcasted_iota(jnp.int32, (C, C), d) for d in range(2))
    z_first = jnp.where((line & 15) * ZS + (line >> 4) == at, 1.0, 0.0).astype(BF16)
    z_order[...] = z_first
    w_g[:C], w_g[C:] = dot(z_first, ga).astype(BF16), gb
    w_v[:C], w_v[C:] = dot(z_first, va).astype(BF16), vb
    for slot in range(3):
        fetched[8 + slot].wait()
        gains[slot] = jnp.transpose(jnp.broadcast_to(norms_ref[slot], (C, C)))

    fetched[7].wait()
    pl.semaphore_wait(barrier, COLS - 1 + 2 * (ROWS - 1))

    def r_copy(i, dz, dl):
        peer = col_peer(dz, dl)
        return remote(x_ref.at[OWN * peer + i], x_rows.at[i, col], r_send, r_recv.at[i], row, peer)

    def r_own(i):
        return pltpu.make_async_copy(x_ref.at[OWN * col + i], x_rows.at[i, col], r_recv.at[i])

    for i in range(OWN):
        for dz, dl in COL_STEPS:
            r_copy(i, dz, dl).start()
        r_own(i).start()

    for copy in fetched[1:6] + fetched[11:]:
        copy.wait()
    w_gate_t[...] = turned(w_gate_ref[...]).astype(BF16)
    w_o1_t[...] = turned(w_out1_ref[...]).astype(BF16)
    w_o2_t[...] = turned(w_out2_ref[...]).astype(BF16)
    w_gate2_t[...] = turned(w_gate2_ref[...]).astype(BF16)
    w_qv_t[0] = turned(w_qkv_ref[:, :C]).astype(BF16)
    w_qv_t[1] = turned(w_qkv_ref[:, 2 * C :]).astype(BF16)
    w_k_t[...] = turned(w_qkv_ref[:, C : 2 * C]).astype(BF16)
    length = jnp.sum(mask_ref[...].reshape(1, N).astype(F32), axis=1, keepdims=True)
    lane = lax.broadcasted_iota(jnp.int32, (1, N), 1)
    mask = jnp.where((OWN * (lane & 127) + (lane >> 7)).astype(F32) < length, 1.0, 0.0)
    key_mask = jnp.transpose(jnp.broadcast_to(mask, (C, N)))
    for b in range(4):
        line = jnp.zeros((1, N), F32)
        for a in range(4):
            line = line + jnp.where(((lane & 127) >> 5) == a, pattern_ref[a, b].astype(F32), 0.0)
        for i in range(OWN):
            rows = slice(i * 128 + 32 * b, i * 128 + 32 * (b + 1))
            penalty[rows, :] = jnp.where(wide(key_mask[rows]) * line > 0.0, 0.0, MASKED)
    fetched[6].wait()

    def z_copy(i, src, dst, send, recv, dz):
        peer = lax.rem(z + dz, ZS)
        return remote(src.at[i, peer], dst.at[i, z], send, recv, row, peer * 2 + x_lo)

    def z_exchange(i, src, dst, send, recv):
        for dz in Z_STEPS:
            z_copy(i, src, dst, send, recv, dz).start()
        pltpu.make_async_copy(src.at[i, z], dst.at[i, z], recv).start()

    def xy_exchange(i, src, dst, send, recv):
        for dx, dy in XY_STEPS:
            peer, r, c = xy_peer(dx, dy)
            remote(src.at[i, peer], dst.at[i, g], send, recv, r, c).start()
        pltpu.make_async_copy(src.at[i, g], dst.at[i, g], recv).start()

    for i in range(OWN):
        arrive(x_rows.at[i], r_recv.at[i])
        wide_t[0, i * N : (i + 1) * N, :] = x_rows[i].astype(F32).reshape(N, C)
        x_t = jnp.concatenate(
            [jnp.transpose(wide_t[0, pl.ds(i * N + b, 128, stride=OWN), :]) for b in range(OWN)], axis=1
        )
        xt[i] = x_t
        normed = norm_columns(x_t, gains[0]).astype(BF16)
        an_t[i] = normed
        own_token = row * 48 + col * OWN + i
        mine = jnp.where(own_token.astype(F32) < length, 1.0, 0.0)
        factors = sigmoid(dot(w_g[...], normed)) * dot(w_v[...], normed) * (mask * mine)
        send_lz[i] = factors[:C].astype(BF16).reshape(ZS, GS, N)
        send_rx[i] = factors[C:].reshape(GS, ZS, N).astype(BF16)
        z_exchange(i, send_lz, recv_lz, lz_send, lz_recv.at[i])
        xy_exchange(i, send_rx, recv_rx, rx_send, rx_recv.at[i])
    for i in range(OWN):
        gate1[i] = sigmoid(dot(w_gate_t[...], an_t[i]))

    def spread(i, half, arrived):
        base = (2 * i + half) * C
        for b in range(3):
            wide_t[b, base : base + C, :] = arrived[:, b * 128 : (b + 1) * 128]
        return base

    def right_on(i):
        arrive(recv_rx.at[i], rx_recv.at[i])
        base = spread(i, 0, recv_rx[i].astype(F32).reshape(C, N))
        for to in range(ZS):
            for b in range(3):
                piece = wide_t[b, pl.ds(base + to, GS, stride=ZS), :]
                send_rz[i, to, :, b * 128 : (b + 1) * 128] = piece.astype(BF16)
        z_exchange(i, send_rz, recv_rz, rz_send, rz_recv)

    def left_on(i):
        arrive(recv_lz.at[i], lz_recv.at[i])
        base = spread(i, 1, recv_lz[i].astype(F32).reshape(C, N))
        for to in range(GS):
            for b in range(3):
                piece = wide_t[b, pl.ds(base + to, ZS, stride=GS), :]
                send_lx[i, to, :, b * 128 : (b + 1) * 128] = piece.astype(BF16)
        xy_exchange(i, send_lx, recv_lx, lx_send, lx_recv.at[i])

    right_on(0)
    right_on(1)
    left_on(0)
    right_on(2)
    left_on(1)
    left_on(2)
    arrive(recv_rz, rz_recv)
    right = jnp.concatenate(
        [dot(perm_ref[...], recv_rz[i].reshape(C, N)).astype(BF16) for i in range(OWN)], axis=0
    )
    for i in range(OWN):
        arrive(recv_lx.at[i], lx_recv.at[i])
        left = dot(z_order[...], recv_lx[i].astype(F32).reshape(C, N).astype(BF16)).astype(BF16)
        send_p[i] = dot_nt(left, right).astype(BF16).reshape(ZS, GS, N)
        z_exchange(i, send_p, recv_p, p_send, p_recv.at[i])

    for i in range(OWN):
        arrive(recv_p.at[i], p_recv.at[i])
        base = spread(i, 0, recv_p[i].astype(F32).reshape(C, N))
        for to in range(GS):
            for b in range(3):
                piece = wide_t[b, pl.ds(base + to, ZS, stride=GS), :]
                send_x[i, to, :, b * 128 : (b + 1) * 128] = piece.astype(BF16)
        xy_exchange(i, send_x, recv_x, x_send, x_recv.at[i])

    def bz_copy(i, dz):
        ref = bias_all.at[i, x_at, y, z]
        return remote(ref, ref, bz_send, bz_recv.at[i], *place(x_at, y, lax.rem(z + dz, ZS)))

    def plane_copy(ref, send, recv, dx, dy):
        return remote(ref, ref, send, recv, *place(lax.rem(x_at + dx, 4), lax.rem(y + dy, 4), z))

    def own_pieces(i):
        ref = bias_all.at[i, x_at, y]
        for d in RING_STEPS:
            plane_copy(ref, ba_send, bx_recv.at[i], d, 0).start()
            plane_copy(ref, ba_send, by_recv.at[i], 0, d).start()

    def passed_pieces(i):
        for e in RING_STEPS:
            from_x = bias_all.at[i, lax.rem(x_at + e, 4), y, :4]
            from_y = bias_all.at[i, x_at, lax.rem(y + e, 4), 4:]
            for d in RING_STEPS:
                plane_copy(from_x, bb_send, bb_recv.at[i], 0, d).start()
                plane_copy(from_y, bb_send, bb_recv.at[i], d, 0).start()

    scale = LOG2E / math.sqrt(WIDTH)
    head_of = lax.broadcasted_iota(jnp.int32, (C, N), 0)

    def project(i):
        attend = an_t[i]
        queries = dot(w_qv_t[0], attend) * scale
        values_ref[i] = dot(w_qv_t[1], attend).astype(BF16)
        keys = jnp.transpose(dot(w_k_t[...], attend)).astype(BF16)
        gate2_ref[i] = sigmoid(dot(w_gate2_t[...], attend))
        for h in range(HEADS):
            inside = (head_of >= WIDTH * h) & (head_of < WIDTH * (h + 1))
            scores_ref[i, h] = dot(keys, jnp.where(inside, queries, 0.0).astype(BF16)) + penalty[...]

    for i in range(OWN):
        arrive(recv_x.at[i], x_recv.at[i])
        product = recv_x[i].astype(F32).reshape(C, N)
        update = dot(w_o1_t[...], norm_columns(product, gains[1]).astype(BF16))
        middle = (xt[i] + gate1[i] * update).astype(BF16).astype(F32)
        mid[i] = middle
        attend = norm_columns(middle, gains[2]).astype(BF16)
        an_t[i] = attend
        bias_all[i, x_at, y, z] = (dot(w_bias_ref[...], attend) * LOG2E).astype(BF16)
        for dz in Z_STEPS:
            bz_copy(i, dz).start()
        project(i)

    for i in range(OWN):
        arrive(bias_all.at[i, 0, 0, :7], bz_recv.at[i])
        own_pieces(i)
    for i in range(OWN):
        arrive(bias_all.at[i, 0, :3], bx_recv.at[i])
        arrive(bias_all.at[i, 0, :3], by_recv.at[i])
        passed_pieces(i)
    def o_exchange(b, first, count):
        target = out_ref.at[b, pl.ds(OWN * col + first, count)]
        for dz, dl in COL_STEPS:
            peer = col_peer(dz, dl)
            remote(send_o.at[b, peer, first : first + count], target, o_send, o_recv, row, peer).start()
        pltpu.make_async_copy(send_o.at[b, col, first : first + count], target, o_recv).start()

    for b in range(OWN):
        arrive(bias_all.at[b, :3, :3], bb_recv.at[b])
        base = b * C * HEADS
        for r in range(ROWS):
            for c in range(COLS):
                piece = bias_all[b, (r // 4) * 2 + c % 2, r % 4, c // 2].astype(F32)
                at = base + (r * COLS + c) * HEADS
                for k in range(3):
                    wide_t[k, at : at + HEADS, :] = piece[:, k * 128 : (k + 1) * 128]
        lanes = slice(b * 128, (b + 1) * 128)
        for h in range(HEADS):
            for k in range(3):
                part = wide_t[k, pl.ds(base + h, C, stride=HEADS), :]
                bias_t[h, k * 128 : (k + 1) * 128, :] = jnp.transpose(part)
        for i in range(OWN):
            parts = []
            for h in range(HEADS):
                scores = scores_ref[i, h, :, lanes] + bias_t[h]
                weights = jnp.exp2(scores - jnp.max(scores, axis=0, keepdims=True))
                total = jnp.sum(weights, axis=0, keepdims=True)
                mixed = dot(values_ref[i, WIDTH * h : WIDTH * (h + 1)], weights.astype(BF16))
                parts.append(mixed / total)
            gated = (gate2_ref[i, :, lanes] * jnp.concatenate(parts, axis=0)).astype(BF16)
            result = mid[i, :, lanes] + dot(w_o2_t[...], gated)
            send_o[b, :, i] = jnp.transpose(result).reshape(COLS, 8, C).astype(BF16)
            if b == OWN - 1:
                o_exchange(b, i, 1)
        if b < OWN - 1:
            o_exchange(b, 0, OWN)

    arrive(x_rows.at[:, :15], r_send)
    arrive(send_lz.at[:, :7], lz_send)
    arrive(send_rx.at[:, :15], rx_send)
    arrive(send_rz.at[:, :7], rz_send)
    arrive(send_lx.at[:, :15], lx_send)
    arrive(send_p.at[:, :7], p_send)
    arrive(send_x.at[:, :15], x_send)
    arrive(bias_all.at[:, 0, 0, :7], bz_send)
    arrive(bias_all.at[:, :2, :3], ba_send)
    arrive(bias_all.at[:, :3, :3], bb_send)
    arrive(send_o.at[:, :15], o_send)
    arrive(out_ref, o_recv)


def interleave(blocks_ref, out_ref, lines):
    for b in range(OWN):
        lines[pl.ds(b, N, stride=OWN), :] = blocks_ref[b].astype(F32).reshape(N, C)
    out_ref[...] = lines[...].reshape(out_ref.shape).astype(BF16)


def owner_order():
    perm = np.zeros((C, C), np.float32)
    for owner in range(C):
        r, c = owner // COLS, owner % COLS
        perm[owner, (c // 2) * GS + 2 * r + c % 2] = 1.0
    return perm


def shards(
    pair_state, token_mask, block_pattern, triangle_norm, triangle_input, triangle_gate, product_norm,
    triangle_output, attend_norm, attend_inputs, attend_gate, attend_bias, attend_output,
):
    vmem = pl.BlockSpec(memory_space=pltpu.VMEM)
    hbm = pl.BlockSpec(memory_space=pl.ANY)
    dma = pltpu.SemaphoreType.DMA
    V = pltpu.VMEM
    blocks = pl.pallas_call(
        kernel,
        out_shape=jax.ShapeDtypeStruct((OWN, 48, 8, C), BF16),
        in_specs=[hbm] * 14,
        out_specs=hbm,
        scratch_shapes=[
            V((OWN, COLS, 24, C), BF16),
            V((OWN, ZS, GS, N), BF16), V((OWN, ZS, GS, N), BF16), V((OWN, GS, ZS, N), BF16), V((OWN, GS, ZS, N), BF16),
            V((OWN, ZS, GS, N), BF16), V((OWN, ZS, GS, N), BF16), V((OWN, GS, ZS, N), BF16), V((OWN, GS, ZS, N), BF16),
            V((OWN, ZS, GS, N), BF16), V((OWN, ZS, GS, N), BF16),
            V((OWN, GS, 8, N), BF16), V((OWN, GS, 8, N), BF16),
            V((OWN, 4, 4, ZS, HEADS, N), BF16),
            V((OWN, COLS, OWN, 8, C), BF16),
            V((OWN, C, N), F32), V((OWN, C, N), F32), V((OWN, C, N), F32), V((OWN, C, N), BF16),
            V((3, HEADS * N, 128), F32), V((HEADS, N, C), F32), V((N, N), F32),
            V((OWN, HEADS, N, N), F32), V((OWN, C, N), BF16), V((OWN, C, N), F32),
            V((N,), jnp.int32), pltpu.SMEM((4, 4), jnp.int32), V((3, 1, C), F32), V((HEADS, C), BF16),
            V((48, 24, C), BF16), V((C, C), BF16), V((C, 4 * C), BF16), V((C, C), BF16), V((C, C), BF16),
            V((C, 3 * C), BF16), V((C, C), BF16), V((C, C), BF16),
            V((2 * C, C), BF16), V((2 * C, C), BF16), V((C, C), BF16), V((C, C), BF16),
            V((2, C, C), BF16), V((C, C), BF16), V((C, C), BF16), V((C, C), BF16), V((3, C, C), F32), V((C, C), BF16),
            dma, dma((OWN,)), dma, dma((OWN,)), dma, dma((OWN,)), dma, dma, dma, dma((OWN,)),
            dma, dma((OWN,)), dma, dma((OWN,)),
            dma, dma((OWN,)), dma, dma((OWN,)), dma((OWN,)), dma, dma((OWN,)), dma, dma, dma((14,)),
        ],
        compiler_params=pltpu.CompilerParams(
            collective_id=0, has_side_effects=True, vmem_limit_bytes=48 * 1024 * 1024
        ),
        name="pairformer",
    )(*(pltpu.with_memory_space_constraint(v, pltpu.HBM) for v in (
        pair_state, token_mask, block_pattern, jnp.asarray(owner_order(), BF16),
        triangle_norm.reshape(1, C), triangle_input, triangle_gate, product_norm.reshape(1, C), triangle_output,
        attend_norm.reshape(1, C), attend_inputs, attend_gate, attend_bias.T, attend_output,
    )))
    return pl.pallas_call(
        interleave,
        out_shape=jax.ShapeDtypeStruct(pair_state.shape, BF16),
        in_specs=[vmem],
        out_specs=vmem,
        scratch_shapes=[V((48 * 24, C), F32)],
        compiler_params=pltpu.CompilerParams(vmem_limit_bytes=6 * 1024 * 1024),
        name="interleave",
    )(blocks)


def solution(mesh):
    tile = P(("crop", "row"), "col", None)
    return jax.shard_map(
        shards,
        mesh=mesh,
        in_specs=(tile, P("crop"), P("crop", None)) + (P(),) * 10,
        out_specs=tile,
        check_vma=False,
    )
```

```python
import functools
import math

import jax
import jax.numpy as jnp
import numpy as np
from jax import lax
from jax.experimental import pallas as pl
from jax.experimental.pallas import tpu as pltpu
from jax.sharding import PartitionSpec as P

MESH = pl.DeviceIdType.MESH
F32 = jnp.float32
BF16 = jnp.bfloat16
EPS = 1e-05
ROWS, COLS, C, N = 8, 16, 128, 384
HEADS, WIDTH = 4, 32
ZS, GS, OWN = 8, 16, 3
LOG2E = 1.4426950408889634
MASKED = -1e30


def dot(a, b):
    return jnp.dot(a, b, preferred_element_type=F32)


def dot_nt(a, b):
    return lax.dot_general(a, b, (((1,), (1,)), ((), ())), preferred_element_type=F32)


def dot_tn(a, b):
    return lax.dot_general(a, b, (((0,), (0,)), ((), ())), preferred_element_type=F32)


def wide(gain):
    return jnp.concatenate([gain] * (N // 128), axis=1)


def norm_columns(v, gain):
    centered = v - jnp.mean(v, axis=0, keepdims=True)
    variance = jnp.mean(centered * centered, axis=0, keepdims=True)
    return centered * lax.rsqrt(variance + EPS) * wide(gain)


def sigmoid(v):
    return 1.0 / (1.0 + jnp.exp(-v))


def turned(w):
    return jnp.transpose(w.astype(F32))


RING_STEPS = (2, 1, 3)
Z_STEPS = (4, 3, 5, 2, 6, 1, 7)
COL_STEPS = tuple((dz, dl) for dz in Z_STEPS for dl in (1, 0)) + ((0, 1),)
XY_STEPS = tuple(sorted(
    ((dx, dy) for dx in range(4) for dy in range(4) if dx or dy),
    key=lambda s: -(min(s[0], 4 - s[0]) + min(s[1], 4 - s[1])),
))


def kernel(
    x_hbm, mask_hbm, pattern_hbm, perm_hbm,
    norm1_hbm, w_in_hbm, w_gate_hbm, norm2_hbm, w_out1_hbm,
    norm3_hbm, w_qkv_hbm, w_gate2_hbm, w_bias_hbm, w_out2_hbm,
    out_ref,
    x_rows, send_lz, recv_lz, send_rx, recv_rx, send_rz, recv_rz, send_lx, recv_lx, send_p, recv_p, send_x, recv_x,
    bias_all, send_o, xt, gate1, mid, an_t, wide_t, bias_t, penalty, scores_ref, values_ref, gate2_ref,
    mask_ref, pattern_ref, norms_ref, w_bias_ref,
    x_ref, perm_ref, w_in_ref, w_gate_ref, w_out1_ref, w_qkv_ref, w_gate2_ref, w_out2_ref,
    w_g, w_v, w_gate_t, w_o1_t, w_qv_t, w_k_t, w_gate2_t, w_o2_t, gains, z_order,
    r_send, r_recv, lz_send, lz_recv, rx_send, rx_recv, rz_send, rz_recv, lx_send, lx_recv, p_send, p_recv, x_send, x_recv,
    bz_send, bz_recv, ba_send, bx_recv, by_recv, bb_send, bb_recv, o_send, o_recv, fetch,
):
    row, col = lax.axis_index("row"), lax.axis_index("col")
    z, x_lo = col // 2, col % 2
    x_hi, y = row // 4, row % 4
    g = row * 2 + x_lo
    x_at = x_hi * 2 + x_lo

    def place(x, y, z):
        return (x // 2) * 4 + y, z * 2 + x % 2

    def signal(r, c):
        pl.semaphore_signal(barrier, inc=1, device_id={"row": r, "col": c}, device_id_type=MESH)

    def remote(src, dst, send, recv, r, c):
        return pltpu.make_async_remote_copy(
            src_ref=src, dst_ref=dst, send_sem=send, recv_sem=recv,
            device_id={"row": r, "col": c}, device_id_type=MESH,
        )

    def arrive(ref, sem):
        pltpu.make_async_copy(ref, ref, sem).wait()

    def col_peer(dz, dl):
        return lax.rem(z + dz, ZS) * 2 + lax.rem(x_lo + dl, 2)

    def xy_peer(dx, dy):
        xx, yy = lax.rem(x_at + dx, 4), lax.rem(y + dy, 4)
        r, c = place(xx, yy, z)
        return r * 2 + xx % 2, r, c

    barrier = pltpu.get_barrier_semaphore()
    for dz, dl in COL_STEPS:
        signal(row, col_peer(dz, dl))
    for dx, dy in XY_STEPS:
        if (dx, dy) != (1, 0) and (dx, dy) != (3, 0) and (dx, dy) != (2, 0):
            _, r, c = xy_peer(dx, dy)
            signal(r, c)
    _, r, c = xy_peer(2, 0)
    signal(r, c)
    other = x_at + 1 + 2 * (1 - x_at % 2)
    r, c = place(lax.rem(other, 4), y, z)
    signal(r, c)

    fetched = [
        pltpu.make_async_copy(src, dst, fetch.at[n])
        for n, (src, dst) in enumerate((
            (w_in_hbm, w_in_ref), (w_gate_hbm, w_gate_ref), (w_out1_hbm, w_out1_ref), (w_qkv_hbm, w_qkv_ref),
            (w_gate2_hbm, w_gate2_ref), (w_out2_hbm, w_out2_ref), (perm_hbm, perm_ref), (x_hbm, x_ref),
            (norm1_hbm, norms_ref.at[0]), (norm2_hbm, norms_ref.at[1]), (norm3_hbm, norms_ref.at[2]),
            (mask_hbm, mask_ref), (pattern_hbm, pattern_ref), (w_bias_hbm, w_bias_ref),
        ))
    ]
    for copy in fetched:
        copy.start()

    fetched[0].wait()
    w_t = jnp.concatenate([turned(w_in_ref[:, s * C : (s + 1) * C]) for s in range(4)], axis=0)
    ga, va, gb, vb = (w_t[s * C : (s + 1) * C].astype(BF16) for s in range(4))
    line, at = (lax.broadcasted_iota(jnp.int32, (C, C), d) for d in range(2))
    z_first = jnp.where((line & 15) * ZS + (line >> 4) == at, 1.0, 0.0).astype(BF16)
    z_order[...] = z_first
    w_g[:C], w_g[C:] = dot(z_first, ga).astype(BF16), gb
    w_v[:C], w_v[C:] = dot(z_first, va).astype(BF16), vb
    for slot in range(3):
        fetched[8 + slot].wait()
        gains[slot] = jnp.transpose(jnp.broadcast_to(norms_ref[slot], (C, C)))

    fetched[7].wait()
    pl.semaphore_wait(barrier, COLS - 1 + 2 * (ROWS - 1))

    def r_copy(i, dz, dl):
        peer = col_peer(dz, dl)
        return remote(x_ref.at[OWN * peer + i], x_rows.at[i, col], r_send, r_recv.at[i], row, peer)

    def r_own(i):
        return pltpu.make_async_copy(x_ref.at[OWN * col + i], x_rows.at[i, col], r_recv.at[i])

    for i in range(OWN):
        for dz, dl in COL_STEPS:
            r_copy(i, dz, dl).start()
        r_own(i).start()

    for copy in fetched[1:6] + fetched[11:]:
        copy.wait()
    w_gate_t[...] = turned(w_gate_ref[...]).astype(BF16)
    w_o1_t[...] = turned(w_out1_ref[...]).astype(BF16)
    w_o2_t[...] = turned(w_out2_ref[...]).astype(BF16)
    w_gate2_t[...] = turned(w_gate2_ref[...]).astype(BF16)
    w_qv_t[0] = turned(w_qkv_ref[:, :C]).astype(BF16)
    w_qv_t[1] = turned(w_qkv_ref[:, 2 * C :]).astype(BF16)
    w_k_t[...] = turned(w_qkv_ref[:, C : 2 * C]).astype(BF16)
    length = jnp.sum(mask_ref[...].reshape(1, N).astype(F32), axis=1, keepdims=True)
    lane = lax.broadcasted_iota(jnp.int32, (1, N), 1)
    mask = jnp.where((OWN * (lane & 127) + (lane >> 7)).astype(F32) < length, 1.0, 0.0)
    key_mask = jnp.transpose(jnp.broadcast_to(mask, (C, N)))
    for b in range(4):
        line = jnp.zeros((1, N), F32)
        for a in range(4):
            line = line + jnp.where(((lane & 127) >> 5) == a, pattern_ref[a, b].astype(F32), 0.0)
        for i in range(OWN):
            rows = slice(i * 128 + 32 * b, i * 128 + 32 * (b + 1))
            penalty[rows, :] = jnp.where(wide(key_mask[rows]) * line > 0.0, 0.0, MASKED)
    fetched[6].wait()

    def z_copy(i, src, dst, send, recv, dz):
        peer = lax.rem(z + dz, ZS)
        return remote(src.at[i, peer], dst.at[i, z], send, recv, row, peer * 2 + x_lo)

    def z_exchange(i, src, dst, send, recv):
        for dz in Z_STEPS:
            z_copy(i, src, dst, send, recv, dz).start()
        pltpu.make_async_copy(src.at[i, z], dst.at[i, z], recv).start()

    def xy_exchange(i, src, dst, send, recv):
        for dx, dy in XY_STEPS:
            peer, r, c = xy_peer(dx, dy)
            remote(src.at[i, peer], dst.at[i, g], send, recv, r, c).start()
        pltpu.make_async_copy(src.at[i, g], dst.at[i, g], recv).start()

    for i in range(OWN):
        arrive(x_rows.at[i], r_recv.at[i])
        wide_t[0, i * N : (i + 1) * N, :] = x_rows[i].astype(F32).reshape(N, C)
        x_t = jnp.concatenate(
            [jnp.transpose(wide_t[0, pl.ds(i * N + b, 128, stride=OWN), :]) for b in range(OWN)], axis=1
        )
        xt[i] = x_t
        normed = norm_columns(x_t, gains[0]).astype(BF16)
        an_t[i] = normed
        own_token = row * 48 + col * OWN + i
        mine = jnp.where(own_token.astype(F32) < length, 1.0, 0.0)
        factors = sigmoid(dot(w_g[C:], normed)) * dot(w_v[C:], normed) * (mask * mine)
        send_rx[i] = factors.reshape(GS, ZS, N).astype(BF16)
        xy_exchange(i, send_rx, recv_rx, rx_send, rx_recv.at[i])
        factors = sigmoid(dot(w_g[:C], normed)) * dot(w_v[:C], normed) * (mask * mine)
        send_lz[i] = factors.astype(BF16).reshape(ZS, GS, N)
        z_exchange(i, send_lz, recv_lz, lz_send, lz_recv.at[i])

    def spread(i, half, arrived):
        base = (2 * i + half) * C
        for b in range(3):
            wide_t[b, base : base + C, :] = arrived[:, b * 128 : (b + 1) * 128]
        return base

    def right_on(i):
        arrive(recv_rx.at[i], rx_recv.at[i])
        base = spread(i, 0, recv_rx[i].astype(F32).reshape(C, N))
        for to in range(ZS):
            for b in range(3):
                piece = wide_t[b, pl.ds(base + to, GS, stride=ZS), :]
                send_rz[i, to, :, b * 128 : (b + 1) * 128] = piece.astype(BF16)
        z_exchange(i, send_rz, recv_rz, rz_send, rz_recv)

    def left_on(i):
        arrive(recv_lz.at[i], lz_recv.at[i])
        base = spread(i, 1, recv_lz[i].astype(F32).reshape(C, N))
        for to in range(GS):
            for b in range(3):
                piece = wide_t[b, pl.ds(base + to, ZS, stride=GS), :]
                send_lx[i, to, :, b * 128 : (b + 1) * 128] = piece.astype(BF16)
        xy_exchange(i, send_lx, recv_lx, lx_send, lx_recv.at[i])

    right_on(0)
    right_on(1)
    left_on(0)
    right_on(2)
    left_on(1)
    left_on(2)
    for i in range(OWN):
        gate1[i] = sigmoid(dot(w_gate_t[...], an_t[i]))
    arrive(recv_rz, rz_recv)
    right = jnp.concatenate(
        [dot(perm_ref[...], recv_rz[i].reshape(C, N)).astype(BF16) for i in range(OWN)], axis=0
    )
    for i in range(OWN):
        arrive(recv_lx.at[i], lx_recv.at[i])
        left = dot(z_order[...], recv_lx[i].astype(F32).reshape(C, N).astype(BF16)).astype(BF16)
        send_p[i] = dot_nt(left, right).astype(BF16).reshape(ZS, GS, N)
        z_exchange(i, send_p, recv_p, p_send, p_recv.at[i])

    for i in range(OWN):
        arrive(recv_p.at[i], p_recv.at[i])
        base = spread(i, 0, recv_p[i].astype(F32).reshape(C, N))
        for to in range(GS):
            for b in range(3):
                piece = wide_t[b, pl.ds(base + to, ZS, stride=GS), :]
                send_x[i, to, :, b * 128 : (b + 1) * 128] = piece.astype(BF16)
        xy_exchange(i, send_x, recv_x, x_send, x_recv.at[i])

    def bz_copy(i, dz):
        ref = bias_all.at[i, x_at, y, z]
        return remote(ref, ref, bz_send, bz_recv.at[i], *place(x_at, y, lax.rem(z + dz, ZS)))

    def plane_copy(ref, send, recv, dx, dy):
        return remote(ref, ref, send, recv, *place(lax.rem(x_at + dx, 4), lax.rem(y + dy, 4), z))

    def own_pieces(i):
        ref = bias_all.at[i, x_at, y]
        for d in RING_STEPS:
            plane_copy(ref, ba_send, bx_recv.at[i], d, 0).start()
            plane_copy(ref, ba_send, by_recv.at[i], 0, d).start()

    def passed_pieces(i):
        for e in RING_STEPS:
            from_x = bias_all.at[i, lax.rem(x_at + e, 4), y, :4]
            from_y = bias_all.at[i, x_at, lax.rem(y + e, 4), 4:]
            for d in RING_STEPS:
                plane_copy(from_x, bb_send, bb_recv.at[i], 0, d).start()
                plane_copy(from_y, bb_send, bb_recv.at[i], d, 0).start()

    scale = LOG2E / math.sqrt(WIDTH)
    head_of = lax.broadcasted_iota(jnp.int32, (C, N), 0)

    def project(i):
        attend = an_t[i]
        queries = dot(w_qv_t[0], attend) * scale
        values_ref[i] = dot(w_qv_t[1], attend).astype(BF16)
        keys = jnp.transpose(dot(w_k_t[...], attend)).astype(BF16)
        gate2_ref[i] = sigmoid(dot(w_gate2_t[...], attend))
        for h in range(HEADS):
            inside = (head_of >= WIDTH * h) & (head_of < WIDTH * (h + 1))
            scores_ref[i, h] = dot(keys, jnp.where(inside, queries, 0.0).astype(BF16)) + penalty[...]

    for i in range(OWN):
        arrive(recv_x.at[i], x_recv.at[i])
        product = recv_x[i].astype(F32).reshape(C, N)
        update = dot(w_o1_t[...], norm_columns(product, gains[1]).astype(BF16))
        middle = (xt[i] + gate1[i] * update).astype(BF16).astype(F32)
        mid[i] = middle
        attend = norm_columns(middle, gains[2]).astype(BF16)
        an_t[i] = attend
        bias_all[i, x_at, y, z] = (dot(w_bias_ref[...], attend) * LOG2E).astype(BF16)
        for dz in Z_STEPS:
            bz_copy(i, dz).start()

    for i in range(OWN):
        arrive(bias_all.at[i, 0, 0, :7], bz_recv.at[i])
        own_pieces(i)
        if i < OWN - 1:
            project(i)
    for i in range(OWN):
        arrive(bias_all.at[i, 0, :3], bx_recv.at[i])
        arrive(bias_all.at[i, 0, :3], by_recv.at[i])
        passed_pieces(i)
        if i == 0:
            project(OWN - 1)
    def o_exchange(b):
        target = out_ref.at[b, pl.ds(OWN * col, OWN)]
        for dz, dl in COL_STEPS:
            peer = col_peer(dz, dl)
            remote(send_o.at[b, peer], target, o_send, o_recv, row, peer).start()
        pltpu.make_async_copy(send_o.at[b, col], target, o_recv).start()

    for b in range(OWN):
        arrive(bias_all.at[b, :3, :3], bb_recv.at[b])
        base = b * C * HEADS
        for r in range(ROWS):
            for c in range(COLS):
                piece = bias_all[b, (r // 4) * 2 + c % 2, r % 4, c // 2].astype(F32)
                at = base + (r * COLS + c) * HEADS
                for k in range(3):
                    wide_t[k, at : at + HEADS, :] = piece[:, k * 128 : (k + 1) * 128]
        lanes = slice(b * 128, (b + 1) * 128)
        for h in range(HEADS):
            for k in range(3):
                part = wide_t[k, pl.ds(base + h, C, stride=HEADS), :]
                bias_t[h, k * 128 : (k + 1) * 128, :] = jnp.transpose(part)
        for i in range(OWN):
            parts = []
            for h in range(HEADS):
                scores = scores_ref[i, h, :, lanes] + bias_t[h]
                weights = jnp.exp2(scores - jnp.max(scores, axis=0, keepdims=True))
                total = jnp.sum(weights, axis=0, keepdims=True)
                mixed = dot(values_ref[i, WIDTH * h : WIDTH * (h + 1)], weights.astype(BF16))
                parts.append(mixed / total)
            gated = (gate2_ref[i, :, lanes] * jnp.concatenate(parts, axis=0)).astype(BF16)
            result = mid[i, :, lanes] + dot(w_o2_t[...], gated)
            send_o[b, :, i] = jnp.transpose(result).reshape(COLS, 8, C).astype(BF16)
        o_exchange(b)

    arrive(x_rows.at[:, :15], r_send)
    arrive(send_lz.at[:, :7], lz_send)
    arrive(send_rx.at[:, :15], rx_send)
    arrive(send_rz.at[:, :7], rz_send)
    arrive(send_lx.at[:, :15], lx_send)
    arrive(send_p.at[:, :7], p_send)
    arrive(send_x.at[:, :15], x_send)
    arrive(bias_all.at[:, 0, 0, :7], bz_send)
    arrive(bias_all.at[:, :2, :3], ba_send)
    arrive(bias_all.at[:, :3, :3], bb_send)
    arrive(send_o.at[:, :15], o_send)
    arrive(out_ref, o_recv)


def interleave(blocks_ref, out_ref, lines):
    for b in range(OWN):
        lines[pl.ds(b, N, stride=OWN), :] = blocks_ref[b].astype(F32).reshape(N, C)
    out_ref[...] = lines[...].reshape(out_ref.shape).astype(BF16)


def owner_order():
    perm = np.zeros((C, C), np.float32)
    for owner in range(C):
        r, c = owner // COLS, owner % COLS
        perm[owner, (c // 2) * GS + 2 * r + c % 2] = 1.0
    return perm


def shards(
    pair_state, token_mask, block_pattern, triangle_norm, triangle_input, triangle_gate, product_norm,
    triangle_output, attend_norm, attend_inputs, attend_gate, attend_bias, attend_output,
):
    vmem = pl.BlockSpec(memory_space=pltpu.VMEM)
    hbm = pl.BlockSpec(memory_space=pl.ANY)
    dma = pltpu.SemaphoreType.DMA
    V = pltpu.VMEM
    blocks = pl.pallas_call(
        kernel,
        out_shape=jax.ShapeDtypeStruct((OWN, 48, 8, C), BF16),
        in_specs=[hbm] * 14,
        out_specs=hbm,
        scratch_shapes=[
            V((OWN, COLS, 24, C), BF16),
            V((OWN, ZS, GS, N), BF16), V((OWN, ZS, GS, N), BF16), V((OWN, GS, ZS, N), BF16), V((OWN, GS, ZS, N), BF16),
            V((OWN, ZS, GS, N), BF16), V((OWN, ZS, GS, N), BF16), V((OWN, GS, ZS, N), BF16), V((OWN, GS, ZS, N), BF16),
            V((OWN, ZS, GS, N), BF16), V((OWN, ZS, GS, N), BF16),
            V((OWN, GS, 8, N), BF16), V((OWN, GS, 8, N), BF16),
            V((OWN, 4, 4, ZS, HEADS, N), BF16),
            V((OWN, COLS, OWN, 8, C), BF16),
            V((OWN, C, N), F32), V((OWN, C, N), F32), V((OWN, C, N), F32), V((OWN, C, N), BF16),
            V((3, HEADS * N, 128), F32), V((HEADS, N, C), F32), V((N, N), F32),
            V((OWN, HEADS, N, N), F32), V((OWN, C, N), BF16), V((OWN, C, N), F32),
            V((N,), jnp.int32), pltpu.SMEM((4, 4), jnp.int32), V((3, 1, C), F32), V((HEADS, C), BF16),
            V((48, 24, C), BF16), V((C, C), BF16), V((C, 4 * C), BF16), V((C, C), BF16), V((C, C), BF16),
            V((C, 3 * C), BF16), V((C, C), BF16), V((C, C), BF16),
            V((2 * C, C), BF16), V((2 * C, C), BF16), V((C, C), BF16), V((C, C), BF16),
            V((2, C, C), BF16), V((C, C), BF16), V((C, C), BF16), V((C, C), BF16), V((3, C, C), F32), V((C, C), BF16),
            dma, dma((OWN,)), dma, dma((OWN,)), dma, dma((OWN,)), dma, dma, dma, dma((OWN,)),
            dma, dma((OWN,)), dma, dma((OWN,)),
            dma, dma((OWN,)), dma, dma((OWN,)), dma((OWN,)), dma, dma((OWN,)), dma, dma, dma((14,)),
        ],
        compiler_params=pltpu.CompilerParams(
            collective_id=0, has_side_effects=True, vmem_limit_bytes=48 * 1024 * 1024
        ),
        name="pairformer",
    )(*(pltpu.with_memory_space_constraint(v, pltpu.HBM) for v in (
        pair_state, token_mask, block_pattern, jnp.asarray(owner_order(), BF16),
        triangle_norm.reshape(1, C), triangle_input, triangle_gate, product_norm.reshape(1, C), triangle_output,
        attend_norm.reshape(1, C), attend_inputs, attend_gate, attend_bias.T, attend_output,
    )))
    return pl.pallas_call(
        interleave,
        out_shape=jax.ShapeDtypeStruct(pair_state.shape, BF16),
        in_specs=[vmem],
        out_specs=vmem,
        scratch_shapes=[V((48 * 24, C), F32)],
        compiler_params=pltpu.CompilerParams(vmem_limit_bytes=6 * 1024 * 1024),
        name="interleave",
    )(blocks)


def solution(mesh):
    tile = P(("crop", "row"), "col", None)
    return jax.shard_map(
        shards,
        mesh=mesh,
        in_specs=(tile, P("crop"), P("crop", None)) + (P(),) * 10,
        out_specs=tile,
        check_vma=False,
    )
```

```python
import functools
import math

import jax
import jax.numpy as jnp
import numpy as np
from jax import lax
from jax.experimental import pallas as pl
from jax.experimental.pallas import tpu as pltpu
from jax.sharding import PartitionSpec as P

MESH = pl.DeviceIdType.MESH
F32 = jnp.float32
BF16 = jnp.bfloat16
EPS = 1e-05
ROWS, COLS, C, N = 8, 16, 128, 384
HEADS, WIDTH = 4, 32
ZS, GS, OWN = 8, 16, 3
LOG2E = 1.4426950408889634
MASKED = -1e30


def dot(a, b):
    return jnp.dot(a, b, preferred_element_type=F32)


def dot_nt(a, b):
    return lax.dot_general(a, b, (((1,), (1,)), ((), ())), preferred_element_type=F32)


def dot_tn(a, b):
    return lax.dot_general(a, b, (((0,), (0,)), ((), ())), preferred_element_type=F32)


def wide(gain):
    return jnp.concatenate([gain] * (N // 128), axis=1)


def norm_columns(v, gain):
    centered = v - jnp.mean(v, axis=0, keepdims=True)
    variance = jnp.mean(centered * centered, axis=0, keepdims=True)
    return centered * lax.rsqrt(variance + EPS) * wide(gain)


def sigmoid(v):
    return 1.0 / (1.0 + jnp.exp(-v))


def turned(w):
    return jnp.transpose(w.astype(F32))


RING_STEPS = (2, 1, 3)
Z_STEPS = (4, 3, 5, 2, 6, 1, 7)
COL_STEPS = tuple((dz, dl) for dz in Z_STEPS for dl in (1, 0)) + ((0, 1),)
XY_STEPS = tuple(sorted(
    ((dx, dy) for dx in range(4) for dy in range(4) if dx or dy),
    key=lambda s: -(min(s[0], 4 - s[0]) + min(s[1], 4 - s[1])),
))


def kernel(
    x_hbm, mask_hbm, pattern_hbm, perm_hbm,
    norm1_hbm, w_in_hbm, w_gate_hbm, norm2_hbm, w_out1_hbm,
    norm3_hbm, w_qkv_hbm, w_gate2_hbm, w_bias_hbm, w_out2_hbm,
    out_ref,
    x_rows, send_za, recv_za, send_fa, recv_fa, send_fb, recv_fb, send_zb, recv_zb, send_p, recv_p, send_x, recv_x,
    bias_all, send_o, xt, gate1, mid, an_t, wide_t, bias_t, penalty, scores_ref, values_ref, gate2_ref,
    mask_ref, pattern_ref, norms_ref, w_bias_ref,
    x_ref, perm_ref, w_in_ref, w_gate_ref, w_out1_ref, w_qkv_ref, w_gate2_ref, w_out2_ref,
    w_g, w_v, w_gate_t, w_o1_t, w_qv_t, w_k_t, w_gate2_t, w_o2_t, gains,
    r_send, r_recv, za_send, za_recv, fa_send, fa_recv, fb_send, fb_recv, zb_send, zb_recv, p_send, p_recv, x_send, x_recv,
    bz_send, bz_recv, ba_send, bx_recv, by_recv, bb_send, bb_recv, o_send, o_recv, fetch,
):
    row, col = lax.axis_index("row"), lax.axis_index("col")
    z, x_lo = col // 2, col % 2
    x_hi, y = row // 4, row % 4
    g = row * 2 + x_lo
    x_at = x_hi * 2 + x_lo

    def place(x, y, z):
        return (x // 2) * 4 + y, z * 2 + x % 2

    def signal(r, c):
        pl.semaphore_signal(barrier, inc=1, device_id={"row": r, "col": c}, device_id_type=MESH)

    def remote(src, dst, send, recv, r, c):
        return pltpu.make_async_remote_copy(
            src_ref=src, dst_ref=dst, send_sem=send, recv_sem=recv,
            device_id={"row": r, "col": c}, device_id_type=MESH,
        )

    def arrive(ref, sem):
        pltpu.make_async_copy(ref, ref, sem).wait()

    def col_peer(dz, dl):
        return lax.rem(z + dz, ZS) * 2 + lax.rem(x_lo + dl, 2)

    def xy_peer(dx, dy):
        xx, yy = lax.rem(x_at + dx, 4), lax.rem(y + dy, 4)
        r, c = place(xx, yy, z)
        return r * 2 + xx % 2, r, c

    barrier = pltpu.get_barrier_semaphore()
    for dz, dl in COL_STEPS:
        signal(row, col_peer(dz, dl))
    for dx, dy in XY_STEPS:
        if (dx, dy) != (1, 0) and (dx, dy) != (3, 0) and (dx, dy) != (2, 0):
            _, r, c = xy_peer(dx, dy)
            signal(r, c)
    _, r, c = xy_peer(2, 0)
    signal(r, c)
    other = x_at + 1 + 2 * (1 - x_at % 2)
    r, c = place(lax.rem(other, 4), y, z)
    signal(r, c)

    fetched = [
        pltpu.make_async_copy(src, dst, fetch.at[n])
        for n, (src, dst) in enumerate((
            (w_in_hbm, w_in_ref), (w_gate_hbm, w_gate_ref), (w_out1_hbm, w_out1_ref), (w_qkv_hbm, w_qkv_ref),
            (w_gate2_hbm, w_gate2_ref), (w_out2_hbm, w_out2_ref), (perm_hbm, perm_ref), (x_hbm, x_ref),
            (norm1_hbm, norms_ref.at[0]), (norm2_hbm, norms_ref.at[1]), (norm3_hbm, norms_ref.at[2]),
            (mask_hbm, mask_ref), (pattern_hbm, pattern_ref), (w_bias_hbm, w_bias_ref),
        ))
    ]
    for copy in fetched:
        copy.start()

    fetched[0].wait()
    w_t = jnp.concatenate([turned(w_in_ref[:, s * C : (s + 1) * C]) for s in range(4)], axis=0)
    ga, va, gb, vb = (w_t[s * C : (s + 1) * C].astype(BF16) for s in range(4))
    line, at = (lax.broadcasted_iota(jnp.int32, (C, C), d) for d in range(2))
    z_first = jnp.where((line & 15) * ZS + (line >> 4) == at, 1.0, 0.0).astype(BF16)
    w_g[:C], w_g[C:] = dot(z_first, gb).astype(BF16), ga
    w_v[:C], w_v[C:] = dot(z_first, vb).astype(BF16), va
    for slot in range(3):
        fetched[8 + slot].wait()
        gains[slot] = jnp.transpose(jnp.broadcast_to(norms_ref[slot], (C, C)))

    fetched[7].wait()
    pl.semaphore_wait(barrier, COLS - 1 + 2 * (ROWS - 1))

    def r_copy(i, dz, dl):
        peer = col_peer(dz, dl)
        return remote(x_ref.at[OWN * peer + i], x_rows.at[i, col], r_send, r_recv.at[i], row, peer)

    def r_own(i):
        return pltpu.make_async_copy(x_ref.at[OWN * col + i], x_rows.at[i, col], r_recv.at[i])

    for i in range(OWN):
        for dz, dl in COL_STEPS:
            r_copy(i, dz, dl).start()
        r_own(i).start()

    for copy in fetched[1:6] + fetched[11:]:
        copy.wait()
    w_gate_t[...] = turned(w_gate_ref[...]).astype(BF16)
    w_o1_t[...] = turned(w_out1_ref[...]).astype(BF16)
    w_o2_t[...] = turned(w_out2_ref[...]).astype(BF16)
    w_gate2_t[...] = turned(w_gate2_ref[...]).astype(BF16)
    w_qv_t[0] = turned(w_qkv_ref[:, :C]).astype(BF16)
    w_qv_t[1] = turned(w_qkv_ref[:, 2 * C :]).astype(BF16)
    w_k_t[...] = turned(w_qkv_ref[:, C : 2 * C]).astype(BF16)
    length = jnp.sum(mask_ref[...].reshape(1, N).astype(F32), axis=1, keepdims=True)
    lane = lax.broadcasted_iota(jnp.int32, (1, N), 1)
    mask = jnp.where((OWN * (lane & 127) + (lane >> 7)).astype(F32) < length, 1.0, 0.0)
    key_mask = jnp.transpose(jnp.broadcast_to(mask, (C, N)))
    for b in range(4):
        line = jnp.zeros((1, N), F32)
        for a in range(4):
            line = line + jnp.where(((lane & 127) >> 5) == a, pattern_ref[a, b].astype(F32), 0.0)
        for i in range(OWN):
            rows = slice(i * 128 + 32 * b, i * 128 + 32 * (b + 1))
            penalty[rows, :] = jnp.where(wide(key_mask[rows]) * line > 0.0, 0.0, MASKED)
    fetched[6].wait()

    def z_copy(i, src, dst, send, recv, dz):
        peer = lax.rem(z + dz, ZS)
        return remote(src.at[i, peer], dst.at[i, z], send, recv, row, peer * 2 + x_lo)

    def z_exchange(i, src, dst, send, recv):
        for dz in Z_STEPS:
            z_copy(i, src, dst, send, recv, dz).start()
        pltpu.make_async_copy(src.at[i, z], dst.at[i, z], recv).start()

    def xy_exchange(i, src, dst, send, recv):
        for dx, dy in XY_STEPS:
            peer, r, c = xy_peer(dx, dy)
            remote(src.at[i, peer], dst.at[i, g], send, recv, r, c).start()
        pltpu.make_async_copy(src.at[i, g], dst.at[i, g], recv).start()

    for i in range(OWN):
        arrive(x_rows.at[i], r_recv.at[i])
        wide_t[0, i * N : (i + 1) * N, :] = x_rows[i].astype(F32).reshape(N, C)
        x_t = jnp.concatenate(
            [jnp.transpose(wide_t[0, pl.ds(i * N + b, 128, stride=OWN), :]) for b in range(OWN)], axis=1
        )
        xt[i] = x_t
        normed = norm_columns(x_t, gains[0]).astype(BF16)
        an_t[i] = normed
        own_token = row * 48 + col * OWN + i
        mine = jnp.where(own_token.astype(F32) < length, 1.0, 0.0)
        factors = sigmoid(dot(w_g[C:], normed)) * dot(w_v[C:], normed) * (mask * mine)
        send_fa[i] = factors.reshape(GS, ZS, N).astype(BF16)
        xy_exchange(i, send_fa, recv_fa, fa_send, fa_recv.at[i])
        factors = sigmoid(dot(w_g[:C], normed)) * dot(w_v[:C], normed) * (mask * mine)
        send_za[i] = factors.astype(BF16).reshape(ZS, GS, N)
        z_exchange(i, send_za, recv_za, za_send, za_recv.at[i])

    def spread(i, half, arrived):
        base = (2 * i + half) * C
        for b in range(3):
            wide_t[b, base : base + C, :] = arrived[:, b * 128 : (b + 1) * 128]
        return base

    def plane_on(i):
        arrive(recv_fa.at[i], fa_recv.at[i])
        base = spread(i, 0, recv_fa[i].astype(F32).reshape(C, N))
        for to in range(ZS):
            for b in range(3):
                piece = wide_t[b, pl.ds(base + to, GS, stride=ZS), :]
                send_fb[i, to, :, b * 128 : (b + 1) * 128] = piece.astype(BF16)
        z_exchange(i, send_fb, recv_fb, fb_send, fb_recv.at[i])

    def z_on(i):
        arrive(recv_za.at[i], za_recv.at[i])
        base = spread(i, 1, recv_za[i].astype(F32).reshape(C, N))
        for to in range(GS):
            for b in range(3):
                piece = wide_t[b, pl.ds(base + to, ZS, stride=GS), :]
                send_zb[i, to, :, b * 128 : (b + 1) * 128] = piece.astype(BF16)
        xy_exchange(i, send_zb, recv_zb, zb_send, zb_recv)

    plane_on(0)
    plane_on(1)
    z_on(0)
    plane_on(2)
    z_on(1)
    z_on(2)
    for i in range(OWN):
        gate1[i] = sigmoid(dot(w_gate_t[...], an_t[i]))
    arrive(recv_zb, zb_recv)
    right = jnp.concatenate(
        [dot(perm_ref[...], recv_zb[i].astype(F32).reshape(C, N).astype(BF16)).astype(BF16) for i in range(OWN)], axis=0
    )
    for i in range(OWN):
        arrive(recv_fb.at[i], fb_recv.at[i])
        left = recv_fb[i].reshape(C, N)
        send_p[i] = dot_nt(left, right).astype(BF16).reshape(ZS, GS, N)
        z_exchange(i, send_p, recv_p, p_send, p_recv.at[i])

    for i in range(OWN):
        arrive(recv_p.at[i], p_recv.at[i])
        base = spread(i, 0, recv_p[i].astype(F32).reshape(C, N))
        for to in range(GS):
            for b in range(3):
                piece = wide_t[b, pl.ds(base + to, ZS, stride=GS), :]
                send_x[i, to, :, b * 128 : (b + 1) * 128] = piece.astype(BF16)
        xy_exchange(i, send_x, recv_x, x_send, x_recv.at[i])

    def bz_copy(i, dz):
        ref = bias_all.at[i, x_at, y, z]
        return remote(ref, ref, bz_send, bz_recv.at[i], *place(x_at, y, lax.rem(z + dz, ZS)))

    def plane_copy(ref, send, recv, dx, dy):
        return remote(ref, ref, send, recv, *place(lax.rem(x_at + dx, 4), lax.rem(y + dy, 4), z))

    def own_pieces(i):
        ref = bias_all.at[i, x_at, y]
        for d in RING_STEPS:
            plane_copy(ref, ba_send, bx_recv.at[i], d, 0).start()
            plane_copy(ref, ba_send, by_recv.at[i], 0, d).start()

    def passed_pieces(i):
        for e in RING_STEPS:
            from_x = bias_all.at[i, lax.rem(x_at + e, 4), y, :4]
            from_y = bias_all.at[i, x_at, lax.rem(y + e, 4), 4:]
            for d in RING_STEPS:
                plane_copy(from_x, bb_send, bb_recv.at[i], 0, d).start()
                plane_copy(from_y, bb_send, bb_recv.at[i], d, 0).start()

    scale = LOG2E / math.sqrt(WIDTH)
    head_of = lax.broadcasted_iota(jnp.int32, (C, N), 0)

    def project(i):
        attend = an_t[i]
        queries = dot(w_qv_t[0], attend) * scale
        values_ref[i] = dot(w_qv_t[1], attend).astype(BF16)
        keys = jnp.transpose(dot(w_k_t[...], attend)).astype(BF16)
        gate2_ref[i] = sigmoid(dot(w_gate2_t[...], attend))
        for h in range(HEADS):
            inside = (head_of >= WIDTH * h) & (head_of < WIDTH * (h + 1))
            scores_ref[i, h] = dot(keys, jnp.where(inside, queries, 0.0).astype(BF16)) + penalty[...]

    for i in range(OWN):
        arrive(recv_x.at[i], x_recv.at[i])
        product = recv_x[i].astype(F32).reshape(C, N)
        update = dot(w_o1_t[...], norm_columns(product, gains[1]).astype(BF16))
        middle = (xt[i] + gate1[i] * update).astype(BF16).astype(F32)
        mid[i] = middle
        attend = norm_columns(middle, gains[2]).astype(BF16)
        an_t[i] = attend
        bias_all[i, x_at, y, z] = (dot(w_bias_ref[...], attend) * LOG2E).astype(BF16)
        for dz in Z_STEPS:
            bz_copy(i, dz).start()

    for i in range(OWN):
        arrive(bias_all.at[i, 0, 0, :7], bz_recv.at[i])
        own_pieces(i)
        if i < OWN - 1:
            project(i)
    for i in range(OWN):
        arrive(bias_all.at[i, 0, :3], bx_recv.at[i])
        arrive(bias_all.at[i, 0, :3], by_recv.at[i])
        passed_pieces(i)
        if i == 0:
            project(OWN - 1)
    def o_exchange(b):
        target = out_ref.at[b, pl.ds(OWN * col, OWN)]
        for dz, dl in COL_STEPS:
            peer = col_peer(dz, dl)
            remote(send_o.at[b, peer], target, o_send, o_recv, row, peer).start()
        pltpu.make_async_copy(send_o.at[b, col], target, o_recv).start()

    for b in range(OWN):
        arrive(bias_all.at[b, :3, :3], bb_recv.at[b])
        base = b * C * HEADS
        for r in range(ROWS):
            for c in range(COLS):
                piece = bias_all[b, (r // 4) * 2 + c % 2, r % 4, c // 2].astype(F32)
                at = base + (r * COLS + c) * HEADS
                for k in range(3):
                    wide_t[k, at : at + HEADS, :] = piece[:, k * 128 : (k + 1) * 128]
        lanes = slice(b * 128, (b + 1) * 128)
        for h in range(HEADS):
            for k in range(3):
                part = wide_t[k, pl.ds(base + h, C, stride=HEADS), :]
                bias_t[h, k * 128 : (k + 1) * 128, :] = jnp.transpose(part)
        for i in range(OWN):
            parts = []
            for h in range(HEADS):
                scores = scores_ref[i, h, :, lanes] + bias_t[h]
                weights = jnp.exp2(scores - jnp.max(scores, axis=0, keepdims=True))
                total = jnp.sum(weights, axis=0, keepdims=True)
                mixed = dot(values_ref[i, WIDTH * h : WIDTH * (h + 1)], weights.astype(BF16))
                parts.append(mixed / total)
            gated = (gate2_ref[i, :, lanes] * jnp.concatenate(parts, axis=0)).astype(BF16)
            result = mid[i, :, lanes] + dot(w_o2_t[...], gated)
            send_o[b, :, i] = jnp.transpose(result).reshape(COLS, 8, C).astype(BF16)
        o_exchange(b)

    arrive(x_rows.at[:, :15], r_send)
    arrive(send_za.at[:, :7], za_send)
    arrive(send_fa.at[:, :15], fa_send)
    arrive(send_fb.at[:, :7], fb_send)
    arrive(send_zb.at[:, :15], zb_send)
    arrive(send_p.at[:, :7], p_send)
    arrive(send_x.at[:, :15], x_send)
    arrive(bias_all.at[:, 0, 0, :7], bz_send)
    arrive(bias_all.at[:, :2, :3], ba_send)
    arrive(bias_all.at[:, :3, :3], bb_send)
    arrive(send_o.at[:, :15], o_send)
    arrive(out_ref, o_recv)


def interleave(blocks_ref, out_ref, lines):
    for b in range(OWN):
        lines[pl.ds(b, N, stride=OWN), :] = blocks_ref[b].astype(F32).reshape(N, C)
    out_ref[...] = lines[...].reshape(out_ref.shape).astype(BF16)


def owner_order():
    perm = np.zeros((C, C), np.float32)
    for owner in range(C):
        r, c = owner // COLS, owner % COLS
        perm[owner, (2 * r + c % 2) * ZS + c // 2] = 1.0
    return perm


def shards(
    pair_state, token_mask, block_pattern, triangle_norm, triangle_input, triangle_gate, product_norm,
    triangle_output, attend_norm, attend_inputs, attend_gate, attend_bias, attend_output,
):
    vmem = pl.BlockSpec(memory_space=pltpu.VMEM)
    hbm = pl.BlockSpec(memory_space=pl.ANY)
    dma = pltpu.SemaphoreType.DMA
    V = pltpu.VMEM
    blocks = pl.pallas_call(
        kernel,
        out_shape=jax.ShapeDtypeStruct((OWN, 48, 8, C), BF16),
        in_specs=[hbm] * 14,
        out_specs=hbm,
        scratch_shapes=[
            V((OWN, COLS, 24, C), BF16),
            V((OWN, ZS, GS, N), BF16), V((OWN, ZS, GS, N), BF16), V((OWN, GS, ZS, N), BF16), V((OWN, GS, ZS, N), BF16),
            V((OWN, ZS, GS, N), BF16), V((OWN, ZS, GS, N), BF16), V((OWN, GS, ZS, N), BF16), V((OWN, GS, ZS, N), BF16),
            V((OWN, ZS, GS, N), BF16), V((OWN, ZS, GS, N), BF16),
            V((OWN, GS, 8, N), BF16), V((OWN, GS, 8, N), BF16),
            V((OWN, 4, 4, ZS, HEADS, N), BF16),
            V((OWN, COLS, OWN, 8, C), BF16),
            V((OWN, C, N), F32), V((OWN, C, N), F32), V((OWN, C, N), F32), V((OWN, C, N), BF16),
            V((3, HEADS * N, 128), F32), V((HEADS, N, C), F32), V((N, N), F32),
            V((OWN, HEADS, N, N), F32), V((OWN, C, N), BF16), V((OWN, C, N), F32),
            V((N,), jnp.int32), pltpu.SMEM((4, 4), jnp.int32), V((3, 1, C), F32), V((HEADS, C), BF16),
            V((48, 24, C), BF16), V((C, C), BF16), V((C, 4 * C), BF16), V((C, C), BF16), V((C, C), BF16),
            V((C, 3 * C), BF16), V((C, C), BF16), V((C, C), BF16),
            V((2 * C, C), BF16), V((2 * C, C), BF16), V((C, C), BF16), V((C, C), BF16),
            V((2, C, C), BF16), V((C, C), BF16), V((C, C), BF16), V((C, C), BF16), V((3, C, C), F32),
            dma, dma((OWN,)), dma, dma((OWN,)), dma, dma((OWN,)), dma, dma((OWN,)), dma, dma,
            dma, dma((OWN,)), dma, dma((OWN,)),
            dma, dma((OWN,)), dma, dma((OWN,)), dma((OWN,)), dma, dma((OWN,)), dma, dma, dma((14,)),
        ],
        compiler_params=pltpu.CompilerParams(
            collective_id=0, has_side_effects=True, vmem_limit_bytes=48 * 1024 * 1024
        ),
        name="pairformer",
    )(*(pltpu.with_memory_space_constraint(v, pltpu.HBM) for v in (
        pair_state, token_mask, block_pattern, jnp.asarray(owner_order(), BF16),
        triangle_norm.reshape(1, C), triangle_input, triangle_gate, product_norm.reshape(1, C), triangle_output,
        attend_norm.reshape(1, C), attend_inputs, attend_gate, attend_bias.T, attend_output,
    )))
    return pl.pallas_call(
        interleave,
        out_shape=jax.ShapeDtypeStruct(pair_state.shape, BF16),
        in_specs=[vmem],
        out_specs=vmem,
        scratch_shapes=[V((48 * 24, C), F32)],
        compiler_params=pltpu.CompilerParams(vmem_limit_bytes=6 * 1024 * 1024),
        name="interleave",
    )(blocks)


def solution(mesh):
    tile = P(("crop", "row"), "col", None)
    return jax.shard_map(
        shards,
        mesh=mesh,
        in_specs=(tile, P("crop"), P("crop", None)) + (P(),) * 10,
        out_specs=tile,
        check_vma=False,
    )
```

```python
import functools
import math

import jax
import jax.numpy as jnp
import numpy as np
from jax import lax
from jax.experimental import pallas as pl
from jax.experimental.pallas import tpu as pltpu
from jax.sharding import PartitionSpec as P

MESH = pl.DeviceIdType.MESH
F32 = jnp.float32
BF16 = jnp.bfloat16
EPS = 1e-05
ROWS, COLS, C, N = 8, 16, 128, 384
HEADS, WIDTH = 4, 32
ZS, GS, OWN = 8, 16, 3
LOG2E = 1.4426950408889634
MASKED = -1e30


def dot(a, b):
    return jnp.dot(a, b, preferred_element_type=F32)


def dot_nt(a, b):
    return lax.dot_general(a, b, (((1,), (1,)), ((), ())), preferred_element_type=F32)


def dot_tn(a, b):
    return lax.dot_general(a, b, (((0,), (0,)), ((), ())), preferred_element_type=F32)


def wide(gain):
    return jnp.concatenate([gain] * (N // 128), axis=1)


def norm_columns(v, gain):
    centered = v - jnp.mean(v, axis=0, keepdims=True)
    variance = jnp.mean(centered * centered, axis=0, keepdims=True)
    return centered * lax.rsqrt(variance + EPS) * wide(gain)


def sigmoid(v):
    return 1.0 / (1.0 + jnp.exp(-v))


def turned(w):
    return jnp.transpose(w.astype(F32))


RING_STEPS = (2, 1, 3)
Z_STEPS = (4, 3, 5, 2, 6, 1, 7)
COL_STEPS = tuple((dz, dl) for dz in Z_STEPS for dl in (1, 0)) + ((0, 1),)
XY_STEPS = tuple(sorted(
    ((dx, dy) for dx in range(4) for dy in range(4) if dx or dy),
    key=lambda s: -(min(s[0], 4 - s[0]) + min(s[1], 4 - s[1])),
))


def kernel(
    x_hbm, mask_hbm, pattern_hbm, perm_hbm,
    norm1_hbm, w_in_hbm, w_gate_hbm, norm2_hbm, w_out1_hbm,
    norm3_hbm, w_qkv_hbm, w_gate2_hbm, w_bias_hbm, w_out2_hbm,
    out_ref,
    x_rows, send_za, recv_za, send_fa, recv_fa, send_fb, recv_fb, send_zb, recv_zb, send_p, recv_p, send_x, recv_x,
    bias_all, send_o, xt, gate1, mid, an_t, wide_t, bias_t, penalty, scores_ref, values_ref, gate2_ref,
    mask_ref, pattern_ref, norms_ref, w_bias_ref,
    x_ref, perm_ref, w_in_ref, w_gate_ref, w_out1_ref, w_qkv_ref, w_gate2_ref, w_out2_ref,
    w_g, w_v, w_gate_t, w_o1_t, w_qv_t, w_k_t, w_gate2_t, w_o2_t, gains,
    r_send, r_recv, za_send, za_recv, fa_send, fa_recv, fb_send, fb_recv, zb_send, zb_recv, p_send, p_recv, x_send, x_recv,
    bz_send, bz_recv, ba_send, bx_recv, by_recv, bb_send, bb_recv, o_send, o_recv, fetch,
):
    row, col = lax.axis_index("row"), lax.axis_index("col")
    z, x_lo = col // 2, col % 2
    x_hi, y = row // 4, row % 4
    g = row * 2 + x_lo
    x_at = x_hi * 2 + x_lo

    def place(x, y, z):
        return (x // 2) * 4 + y, z * 2 + x % 2

    def signal(r, c):
        pl.semaphore_signal(barrier, inc=1, device_id={"row": r, "col": c}, device_id_type=MESH)

    def remote(src, dst, send, recv, r, c):
        return pltpu.make_async_remote_copy(
            src_ref=src, dst_ref=dst, send_sem=send, recv_sem=recv,
            device_id={"row": r, "col": c}, device_id_type=MESH,
        )

    def arrive(ref, sem):
        pltpu.make_async_copy(ref, ref, sem).wait()

    def col_peer(dz, dl):
        return lax.rem(z + dz, ZS) * 2 + lax.rem(x_lo + dl, 2)

    def xy_peer(dx, dy):
        xx, yy = lax.rem(x_at + dx, 4), lax.rem(y + dy, 4)
        r, c = place(xx, yy, z)
        return r * 2 + xx % 2, r, c

    barrier = pltpu.get_barrier_semaphore()
    for dz, dl in COL_STEPS:
        signal(row, col_peer(dz, dl))
    for dx, dy in XY_STEPS:
        if (dx, dy) != (1, 0) and (dx, dy) != (3, 0) and (dx, dy) != (2, 0):
            _, r, c = xy_peer(dx, dy)
            signal(r, c)
    _, r, c = xy_peer(2, 0)
    signal(r, c)
    other = x_at + 1 + 2 * (1 - x_at % 2)
    r, c = place(lax.rem(other, 4), y, z)
    signal(r, c)

    fetched = [
        pltpu.make_async_copy(src, dst, fetch.at[n])
        for n, (src, dst) in enumerate((
            (w_in_hbm, w_in_ref), (w_gate_hbm, w_gate_ref), (w_out1_hbm, w_out1_ref), (w_qkv_hbm, w_qkv_ref),
            (w_gate2_hbm, w_gate2_ref), (w_out2_hbm, w_out2_ref), (perm_hbm, perm_ref), (x_hbm, x_ref),
            (norm1_hbm, norms_ref.at[0]), (norm2_hbm, norms_ref.at[1]), (norm3_hbm, norms_ref.at[2]),
            (mask_hbm, mask_ref), (pattern_hbm, pattern_ref), (w_bias_hbm, w_bias_ref),
        ))
    ]
    for copy in fetched:
        copy.start()

    fetched[0].wait()
    w_t = jnp.concatenate([turned(w_in_ref[:, s * C : (s + 1) * C]) for s in range(4)], axis=0)
    ga, va, gb, vb = (w_t[s * C : (s + 1) * C].astype(BF16) for s in range(4))
    line, at = (lax.broadcasted_iota(jnp.int32, (C, C), d) for d in range(2))
    z_first = jnp.where((line & 15) * ZS + (line >> 4) == at, 1.0, 0.0).astype(BF16)
    w_g[:C], w_g[C:] = dot(z_first, gb).astype(BF16), ga
    w_v[:C], w_v[C:] = dot(z_first, vb).astype(BF16), va
    for slot in range(3):
        fetched[8 + slot].wait()
        gains[slot] = jnp.transpose(jnp.broadcast_to(norms_ref[slot], (C, C)))

    fetched[7].wait()
    pl.semaphore_wait(barrier, COLS - 1 + 2 * (ROWS - 1))

    def r_copy(i, dz, dl):
        peer = col_peer(dz, dl)
        return remote(x_ref.at[OWN * peer + i], x_rows.at[i, col], r_send, r_recv.at[i], row, peer)

    def r_own(i):
        return pltpu.make_async_copy(x_ref.at[OWN * col + i], x_rows.at[i, col], r_recv.at[i])

    for i in range(OWN):
        for dz, dl in COL_STEPS:
            r_copy(i, dz, dl).start()
        r_own(i).start()

    for copy in fetched[1:6] + fetched[11:]:
        copy.wait()
    w_gate_t[...] = turned(w_gate_ref[...]).astype(BF16)
    w_o1_t[...] = turned(w_out1_ref[...]).astype(BF16)
    w_o2_t[...] = turned(w_out2_ref[...]).astype(BF16)
    w_gate2_t[...] = turned(w_gate2_ref[...]).astype(BF16)
    w_qv_t[0] = turned(w_qkv_ref[:, :C]).astype(BF16)
    w_qv_t[1] = turned(w_qkv_ref[:, 2 * C :]).astype(BF16)
    w_k_t[...] = turned(w_qkv_ref[:, C : 2 * C]).astype(BF16)
    length = jnp.sum(mask_ref[...].reshape(1, N).astype(F32), axis=1, keepdims=True)
    lane = lax.broadcasted_iota(jnp.int32, (1, N), 1)
    mask = jnp.where((OWN * (lane & 127) + (lane >> 7)).astype(F32) < length, 1.0, 0.0)
    key_mask = jnp.transpose(jnp.broadcast_to(mask, (C, N)))
    for b in range(4):
        line = jnp.zeros((1, N), F32)
        for a in range(4):
            line = line + jnp.where(((lane & 127) >> 5) == a, pattern_ref[a, b].astype(F32), 0.0)
        for i in range(OWN):
            rows = slice(i * 128 + 32 * b, i * 128 + 32 * (b + 1))
            penalty[rows, :] = jnp.where(wide(key_mask[rows]) * line > 0.0, 0.0, MASKED)
    fetched[6].wait()

    def z_copy(i, src, dst, send, recv, dz):
        peer = lax.rem(z + dz, ZS)
        return remote(src.at[i, peer], dst.at[i, z], send, recv, row, peer * 2 + x_lo)

    def z_exchange(i, src, dst, send, recv):
        for dz in Z_STEPS:
            z_copy(i, src, dst, send, recv, dz).start()
        pltpu.make_async_copy(src.at[i, z], dst.at[i, z], recv).start()

    def xy_exchange(i, src, dst, send, recv):
        for dx, dy in XY_STEPS:
            peer, r, c = xy_peer(dx, dy)
            remote(src.at[i, peer], dst.at[i, g], send, recv, r, c).start()
        pltpu.make_async_copy(src.at[i, g], dst.at[i, g], recv).start()

    for i in range(OWN):
        arrive(x_rows.at[i], r_recv.at[i])
        wide_t[0, i * N : (i + 1) * N, :] = x_rows[i].astype(F32).reshape(N, C)
        x_t = jnp.concatenate(
            [jnp.transpose(wide_t[0, pl.ds(i * N + b, 128, stride=OWN), :]) for b in range(OWN)], axis=1
        )
        xt[i] = x_t
        normed = norm_columns(x_t, gains[0]).astype(BF16)
        an_t[i] = normed
        own_token = row * 48 + col * OWN + i
        mine = jnp.where(own_token.astype(F32) < length, 1.0, 0.0)
        factors = sigmoid(dot(w_g[:C], normed)) * dot(w_v[:C], normed) * (mask * mine)
        send_za[i] = factors.astype(BF16).reshape(ZS, GS, N)
        z_exchange(i, send_za, recv_za, za_send, za_recv.at[i])
        factors = sigmoid(dot(w_g[C:], normed)) * dot(w_v[C:], normed) * (mask * mine)
        send_fa[i] = factors.reshape(GS, ZS, N).astype(BF16)
        xy_exchange(i, send_fa, recv_fa, fa_send, fa_recv.at[i])

    def spread(i, half, arrived):
        base = (2 * i + half) * C
        for b in range(3):
            wide_t[b, base : base + C, :] = arrived[:, b * 128 : (b + 1) * 128]
        return base

    def plane_on(i):
        arrive(recv_fa.at[i], fa_recv.at[i])
        base = spread(i, 0, recv_fa[i].astype(F32).reshape(C, N))
        for to in range(ZS):
            for b in range(3):
                piece = wide_t[b, pl.ds(base + to, GS, stride=ZS), :]
                send_fb[i, to, :, b * 128 : (b + 1) * 128] = piece.astype(BF16)
        z_exchange(i, send_fb, recv_fb, fb_send, fb_recv.at[i])

    def z_on(i):
        arrive(recv_za.at[i], za_recv.at[i])
        base = spread(i, 1, recv_za[i].astype(F32).reshape(C, N))
        for to in range(GS):
            for b in range(3):
                piece = wide_t[b, pl.ds(base + to, ZS, stride=GS), :]
                send_zb[i, to, :, b * 128 : (b + 1) * 128] = piece.astype(BF16)
        xy_exchange(i, send_zb, recv_zb, zb_send, zb_recv)

    for i in range(OWN):
        plane_on(i)
        z_on(i)
    for i in range(OWN):
        gate1[i] = sigmoid(dot(w_gate_t[...], an_t[i]))
    arrive(recv_zb, zb_recv)
    right = jnp.concatenate(
        [dot(perm_ref[...], recv_zb[i].astype(F32).reshape(C, N).astype(BF16)).astype(BF16) for i in range(OWN)], axis=0
    )
    for i in range(OWN):
        arrive(recv_fb.at[i], fb_recv.at[i])
        left = recv_fb[i].reshape(C, N)
        send_p[i] = dot_nt(left, right).astype(BF16).reshape(ZS, GS, N)
        z_exchange(i, send_p, recv_p, p_send, p_recv.at[i])

    for i in range(OWN):
        arrive(recv_p.at[i], p_recv.at[i])
        base = spread(i, 0, recv_p[i].astype(F32).reshape(C, N))
        for to in range(GS):
            for b in range(3):
                piece = wide_t[b, pl.ds(base + to, ZS, stride=GS), :]
                send_x[i, to, :, b * 128 : (b + 1) * 128] = piece.astype(BF16)
        xy_exchange(i, send_x, recv_x, x_send, x_recv.at[i])

    def bz_copy(i, dz):
        ref = bias_all.at[i, x_at, y, z]
        return remote(ref, ref, bz_send, bz_recv.at[i], *place(x_at, y, lax.rem(z + dz, ZS)))

    def plane_copy(ref, send, recv, dx, dy):
        return remote(ref, ref, send, recv, *place(lax.rem(x_at + dx, 4), lax.rem(y + dy, 4), z))

    def own_pieces(i):
        ref = bias_all.at[i, x_at, y]
        for d in RING_STEPS:
            plane_copy(ref, ba_send, bx_recv.at[i], d, 0).start()
            plane_copy(ref, ba_send, by_recv.at[i], 0, d).start()

    def passed_pieces(i):
        for e in RING_STEPS:
            from_x = bias_all.at[i, lax.rem(x_at + e, 4), y, :4]
            from_y = bias_all.at[i, x_at, lax.rem(y + e, 4), 4:]
            for d in RING_STEPS:
                plane_copy(from_x, bb_send, bb_recv.at[i], 0, d).start()
                plane_copy(from_y, bb_send, bb_recv.at[i], d, 0).start()

    scale = LOG2E / math.sqrt(WIDTH)
    head_of = lax.broadcasted_iota(jnp.int32, (C, N), 0)

    def project(i):
        attend = an_t[i]
        queries = dot(w_qv_t[0], attend) * scale
        values_ref[i] = dot(w_qv_t[1], attend).astype(BF16)
        keys = jnp.transpose(dot(w_k_t[...], attend)).astype(BF16)
        gate2_ref[i] = sigmoid(dot(w_gate2_t[...], attend))
        for h in range(HEADS):
            inside = (head_of >= WIDTH * h) & (head_of < WIDTH * (h + 1))
            scores_ref[i, h] = dot(keys, jnp.where(inside, queries, 0.0).astype(BF16)) + penalty[...]

    for i in range(OWN):
        arrive(recv_x.at[i], x_recv.at[i])
        product = recv_x[i].astype(F32).reshape(C, N)
        update = dot(w_o1_t[...], norm_columns(product, gains[1]).astype(BF16))
        middle = (xt[i] + gate1[i] * update).astype(BF16).astype(F32)
        mid[i] = middle
        attend = norm_columns(middle, gains[2]).astype(BF16)
        an_t[i] = attend
        bias_all[i, x_at, y, z] = (dot(w_bias_ref[...], attend) * LOG2E).astype(BF16)
        for dz in Z_STEPS:
            bz_copy(i, dz).start()

    for i in range(OWN):
        arrive(bias_all.at[i, 0, 0, :7], bz_recv.at[i])
        own_pieces(i)
        if i < OWN - 1:
            project(i)
    for i in range(OWN):
        arrive(bias_all.at[i, 0, :3], bx_recv.at[i])
        arrive(bias_all.at[i, 0, :3], by_recv.at[i])
        passed_pieces(i)
        if i == 0:
            project(OWN - 1)
    def o_exchange(b):
        target = out_ref.at[b, pl.ds(OWN * col, OWN)]
        for dz, dl in COL_STEPS:
            peer = col_peer(dz, dl)
            remote(send_o.at[b, peer], target, o_send, o_recv, row, peer).start()
        pltpu.make_async_copy(send_o.at[b, col], target, o_recv).start()

    for b in range(OWN):
        arrive(bias_all.at[b, :3, :3], bb_recv.at[b])
        base = b * C * HEADS
        for r in range(ROWS):
            for c in range(COLS):
                piece = bias_all[b, (r // 4) * 2 + c % 2, r % 4, c // 2].astype(F32)
                at = base + (r * COLS + c) * HEADS
                for k in range(3):
                    wide_t[k, at : at + HEADS, :] = piece[:, k * 128 : (k + 1) * 128]
        lanes = slice(b * 128, (b + 1) * 128)
        for h in range(HEADS):
            for k in range(3):
                part = wide_t[k, pl.ds(base + h, C, stride=HEADS), :]
                bias_t[h, k * 128 : (k + 1) * 128, :] = jnp.transpose(part)
        for i in range(OWN):
            parts = []
            for h in range(0, HEADS, 2):
                pair, totals = [], []
                for k in (h, h + 1):
                    scores = scores_ref[i, k, :, lanes] + bias_t[k]
                    weights = jnp.exp2(scores - jnp.max(scores, axis=0, keepdims=True))
                    totals.append(jnp.sum(weights, axis=0, keepdims=True))
                    pair.append(weights.astype(BF16))
                mixed = dot(values_ref[i, WIDTH * h : WIDTH * (h + 2)], jnp.concatenate(pair, axis=1))
                parts += [mixed[:WIDTH, :C] / totals[0], mixed[WIDTH:, C:] / totals[1]]
            gated = (gate2_ref[i, :, lanes] * jnp.concatenate(parts, axis=0)).astype(BF16)
            result = mid[i, :, lanes] + dot(w_o2_t[...], gated)
            send_o[b, :, i] = jnp.transpose(result).reshape(COLS, 8, C).astype(BF16)
        o_exchange(b)

    arrive(x_rows.at[:, :15], r_send)
    arrive(send_za.at[:, :7], za_send)
    arrive(send_fa.at[:, :15], fa_send)
    arrive(send_fb.at[:, :7], fb_send)
    arrive(send_zb.at[:, :15], zb_send)
    arrive(send_p.at[:, :7], p_send)
    arrive(send_x.at[:, :15], x_send)
    arrive(bias_all.at[:, 0, 0, :7], bz_send)
    arrive(bias_all.at[:, :2, :3], ba_send)
    arrive(bias_all.at[:, :3, :3], bb_send)
    arrive(send_o.at[:, :15], o_send)
    arrive(out_ref, o_recv)


def interleave(blocks_ref, out_ref, lines):
    for b in range(OWN):
        lines[pl.ds(b, N, stride=OWN), :] = blocks_ref[b].astype(F32).reshape(N, C)
    out_ref[...] = lines[...].reshape(out_ref.shape).astype(BF16)


def owner_order():
    perm = np.zeros((C, C), np.float32)
    for owner in range(C):
        r, c = owner // COLS, owner % COLS
        perm[owner, (2 * r + c % 2) * ZS + c // 2] = 1.0
    return perm


def shards(
    pair_state, token_mask, block_pattern, triangle_norm, triangle_input, triangle_gate, product_norm,
    triangle_output, attend_norm, attend_inputs, attend_gate, attend_bias, attend_output,
):
    vmem = pl.BlockSpec(memory_space=pltpu.VMEM)
    hbm = pl.BlockSpec(memory_space=pl.ANY)
    dma = pltpu.SemaphoreType.DMA
    V = pltpu.VMEM
    blocks = pl.pallas_call(
        kernel,
        out_shape=jax.ShapeDtypeStruct((OWN, 48, 8, C), BF16),
        in_specs=[hbm] * 14,
        out_specs=hbm,
        scratch_shapes=[
            V((OWN, COLS, 24, C), BF16),
            V((OWN, ZS, GS, N), BF16), V((OWN, ZS, GS, N), BF16), V((OWN, GS, ZS, N), BF16), V((OWN, GS, ZS, N), BF16),
            V((OWN, ZS, GS, N), BF16), V((OWN, ZS, GS, N), BF16), V((OWN, GS, ZS, N), BF16), V((OWN, GS, ZS, N), BF16),
            V((OWN, ZS, GS, N), BF16), V((OWN, ZS, GS, N), BF16),
            V((OWN, GS, 8, N), BF16), V((OWN, GS, 8, N), BF16),
            V((OWN, 4, 4, ZS, HEADS, N), BF16),
            V((OWN, COLS, OWN, 8, C), BF16),
            V((OWN, C, N), F32), V((OWN, C, N), F32), V((OWN, C, N), F32), V((OWN, C, N), BF16),
            V((3, HEADS * N, 128), F32), V((HEADS, N, C), F32), V((N, N), F32),
            V((OWN, HEADS, N, N), F32), V((OWN, C, N), BF16), V((OWN, C, N), F32),
            V((N,), jnp.int32), pltpu.SMEM((4, 4), jnp.int32), V((3, 1, C), F32), V((HEADS, C), BF16),
            V((48, 24, C), BF16), V((C, C), BF16), V((C, 4 * C), BF16), V((C, C), BF16), V((C, C), BF16),
            V((C, 3 * C), BF16), V((C, C), BF16), V((C, C), BF16),
            V((2 * C, C), BF16), V((2 * C, C), BF16), V((C, C), BF16), V((C, C), BF16),
            V((2, C, C), BF16), V((C, C), BF16), V((C, C), BF16), V((C, C), BF16), V((3, C, C), F32),
            dma, dma((OWN,)), dma, dma((OWN,)), dma, dma((OWN,)), dma, dma((OWN,)), dma, dma,
            dma, dma((OWN,)), dma, dma((OWN,)),
            dma, dma((OWN,)), dma, dma((OWN,)), dma((OWN,)), dma, dma((OWN,)), dma, dma, dma((14,)),
        ],
        compiler_params=pltpu.CompilerParams(
            collective_id=0, has_side_effects=True, vmem_limit_bytes=48 * 1024 * 1024
        ),
        name="pairformer",
    )(*(pltpu.with_memory_space_constraint(v, pltpu.HBM) for v in (
        pair_state, token_mask, block_pattern, jnp.asarray(owner_order(), BF16),
        triangle_norm.reshape(1, C), triangle_input, triangle_gate, product_norm.reshape(1, C), triangle_output,
        attend_norm.reshape(1, C), attend_inputs, attend_gate, attend_bias.T, attend_output,
    )))
    return pl.pallas_call(
        interleave,
        out_shape=jax.ShapeDtypeStruct(pair_state.shape, BF16),
        in_specs=[vmem],
        out_specs=vmem,
        scratch_shapes=[V((48 * 24, C), F32)],
        compiler_params=pltpu.CompilerParams(vmem_limit_bytes=6 * 1024 * 1024),
        name="interleave",
    )(blocks)


def solution(mesh):
    tile = P(("crop", "row"), "col", None)
    return jax.shard_map(
        shards,
        mesh=mesh,
        in_specs=(tile, P("crop"), P("crop", None)) + (P(),) * 10,
        out_specs=tile,
        check_vma=False,
    )
```

```python
import functools
import math

import jax
import jax.numpy as jnp
import numpy as np
from jax import lax
from jax.experimental import pallas as pl
from jax.experimental.pallas import tpu as pltpu
from jax.sharding import PartitionSpec as P

MESH = pl.DeviceIdType.MESH
F32 = jnp.float32
BF16 = jnp.bfloat16
EPS = 1e-05
ROWS, COLS, C, N = 8, 16, 128, 384
HEADS, WIDTH = 4, 32
ZS, GS, OWN = 8, 16, 3
LOG2E = 1.4426950408889634
MASKED = -1e30


def dot(a, b):
    return jnp.dot(a, b, preferred_element_type=F32)


def dot_nt(a, b):
    return lax.dot_general(a, b, (((1,), (1,)), ((), ())), preferred_element_type=F32)


def dot_tn(a, b):
    return lax.dot_general(a, b, (((0,), (0,)), ((), ())), preferred_element_type=F32)


def wide(gain):
    return jnp.concatenate([gain] * (N // 128), axis=1)


def norm_columns(v, gain):
    centered = v - jnp.mean(v, axis=0, keepdims=True)
    variance = jnp.mean(centered * centered, axis=0, keepdims=True)
    return centered * lax.rsqrt(variance + EPS) * wide(gain)


def sigmoid(v):
    return 1.0 / (1.0 + jnp.exp(-v))


def turned(w):
    return jnp.transpose(w.astype(F32))


RING_STEPS = (2, 1, 3)
Z_STEPS = (4, 3, 5, 2, 6, 1, 7)
COL_STEPS = tuple((dz, dl) for dz in Z_STEPS for dl in (1, 0)) + ((0, 1),)
XY_STEPS = tuple(sorted(
    ((dx, dy) for dx in range(4) for dy in range(4) if dx or dy),
    key=lambda s: -(min(s[0], 4 - s[0]) + min(s[1], 4 - s[1])),
))


def kernel(
    x_hbm, mask_hbm, pattern_hbm, perm_hbm,
    norm1_hbm, w_in_hbm, w_gate_hbm, norm2_hbm, w_out1_hbm,
    norm3_hbm, w_qkv_hbm, w_gate2_hbm, w_bias_hbm, w_out2_hbm,
    out_ref,
    x_rows, send_za, recv_za, send_fa, recv_fa, send_fb, recv_fb, send_zb, recv_zb, send_p, recv_p, send_x, recv_x,
    bias_all, send_o, xt, gate1, mid, an_t, wide_t, bias_t, penalty, scores_ref, values_ref, gate2_ref,
    mask_ref, pattern_ref, norms_ref, w_bias_ref,
    x_ref, perm_ref, w_in_ref, w_gate_ref, w_out1_ref, w_qkv_ref, w_gate2_ref, w_out2_ref,
    w_g, w_v, w_gate_t, w_o1_t, w_qv_t, w_k_t, w_gate2_t, w_o2_t, gains,
    r_send, r_recv, za_send, za_recv, fa_send, fa_recv, fb_send, fb_recv, zb_send, zb_recv, p_send, p_recv, x_send, x_recv,
    bz_send, bz_recv, ba_send, bx_recv, by_recv, bb_send, bb_recv, o_send, o_recv, fetch,
):
    row, col = lax.axis_index("row"), lax.axis_index("col")
    z, x_lo = col // 2, col % 2
    x_hi, y = row // 4, row % 4
    g = row * 2 + x_lo
    x_at = x_hi * 2 + x_lo

    def place(x, y, z):
        return (x // 2) * 4 + y, z * 2 + x % 2

    def signal(r, c):
        pl.semaphore_signal(barrier, inc=1, device_id={"row": r, "col": c}, device_id_type=MESH)

    def remote(src, dst, send, recv, r, c):
        return pltpu.make_async_remote_copy(
            src_ref=src, dst_ref=dst, send_sem=send, recv_sem=recv,
            device_id={"row": r, "col": c}, device_id_type=MESH,
        )

    def arrive(ref, sem):
        pltpu.make_async_copy(ref, ref, sem).wait()

    def col_peer(dz, dl):
        return lax.rem(z + dz, ZS) * 2 + lax.rem(x_lo + dl, 2)

    def xy_peer(dx, dy):
        xx, yy = lax.rem(x_at + dx, 4), lax.rem(y + dy, 4)
        r, c = place(xx, yy, z)
        return r * 2 + xx % 2, r, c

    barrier = pltpu.get_barrier_semaphore()
    for dz, dl in COL_STEPS:
        signal(row, col_peer(dz, dl))
    for dx, dy in XY_STEPS:
        if (dx, dy) != (1, 0) and (dx, dy) != (3, 0) and (dx, dy) != (2, 0):
            _, r, c = xy_peer(dx, dy)
            signal(r, c)
    _, r, c = xy_peer(2, 0)
    signal(r, c)
    other = x_at + 1 + 2 * (1 - x_at % 2)
    r, c = place(lax.rem(other, 4), y, z)
    signal(r, c)

    fetched = [
        pltpu.make_async_copy(src, dst, fetch.at[n])
        for n, (src, dst) in enumerate((
            (w_in_hbm, w_in_ref), (w_gate_hbm, w_gate_ref), (w_out1_hbm, w_out1_ref), (w_qkv_hbm, w_qkv_ref),
            (w_gate2_hbm, w_gate2_ref), (w_out2_hbm, w_out2_ref), (perm_hbm, perm_ref), (x_hbm, x_ref),
            (norm1_hbm, norms_ref.at[0]), (norm2_hbm, norms_ref.at[1]), (norm3_hbm, norms_ref.at[2]),
            (mask_hbm, mask_ref), (pattern_hbm, pattern_ref), (w_bias_hbm, w_bias_ref),
        ))
    ]
    for copy in fetched:
        copy.start()

    fetched[0].wait()
    w_t = jnp.concatenate([turned(w_in_ref[:, s * C : (s + 1) * C]) for s in range(4)], axis=0)
    ga, va, gb, vb = (w_t[s * C : (s + 1) * C].astype(BF16) for s in range(4))
    line, at = (lax.broadcasted_iota(jnp.int32, (C, C), d) for d in range(2))
    z_first = jnp.where((line & 15) * ZS + (line >> 4) == at, 1.0, 0.0).astype(BF16)
    w_g[:C], w_g[C:] = dot(z_first, gb).astype(BF16), ga
    w_v[:C], w_v[C:] = dot(z_first, vb).astype(BF16), va
    for slot in range(3):
        fetched[8 + slot].wait()
        gains[slot] = jnp.transpose(jnp.broadcast_to(norms_ref[slot], (C, C)))

    fetched[7].wait()
    pl.semaphore_wait(barrier, COLS - 1 + 2 * (ROWS - 1))

    def r_copy(i, dz, dl):
        peer = col_peer(dz, dl)
        return remote(x_ref.at[OWN * peer + i], x_rows.at[i, col], r_send, r_recv.at[i], row, peer)

    def r_own(i):
        return pltpu.make_async_copy(x_ref.at[OWN * col + i], x_rows.at[i, col], r_recv.at[i])

    for i in range(OWN):
        for dz, dl in COL_STEPS:
            r_copy(i, dz, dl).start()
        r_own(i).start()

    for copy in fetched[1:6] + fetched[11:]:
        copy.wait()
    w_gate_t[...] = turned(w_gate_ref[...]).astype(BF16)
    w_o1_t[...] = turned(w_out1_ref[...]).astype(BF16)
    w_o2_t[...] = turned(w_out2_ref[...]).astype(BF16)
    w_gate2_t[...] = turned(w_gate2_ref[...]).astype(BF16)
    w_qv_t[0] = turned(w_qkv_ref[:, :C]).astype(BF16)
    w_qv_t[1] = turned(w_qkv_ref[:, 2 * C :]).astype(BF16)
    w_k_t[...] = turned(w_qkv_ref[:, C : 2 * C]).astype(BF16)
    length = jnp.sum(mask_ref[...].reshape(1, N).astype(F32), axis=1, keepdims=True)
    lane = lax.broadcasted_iota(jnp.int32, (1, N), 1)
    mask = jnp.where((OWN * (lane & 127) + (lane >> 7)).astype(F32) < length, 1.0, 0.0)
    key_mask = jnp.transpose(jnp.broadcast_to(mask, (C, N)))
    for b in range(4):
        line = jnp.zeros((1, N), F32)
        for a in range(4):
            line = line + jnp.where(((lane & 127) >> 5) == a, pattern_ref[a, b].astype(F32), 0.0)
        for i in range(OWN):
            rows = slice(i * 128 + 32 * b, i * 128 + 32 * (b + 1))
            penalty[rows, :] = jnp.where(wide(key_mask[rows]) * line > 0.0, 0.0, MASKED)
    fetched[6].wait()

    def z_copy(i, src, dst, send, recv, dz):
        peer = lax.rem(z + dz, ZS)
        return remote(src.at[i, peer], dst.at[i, z], send, recv, row, peer * 2 + x_lo)

    def z_exchange(i, src, dst, send, recv):
        for dz in Z_STEPS:
            z_copy(i, src, dst, send, recv, dz).start()
        pltpu.make_async_copy(src.at[i, z], dst.at[i, z], recv).start()

    def xy_exchange(i, src, dst, send, recv):
        for dx, dy in XY_STEPS:
            peer, r, c = xy_peer(dx, dy)
            remote(src.at[i, peer], dst.at[i, g], send, recv, r, c).start()
        pltpu.make_async_copy(src.at[i, g], dst.at[i, g], recv).start()

    for i in range(OWN):
        arrive(x_rows.at[i], r_recv.at[i])
        wide_t[0, i * N : (i + 1) * N, :] = x_rows[i].astype(F32).reshape(N, C)
        x_t = jnp.concatenate(
            [jnp.transpose(wide_t[0, pl.ds(i * N + b, 128, stride=OWN), :]) for b in range(OWN)], axis=1
        )
        xt[i] = x_t
        normed = norm_columns(x_t, gains[0]).astype(BF16)
        an_t[i] = normed
        own_token = row * 48 + col * OWN + i
        mine = jnp.where(own_token.astype(F32) < length, 1.0, 0.0)
        factors = sigmoid(dot(w_g[C:], normed)) * dot(w_v[C:], normed) * (mask * mine)
        send_fa[i] = factors.reshape(GS, ZS, N).astype(BF16)
        xy_exchange(i, send_fa, recv_fa, fa_send, fa_recv.at[i])
        factors = sigmoid(dot(w_g[:C], normed)) * dot(w_v[:C], normed) * (mask * mine)
        send_za[i] = factors.astype(BF16).reshape(ZS, GS, N)
        z_exchange(i, send_za, recv_za, za_send, za_recv.at[i])

    def spread(i, half, arrived):
        base = (2 * i + half) * C
        for b in range(3):
            wide_t[b, base : base + C, :] = arrived[:, b * 128 : (b + 1) * 128]
        return base

    def plane_on(i):
        arrive(recv_fa.at[i], fa_recv.at[i])
        base = spread(i, 0, recv_fa[i].astype(F32).reshape(C, N))
        for to in range(ZS):
            for b in range(3):
                piece = wide_t[b, pl.ds(base + to, GS, stride=ZS), :]
                send_fb[i, to, :, b * 128 : (b + 1) * 128] = piece.astype(BF16)
        z_exchange(i, send_fb, recv_fb, fb_send, fb_recv.at[i])

    def z_on(i):
        arrive(recv_za.at[i], za_recv.at[i])
        base = spread(i, 1, recv_za[i].astype(F32).reshape(C, N))
        for to in range(GS):
            for b in range(3):
                piece = wide_t[b, pl.ds(base + to, ZS, stride=GS), :]
                send_zb[i, to, :, b * 128 : (b + 1) * 128] = piece.astype(BF16)
        xy_exchange(i, send_zb, recv_zb, zb_send, zb_recv)

    plane_on(0)
    z_on(0)
    plane_on(1)
    z_on(1)
    plane_on(2)
    z_on(2)
    for i in range(OWN):
        gate1[i] = sigmoid(dot(w_gate_t[...], an_t[i]))
    arrive(recv_zb, zb_recv)
    right = jnp.concatenate(
        [dot(perm_ref[...], recv_zb[i].astype(F32).reshape(C, N).astype(BF16)).astype(BF16) for i in range(OWN)], axis=0
    )
    for i in range(OWN):
        arrive(recv_fb.at[i], fb_recv.at[i])
        left = recv_fb[i].reshape(C, N)
        send_p[i] = dot_nt(left, right).astype(BF16).reshape(ZS, GS, N)
        z_exchange(i, send_p, recv_p, p_send, p_recv.at[i])

    for i in range(OWN):
        arrive(recv_p.at[i], p_recv.at[i])
        base = spread(i, 0, recv_p[i].astype(F32).reshape(C, N))
        for to in range(GS):
            for b in range(3):
                piece = wide_t[b, pl.ds(base + to, ZS, stride=GS), :]
                send_x[i, to, :, b * 128 : (b + 1) * 128] = piece.astype(BF16)
        xy_exchange(i, send_x, recv_x, x_send, x_recv.at[i])

    def bz_copy(i, dz):
        ref = bias_all.at[i, x_at, y, z]
        return remote(ref, ref, bz_send, bz_recv.at[i], *place(x_at, y, lax.rem(z + dz, ZS)))

    def plane_copy(ref, send, recv, dx, dy):
        return remote(ref, ref, send, recv, *place(lax.rem(x_at + dx, 4), lax.rem(y + dy, 4), z))

    def own_pieces(i):
        ref = bias_all.at[i, x_at, y]
        for d in RING_STEPS:
            plane_copy(ref, ba_send, bx_recv.at[i], d, 0).start()
            plane_copy(ref, ba_send, by_recv.at[i], 0, d).start()

    def passed_pieces(i):
        for e in RING_STEPS:
            from_x = bias_all.at[i, lax.rem(x_at + e, 4), y, :4]
            from_y = bias_all.at[i, x_at, lax.rem(y + e, 4), 4:]
            for d in RING_STEPS:
                plane_copy(from_x, bb_send, bb_recv.at[i], 0, d).start()
                plane_copy(from_y, bb_send, bb_recv.at[i], d, 0).start()

    scale = LOG2E / math.sqrt(WIDTH)
    head_of = lax.broadcasted_iota(jnp.int32, (C, N), 0)

    def project(i):
        attend = an_t[i]
        queries = dot(w_qv_t[0], attend) * scale
        values_ref[i] = dot(w_qv_t[1], attend).astype(BF16)
        keys = jnp.transpose(dot(w_k_t[...], attend)).astype(BF16)
        gate2_ref[i] = sigmoid(dot(w_gate2_t[...], attend))
        for h in range(HEADS):
            inside = (head_of >= WIDTH * h) & (head_of < WIDTH * (h + 1))
            scores_ref[i, h] = dot(keys, jnp.where(inside, queries, 0.0).astype(BF16)) + penalty[...]

    for i in range(OWN):
        arrive(recv_x.at[i], x_recv.at[i])
        product = recv_x[i].astype(F32).reshape(C, N)
        update = dot(w_o1_t[...], norm_columns(product, gains[1]).astype(BF16))
        middle = (xt[i] + gate1[i] * update).astype(BF16).astype(F32)
        mid[i] = middle
        attend = norm_columns(middle, gains[2]).astype(BF16)
        an_t[i] = attend
        bias_all[i, x_at, y, z] = (dot(w_bias_ref[...], attend) * LOG2E).astype(BF16)
        for dz in Z_STEPS:
            bz_copy(i, dz).start()

    for i in range(OWN):
        arrive(bias_all.at[i, 0, 0, :7], bz_recv.at[i])
        own_pieces(i)
        if i < OWN - 1:
            project(i)
    for i in range(OWN):
        arrive(bias_all.at[i, 0, :3], bx_recv.at[i])
        arrive(bias_all.at[i, 0, :3], by_recv.at[i])
        passed_pieces(i)
        if i == 0:
            project(OWN - 1)
    def o_exchange(b):
        target = out_ref.at[b, pl.ds(OWN * col, OWN)]
        for dz, dl in COL_STEPS:
            peer = col_peer(dz, dl)
            remote(send_o.at[b, peer], target, o_send, o_recv, row, peer).start()
        pltpu.make_async_copy(send_o.at[b, col], target, o_recv).start()

    for b in range(OWN):
        arrive(bias_all.at[b, :3, :3], bb_recv.at[b])
        base = b * C * HEADS
        for r in range(ROWS):
            for c in range(COLS):
                piece = bias_all[b, (r // 4) * 2 + c % 2, r % 4, c // 2].astype(F32)
                at = base + (r * COLS + c) * HEADS
                for k in range(3):
                    wide_t[k, at : at + HEADS, :] = piece[:, k * 128 : (k + 1) * 128]
        lanes = slice(b * 128, (b + 1) * 128)
        for h in range(HEADS):
            for k in range(3):
                part = wide_t[k, pl.ds(base + h, C, stride=HEADS), :]
                bias_t[h, k * 128 : (k + 1) * 128, :] = jnp.transpose(part)
        for i in range(OWN):
            parts = []
            for h in range(HEADS):
                scores = scores_ref[i, h, :, lanes] + bias_t[h]
                weights = jnp.exp2(scores - jnp.max(scores, axis=0, keepdims=True))
                total = jnp.sum(weights, axis=0, keepdims=True)
                mixed = dot(values_ref[i, WIDTH * h : WIDTH * (h + 1)], weights.astype(BF16))
                parts.append(mixed / total)
            gated = (gate2_ref[i, :, lanes] * jnp.concatenate(parts, axis=0)).astype(BF16)
            result = mid[i, :, lanes] + dot(w_o2_t[...], gated)
            send_o[b, :, i] = jnp.transpose(result).reshape(COLS, 8, C).astype(BF16)
        o_exchange(b)

    arrive(x_rows.at[:, :15], r_send)
    arrive(send_za.at[:, :7], za_send)
    arrive(send_fa.at[:, :15], fa_send)
    arrive(send_fb.at[:, :7], fb_send)
    arrive(send_zb.at[:, :15], zb_send)
    arrive(send_p.at[:, :7], p_send)
    arrive(send_x.at[:, :15], x_send)
    arrive(bias_all.at[:, 0, 0, :7], bz_send)
    arrive(bias_all.at[:, :2, :3], ba_send)
    arrive(bias_all.at[:, :3, :3], bb_send)
    arrive(send_o.at[:, :15], o_send)
    arrive(out_ref, o_recv)


def interleave(blocks_ref, out_ref, lines):
    for b in range(OWN):
        lines[pl.ds(b, N, stride=OWN), :] = blocks_ref[b].astype(F32).reshape(N, C)
    out_ref[...] = lines[...].reshape(out_ref.shape).astype(BF16)


def owner_order():
    perm = np.zeros((C, C), np.float32)
    for owner in range(C):
        r, c = owner // COLS, owner % COLS
        perm[owner, (2 * r + c % 2) * ZS + c // 2] = 1.0
    return perm


def shards(
    pair_state, token_mask, block_pattern, triangle_norm, triangle_input, triangle_gate, product_norm,
    triangle_output, attend_norm, attend_inputs, attend_gate, attend_bias, attend_output,
):
    vmem = pl.BlockSpec(memory_space=pltpu.VMEM)
    hbm = pl.BlockSpec(memory_space=pl.ANY)
    dma = pltpu.SemaphoreType.DMA
    V = pltpu.VMEM
    blocks = pl.pallas_call(
        kernel,
        out_shape=jax.ShapeDtypeStruct((OWN, 48, 8, C), BF16),
        in_specs=[hbm] * 14,
        out_specs=hbm,
        scratch_shapes=[
            V((OWN, COLS, 24, C), BF16),
            V((OWN, ZS, GS, N), BF16), V((OWN, ZS, GS, N), BF16), V((OWN, GS, ZS, N), BF16), V((OWN, GS, ZS, N), BF16),
            V((OWN, ZS, GS, N), BF16), V((OWN, ZS, GS, N), BF16), V((OWN, GS, ZS, N), BF16), V((OWN, GS, ZS, N), BF16),
            V((OWN, ZS, GS, N), BF16), V((OWN, ZS, GS, N), BF16),
            V((OWN, GS, 8, N), BF16), V((OWN, GS, 8, N), BF16),
            V((OWN, 4, 4, ZS, HEADS, N), BF16),
            V((OWN, COLS, OWN, 8, C), BF16),
            V((OWN, C, N), F32), V((OWN, C, N), F32), V((OWN, C, N), F32), V((OWN, C, N), BF16),
            V((3, HEADS * N, 128), F32), V((HEADS, N, C), F32), V((N, N), F32),
            V((OWN, HEADS, N, N), F32), V((OWN, C, N), BF16), V((OWN, C, N), F32),
            V((N,), jnp.int32), pltpu.SMEM((4, 4), jnp.int32), V((3, 1, C), F32), V((HEADS, C), BF16),
            V((48, 24, C), BF16), V((C, C), BF16), V((C, 4 * C), BF16), V((C, C), BF16), V((C, C), BF16),
            V((C, 3 * C), BF16), V((C, C), BF16), V((C, C), BF16),
            V((2 * C, C), BF16), V((2 * C, C), BF16), V((C, C), BF16), V((C, C), BF16),
            V((2, C, C), BF16), V((C, C), BF16), V((C, C), BF16), V((C, C), BF16), V((3, C, C), F32),
            dma, dma((OWN,)), dma, dma((OWN,)), dma, dma((OWN,)), dma, dma((OWN,)), dma, dma,
            dma, dma((OWN,)), dma, dma((OWN,)),
            dma, dma((OWN,)), dma, dma((OWN,)), dma((OWN,)), dma, dma((OWN,)), dma, dma, dma((14,)),
        ],
        compiler_params=pltpu.CompilerParams(
            collective_id=0, has_side_effects=True, vmem_limit_bytes=48 * 1024 * 1024
        ),
        name="pairformer",
    )(*(pltpu.with_memory_space_constraint(v, pltpu.HBM) for v in (
        pair_state, token_mask, block_pattern, jnp.asarray(owner_order(), BF16),
        triangle_norm.reshape(1, C), triangle_input, triangle_gate, product_norm.reshape(1, C), triangle_output,
        attend_norm.reshape(1, C), attend_inputs, attend_gate, attend_bias.T, attend_output,
    )))
    return pl.pallas_call(
        interleave,
        out_shape=jax.ShapeDtypeStruct(pair_state.shape, BF16),
        in_specs=[vmem],
        out_specs=vmem,
        scratch_shapes=[V((48 * 24, C), F32)],
        compiler_params=pltpu.CompilerParams(vmem_limit_bytes=6 * 1024 * 1024),
        name="interleave",
    )(blocks)


def solution(mesh):
    tile = P(("crop", "row"), "col", None)
    return jax.shard_map(
        shards,
        mesh=mesh,
        in_specs=(tile, P("crop"), P("crop", None)) + (P(),) * 10,
        out_specs=tile,
        check_vma=False,
    )
```
